32 devices in a mesh: grp: 2 (over y), seq: 4 (over z), head: 2 (over x), sub: 2 (over core).
Axes of the slice: x: 2, y: 2, z: 4, core: 2. Of those that a mesh axis runs over, the one named last changes fastest.
Arguments:
- vid_q: bfloat16 [2560, 4096], P(('grp', 'seq', 'sub'), 'head'), parts along dimension 0, may hold values from -6 to 6
- vid_k: bfloat16 [2560, 4096], P(('grp', 'seq', 'sub'), 'head'), parts along dimension 0, may hold values from -6 to 6
- vid_v: bfloat16 [2560, 4096], P(('grp', 'seq', 'sub'), 'head'), parts along dimension 0, may hold values from -6 to 6
- aud_q: bfloat16 [640, 2048], P(('grp', 'seq', 'sub'), 'head'), parts along dimension 0, may hold values from -6 to 6
- cross_k: bfloat16 [2560, 2048], P(('grp', 'seq', 'sub'), 'head'), parts along dimension 0, may hold values from -6 to 6
- cross_v: bfloat16 [2560, 2048], P(('grp', 'seq', 'sub'), 'head'), parts along dimension 0, may hold values from -6 to 6
- cross_q: bfloat16 [2560, 2048], P(('grp', 'seq', 'sub'), 'head'), parts along dimension 0, may hold values from -6 to 6
- aud_k: bfloat16 [640, 2048], P(('grp', 'seq', 'sub'), 'head'), parts along dimension 0, may hold values from -6 to 6
- aud_v: bfloat16 [640, 2048], P(('grp', 'seq', 'sub'), 'head'), parts along dimension 0, may hold values from -6 to 6
- windows: int32 [2, 80], P(None, 'grp'), parts along dimension 1, may hold values from 0 to 40, as said below
Outputs:
- video_self: bfloat16 [2560, 4096], P(('grp', 'seq', 'sub'), 'head'), parts along dimension 0
- audio_out: bfloat16 [640, 2048], P(('grp', 'seq', 'sub'), 'head'), parts along dimension 0
- video_cross: bfloat16 [2560, 2048], P(('grp', 'seq', 'sub'), 'head'), parts along dimension 0
The draws below stay inside these ranges and needn't reach their ends.
There are 2 independent parts, one for each index of `grp`. The reference program is written for one: setup_inputs(seed, part) draws one part's arguments, and reference() takes and returns one part's arrays. A program takes and returns all parts, laid end to end along the dimension named above; each array names one. Nothing has to cross between parts.
Inputs may be any that keep to these rules, and one draw needn't show every extreme that they name: For every stretch c, windows[0, c] lies between max(0, c - 5) and c, and windows[1, c] between c + 1 and min(40, c + 6); in every draw some stretch reaches 5 tiles on both sides.
All inputs are finite; a program needn't handle non-finite values.
Results may differ from the reference program's by a relative error of at most 0.03.
Values may be sent and summed in bfloat16 or wider, within the bound.
A program may use at most 64 MiB of HBM per device.

```python
import jax
import jax.numpy as jnp
from jax import lax

VIDEO_HEADS = 32
HEAD_DIM = 128
AUDIO_HEADS = 32
AUDIO_DIM = 64
TILE_LEN = 32
STRETCH_LEN = 8
WINDOW_REACH = 5
VIDEO_TOKENS = 1280
AUDIO_TOKENS = 320
TILE_COUNT = 40


def drawn(key, query_rows, key_rows, width):
    base_query = jnp.clip(jax.random.normal(jax.random.fold_in(key, 11), (query_rows, width), jnp.float32), -5.0, 5.0)
    base_key = jnp.clip(jax.random.normal(jax.random.fold_in(key, 12), (key_rows, width), jnp.float32), -5.0, 5.0)
    return (base_query, base_key)


def video_pair(key):
    return drawn(jax.random.fold_in(key, 1), VIDEO_TOKENS, VIDEO_TOKENS, VIDEO_HEADS * HEAD_DIM)


def audio_pair(key):
    return drawn(jax.random.fold_in(key, 2), AUDIO_TOKENS, VIDEO_TOKENS, AUDIO_HEADS * AUDIO_DIM)


def window_pair(key):
    return drawn(jax.random.fold_in(key, 3), VIDEO_TOKENS, AUDIO_TOKENS, AUDIO_HEADS * AUDIO_DIM)


def draw_vid_q(key, part):
    return video_pair(key)[0].astype(jnp.bfloat16)


def draw_vid_k(key, part):
    return video_pair(key)[1].astype(jnp.bfloat16)


def draw_aud_q(key, part):
    return audio_pair(key)[0].astype(jnp.bfloat16)


def draw_cross_k(key, part):
    return audio_pair(key)[1].astype(jnp.bfloat16)


def draw_cross_q(key, part):
    return window_pair(key)[0].astype(jnp.bfloat16)


def draw_aud_k(key, part):
    return window_pair(key)[1].astype(jnp.bfloat16)


def draw_windows(key, part):
    below = jax.random.randint(jax.random.fold_in(key, 41), (TILE_COUNT,), 0, WINDOW_REACH + 1)
    above = jax.random.randint(jax.random.fold_in(key, 42), (TILE_COUNT,), 0, WINDOW_REACH + 1)
    chosen = jax.random.randint(jax.random.fold_in(key, 43), (), WINDOW_REACH, TILE_COUNT - WINDOW_REACH)
    below = below.at[chosen].set(WINDOW_REACH)
    above = above.at[chosen].set(WINDOW_REACH)
    stretch_ids = jnp.arange(TILE_COUNT, dtype=jnp.int32)
    first_tile = jnp.maximum(stretch_ids - below, 0)
    after_tile = jnp.minimum(stretch_ids + 1 + above, TILE_COUNT)
    return jnp.stack([first_tile, after_tile]).astype(jnp.int32)


def levels(stream_key, extent, cuts, low, largest):
    loudness, own = 1.0, jax.random.fold_in(stream_key, 6)
    for dim, parts in cuts:
        heights = jnp.exp(jax.random.uniform(jax.random.fold_in(own, dim), (parts,), jnp.float32, low / len(cuts), largest / len(cuts)))
        loudness = loudness * jnp.repeat(heights, extent[dim] // parts).reshape([-1 if axis == dim else 1 for axis in range(len(extent))])
    return loudness


def normal_values(own_key, shape, deviation, limit, cuts=(), held_as=jnp.bfloat16):
    values = jax.random.normal(own_key, shape, jnp.float32) * deviation
    if len(cuts) > 0:
        values = levels(own_key, shape, cuts, -0.22, 0.18) * values
    return jnp.clip(values, min=-limit, max=limit).astype(held_as)


def setup_inputs(seed: int = 0, part: int = 0) -> dict:
    key_of = jax.random.split(jax.random.key(seed), 11)
    part_keys = jax.random.split(jax.random.fold_in(key_of[10], part), 11)
    return {
        "vid_q": draw_vid_q(jax.random.fold_in(jax.random.fold_in(key_of[10], part), 71), part),
        "vid_k": draw_vid_k(jax.random.fold_in(jax.random.fold_in(key_of[10], part), 71), part),
        "vid_v": normal_values(part_keys[2], (VIDEO_TOKENS, VIDEO_HEADS * HEAD_DIM), 1.0, 6.0, ((0, 8), (1, 2))),
        "aud_q": draw_aud_q(jax.random.fold_in(jax.random.fold_in(key_of[10], part), 71), part),
        "cross_k": draw_cross_k(jax.random.fold_in(jax.random.fold_in(key_of[10], part), 71), part),
        "cross_v": normal_values(part_keys[5], (VIDEO_TOKENS, AUDIO_HEADS * AUDIO_DIM), 1.0, 6.0, ((0, 8), (1, 2))),
        "cross_q": draw_cross_q(jax.random.fold_in(jax.random.fold_in(key_of[10], part), 71), part),
        "aud_k": draw_aud_k(jax.random.fold_in(jax.random.fold_in(key_of[10], part), 71), part),
        "aud_v": normal_values(part_keys[8], (AUDIO_TOKENS, AUDIO_HEADS * AUDIO_DIM), 1.0, 6.0, ((0, 8), (1, 2))),
        "windows": draw_windows(jax.random.fold_in(jax.random.fold_in(key_of[10], part), 71), part),
    }


def attend(queries, key_rows, value_rows, scaling, visible):
    scores = jnp.dot(queries, key_rows.T, preferred_element_type=jnp.float32) * scaling
    scores = jnp.where(visible, scores, jnp.float32(-1e30))
    peak = jnp.max(scores, axis=1, keepdims=True)
    weights = jnp.exp(scores - peak)
    summed = jnp.sum(weights, axis=1, keepdims=True)
    mixed = jnp.dot(weights.astype(jnp.bfloat16), value_rows, preferred_element_type=jnp.float32)
    return mixed / summed


def split_heads(matrix, head_count):
    return matrix.reshape(matrix.shape[0], head_count, -1).transpose(1, 0, 2)


def multi_head(queries, key_rows, value_rows, head_count, head_size, visible):
    scaling = 1.0 / (head_size ** 0.5)

    def one_head(triple):
        return attend(triple[0], triple[1], triple[2], scaling, visible)

    stacked = lax.map(one_head, (split_heads(queries, head_count), split_heads(key_rows, head_count), split_heads(value_rows, head_count)))
    return stacked.transpose(1, 0, 2).reshape(queries.shape[0], -1).astype(jnp.bfloat16)


def reference(vid_q, vid_k, vid_v, aud_q, cross_k, cross_v, cross_q, aud_k, aud_v, windows):
    video_self = multi_head(vid_q, vid_k, vid_v, VIDEO_HEADS, HEAD_DIM, True)
    audio_out = multi_head(aud_q, cross_k, cross_v, AUDIO_HEADS, AUDIO_DIM, True)
    video_tile = jnp.arange(VIDEO_TOKENS, dtype=jnp.int32) // TILE_LEN
    audio_stretch = jnp.arange(AUDIO_TOKENS, dtype=jnp.int32) // STRETCH_LEN
    first_tile = windows[0][audio_stretch]
    after_tile = windows[1][audio_stretch]
    visible = (first_tile[None, :] <= video_tile[:, None]) & (video_tile[:, None] < after_tile[None, :])
    video_cross = multi_head(cross_q, aud_k, aud_v, AUDIO_HEADS, AUDIO_DIM, visible)
    return video_self, audio_out, video_cross
```

```python
from functools import partial
import math

import jax
import jax.numpy as jnp
from jax import lax
from jax.experimental import pallas as pl
from jax.experimental.pallas import tpu as pltpu
from jax.sharding import PartitionSpec as P

HEAD_DIM = 128
AUDIO_DIM = 64
TILE_LEN = 32
STRETCH_LEN = 8


def extended(cells, sides, width):
    for axis, dim in sides:
        count = lax.axis_size(axis)
        ends = count - 1
        head = lax.slice_in_dim(cells, 0, width, axis=dim)
        tail = lax.slice_in_dim(cells, cells.shape[dim] - width, cells.shape[dim], axis=dim)
        cells = jnp.concatenate(
            [
                lax.ppermute(tail, axis, [(i, (i + 1) % count) for i in range(ends)]),
                cells,
                lax.ppermute(head, axis, [((i + 1) % count, i) for i in range(ends)]),
            ],
            axis=dim,
        )
    return cells


def start_state(query_count, head_count, head_size):
    running = jnp.full((head_count, query_count), -jnp.inf, jnp.float32)
    summed = jnp.zeros((head_count, query_count), jnp.float32)
    numerator = jnp.zeros((head_count, query_count, head_size), jnp.float32)
    return (running, summed, numerator)


def absorb(state_in, queries, key_rows, value_rows, head_count, scaling, visible):
    running, summed, numerator = state_in
    query_count = queries.shape[0]
    key_count = key_rows.shape[0]
    head_size = queries.shape[1] // head_count
    scores = (
        jnp.einsum(
            "qhe,khe->hqk",
            queries.reshape(query_count, head_count, head_size),
            key_rows.reshape(key_count, head_count, head_size),
            preferred_element_type=jnp.float32,
        )
        * scaling
    )
    if visible is not None:
        scores = jnp.where(visible[None], scores, jnp.float32(-1e30))
    newest = jnp.maximum(running, jnp.max(scores, axis=2))
    shrink = jnp.exp(running - newest)
    weights = jnp.exp(scores - newest[:, :, None])
    summed = summed * shrink + jnp.sum(weights, axis=2)
    numerator = numerator * shrink[:, :, None] + jnp.einsum(
        "hqk,khe->hqe",
        weights.astype(jnp.bfloat16),
        value_rows.reshape(key_count, head_count, head_size),
        preferred_element_type=jnp.float32,
    )
    return (newest, summed, numerator)


def block_split(total_rows):
    block_rows = total_rows
    while block_rows > 512 and block_rows % 2 == 0:
        block_rows = block_rows // 2
    return (block_rows, total_rows // block_rows)


def fold_keys(state_in, shards_in, offset, queries, head_count, scaling):
    key_rows, value_rows = shards_in
    block_rows, block_count = block_split(key_rows.shape[0])
    key_blocks = key_rows.reshape(block_count, block_rows, key_rows.shape[1])
    value_blocks = value_rows.reshape(block_count, block_rows, value_rows.shape[1])

    def one_block(state, paired):
        return (absorb(state, queries, paired[0], paired[1], head_count, scaling, None), None)

    result, unused = lax.scan(one_block, state_in, (key_blocks, value_blocks))
    return result


def normalize_heads(state_in):
    running, summed, numerator = state_in
    mixed = numerator / summed[:, :, None]
    return mixed.transpose(1, 0, 2).reshape(mixed.shape[1], -1).astype(jnp.bfloat16)


def gathered_body(vid_q, vid_k, vid_v, aud_q, cross_k, cross_v, cross_q, aud_k, aud_v, windows):
    video_heads = vid_q.shape[1] // HEAD_DIM
    video_scaling = 1.0 / math.sqrt(HEAD_DIM)
    audio_heads = aud_q.shape[1] // AUDIO_DIM
    audio_scaling = 1.0 / math.sqrt(AUDIO_DIM)
    moved_q, moved_k, moved_v = (
        lax.all_to_all(vid_q, "sub", split_axis=1, concat_axis=0, tiled=True),
        lax.all_to_all(vid_k, "sub", split_axis=1, concat_axis=0, tiled=True),
        lax.all_to_all(vid_v, "sub", split_axis=1, concat_axis=0, tiled=True),
    )
    pair_heads = video_heads // lax.axis_size("sub")
    folder = partial(fold_keys, queries=moved_q, head_count=pair_heads, scaling=video_scaling)
    state = folder(
        start_state(moved_q.shape[0], pair_heads, HEAD_DIM),
        (
            lax.all_gather(moved_k, "seq", axis=0, tiled=True),
            lax.all_gather(moved_v, "seq", axis=0, tiled=True),
        ),
        jnp.int32(0),
    )
    video_self = lax.all_to_all(
        normalize_heads(state), "sub", split_axis=0, concat_axis=1, tiled=True
    )
    folder = partial(fold_keys, queries=aud_q, head_count=audio_heads, scaling=audio_scaling)
    state = folder(
        start_state(aud_q.shape[0], audio_heads, AUDIO_DIM),
        (
            lax.all_gather(cross_k, ("seq", "sub"), axis=0, tiled=True),
            lax.all_gather(cross_v, ("seq", "sub"), axis=0, tiled=True),
        ),
        jnp.int32(0),
    )
    audio_out = normalize_heads(state)
    audio_rows = aud_k.shape[0]
    key_width = aud_k.shape[1]
    padded_rows = extended(
        jnp.concatenate((aud_k, aud_v), axis=1), ((("seq", "sub"), 0),), audio_rows
    )
    near_keys = padded_rows[:, :key_width]
    near_values = padded_rows[:, key_width:]
    position = lax.axis_index(("seq", "sub"))
    audio_index = (position - 1) * audio_rows + jnp.arange(padded_rows.shape[0], dtype=jnp.int32)
    stretch_index = audio_index // STRETCH_LEN
    stretch_ids = jnp.arange(windows.shape[1], dtype=jnp.int32)
    onehot = stretch_index[:, None] == stretch_ids[None, :]
    first_tile = jnp.sum(jnp.where(onehot, windows[0][None, :], 0), axis=1)
    after_tile = jnp.sum(jnp.where(onehot, windows[1][None, :], 0), axis=1)
    video_rows = cross_q.shape[0]
    video_tile = (position * video_rows + jnp.arange(video_rows, dtype=jnp.int32)) // TILE_LEN
    visible = (first_tile[None, :] <= video_tile[:, None]) & (
        video_tile[:, None] < after_tile[None, :]
    )
    state = absorb(
        start_state(video_rows, audio_heads, AUDIO_DIM),
        cross_q,
        near_keys,
        near_values,
        audio_heads,
        audio_scaling,
        visible,
    )
    video_cross = normalize_heads(state)
    return (video_self, audio_out, video_cross)


LANES = 128
AXES = ("seq", "sub")


def softmax_mix(queries, key_rows, value_rows, scaling):
    scores = lax.dot_general(
        queries, key_rows, (((1,), (1,)), ((), ())), preferred_element_type=jnp.float32
    )
    peak = jnp.max(scores, axis=1, keepdims=True)
    weights = jnp.exp2((scores - peak) * jnp.float32(scaling * math.log2(math.e)))
    summed = jnp.sum(weights, axis=1, keepdims=True)
    mixed = jnp.dot(
        weights.astype(jnp.bfloat16), value_rows, preferred_element_type=jnp.float32
    )
    return mixed / summed, peak, summed


def lane_heads(block):
    wide = block.astype(jnp.float32)
    lane = lax.broadcasted_iota(jnp.int32, wide.shape, 1) // AUDIO_DIM
    parts = [jnp.where(lane == i, wide, 0.0) for i in range(LANES // AUDIO_DIM)]
    return jnp.concatenate(parts, axis=0).astype(jnp.bfloat16)


def merge_lane_heads(stacked, rows):
    lane = lax.broadcasted_iota(jnp.int32, (rows, LANES), 1) // AUDIO_DIM
    merged = stacked[:rows]
    for i in range(1, LANES // AUDIO_DIM):
        merged = jnp.where(lane == i, stacked[i * rows : (i + 1) * rows], merged)
    return merged


def exchange_kernel(
    count,
    sub_count,
    vid_q,
    vid_k,
    vid_v,
    aud_q,
    cross_k,
    cross_v,
    cross_q,
    aud_k,
    aud_v,
    windows,
    video_self,
    audio_out,
    video_cross,
    land_q,
    land_k,
    land_v,
    land_aq,
    land_ck,
    land_cv,
    mixed_v,
    mixed_a,
    own_part,
    own_stat,
    far_part,
    far_stat,
    got_part,
    got_stat,
    near_k,
    near_v,
    local_cq,
    send_sem,
    recv_sem,
    near_send,
    near_recv,
    part_send,
    part_recv,
    local_sem,
    ready_sem,
    all_sem,
):
    rows = vid_q.shape[0]
    audio_rows = aud_q.shape[0]
    video_each = vid_q.shape[1] // HEAD_DIM // count
    half = count // 2
    blocks_each = aud_q.shape[1] // LANES // half
    width = blocks_each * LANES
    video_scaling = 1.0 / math.sqrt(HEAD_DIM)
    audio_scaling = 1.0 / math.sqrt(AUDIO_DIM)
    me = lax.axis_index("seq") * sub_count + lax.axis_index("sub")

    side = me // half
    place = me % half

    def device(peer):
        return {"seq": peer // sub_count, "sub": peer % sub_count}

    def peer_at(t):
        return ((side + 1 - t // half) % 2) * half + (place + t + t // half) % half

    def peer_near(t):
        return side * half + (place + 1 + t) % half

    chip = me // sub_count
    core = me % sub_count
    inner = (me >= half - sub_count) & (me < half + sub_count)
    outer = jnp.logical_not(inner)

    def inner_of(which, t):
        return half - (1 - which) * sub_count + (core + t) % sub_count

    def outer_of(which, t):
        return which * (half + sub_count) + (core + t) % sub_count

    def core_peer(t):
        return chip * sub_count + (core + 1 + t) % sub_count

    def near_inner(t):
        return inner_of(side, t)

    def near_outer(t):
        return outer_of(side, t)

    def far_inner(t):
        return inner_of(1 - side, t)

    def far_outer(t):
        return outer_of(1 - side, t)

    def signal(semaphore, peer):
        pl.semaphore_signal(
            semaphore, inc=1, device_id=device(peer), device_id_type=pl.DeviceIdType.MESH
        )

    barrier = pltpu.get_barrier_semaphore()

    @pl.when(inner)
    def _():
        for t in range(sub_count):
            signal(barrier, far_inner(t))

    for t in range(sub_count - 1):
        signal(barrier, core_peer(t))

    own = [
        pltpu.make_async_copy(cross_q, local_cq, local_sem.at[0]),
        pltpu.make_async_copy(aud_k, near_k.at[1], local_sem.at[1]),
        pltpu.make_async_copy(aud_v, near_v.at[1], local_sem.at[2]),
    ]
    for copy in own:
        copy.start()

    def column(index):
        return pl.ds(pl.multiple_of(index * LANES, LANES), LANES)

    def row(index):
        return pl.ds(pl.multiple_of(index * rows, rows), rows)

    def columns(index):
        return pl.ds(pl.multiple_of(index * width, LANES), width)

    def video_way(array, land, h):
        return (
            lambda peer: array.at[:, column(peer * video_each + h)],
            lambda source: land.at[h, row(source), :],
            peer_at,
            count - 1,
            land.at[h],
            land.at[h, pl.ds(0, (count - 1) * rows), :],
        )

    def half_way(array, land):
        return (
            lambda peer: array.at[:, columns(peer % half)],
            lambda source: land.at[row(source % half), :],
            peer_near,
            half - 1,
            land,
            land.at[pl.ds(0, (half - 1) * rows), :],
        )

    ways = [
        (
            lambda peer: aud_q.at[:, columns(peer % half)],
            lambda source: land_aq.at[source],
            peer_at,
            count - 1,
            land_aq,
            land_aq.at[pl.ds(0, count - 1)],
        )
    ]
    audio_ways = [0]
    video_ways = []
    for h in range(video_each):
        video_ways.append(list(range(len(ways), len(ways) + 3)))
        for array, land in ((vid_k, land_k), (vid_v, land_v), (vid_q, land_q)):
            ways.append(video_way(array, land, h))
        if h == 0:
            for array, land in ((cross_k, land_ck), (cross_v, land_cv)):
                audio_ways.append(len(ways))
                ways.append(half_way(array, land))
    first = len(ways)
    early = audio_ways[:1] + video_ways[0]
    late = [k for kinds in video_ways[1:] for k in kinds]
    for h in range(video_each):
        ways.append(
            (
                lambda peer, h=h: mixed_v.at[h, row(peer), :],
                lambda source, h=h: video_self.at[:, column(source * video_each + h)],
                peer_at,
                count - 1,
                mixed_v.at[h],
                mixed_v.at[h, pl.ds(0, (count - 1) * rows), :],
            )
        )
    ways.append(
        (
            lambda peer: mixed_a.at[peer % half],
            lambda source: audio_out.at[:, columns(source % half)],
            peer_near,
            half - 1,
            mixed_a,
            mixed_a.at[pl.ds(0, half - 1)],
        )
    )

    def outgoing(k, peer):
        return pltpu.make_async_remote_copy(
            src_ref=ways[k][0](peer),
            dst_ref=ways[k][1](me),
            send_sem=send_sem.at[k],
            recv_sem=recv_sem.at[k],
            device_id=device(peer),
            device_id_type=pl.DeviceIdType.MESH,
        )

    def kept(k):
        return pltpu.make_async_copy(ways[k][0](me), ways[k][1](me), recv_sem.at[k])

    def await_stream(k):
        pltpu.make_async_copy(ways[k][4], ways[k][4], recv_sem.at[k]).wait()

    def await_sent(k):
        pltpu.make_async_copy(ways[k][5], ways[k][5], send_sem.at[k]).wait()

    def near_copy(j, array, near, side, peer):
        return pltpu.make_async_remote_copy(
            src_ref=array,
            dst_ref=near.at[side],
            send_sem=near_send.at[j],
            recv_sem=near_recv.at[j],
            device_id=device(peer),
            device_id_type=pl.DeviceIdType.MESH,
        )

    near_pairs = ((0, aud_k, near_k), (1, aud_v, near_v))

    def send_right():
        for j, array, near in near_pairs:
            near_copy(j, array, near, 0, me + 1).start()

    def send_left():
        for j, array, near in near_pairs:
            near_copy(2 + j, array, near, 2, me - 1).start()

    def send(k, peer_of, steps):
        def one(t, carry):
            outgoing(k, peer_of(t)).start()
            return carry

        lax.fori_loop(0, steps, one, 0)

    pair = sub_count - 1
    audio_only = audio_ways[1:]

    def send_keep(ks):
        for k in ks:
            send(k, core_peer, pair)
            kept(k).start()

    @pl.when(inner)
    def _():
        pl.semaphore_wait(barrier, 2 * sub_count - 1)
        for t in range(sub_count):
            signal(barrier, near_outer(t))
        for k in early + late:
            send(k, far_inner, sub_count)

        @pl.when(side == 0)
        def _():
            send_right()

            @pl.when(core > 0)
            def _():
                send_left()

        @pl.when(side == 1)
        def _():
            send_left()

            @pl.when(core < sub_count - 1)
            def _():
                send_right()

        send_keep(early + audio_only + late)
        pl.semaphore_wait(ready_sem.at[side], sub_count)

        @pl.when((side == 0) & (core == 0))
        def _():
            send_left()

        @pl.when((side == 1) & (core == sub_count - 1))
        def _():
            send_right()

        for k in early[:1] + audio_only + early[1:] + late:
            send(k, near_outer, sub_count)

        pl.semaphore_wait(ready_sem.at[1 - side], sub_count)
        signal(all_sem, near_outer(0))
        for k in early + late:
            send(k, far_outer, sub_count)

    @pl.when(outer)
    def _():
        pl.semaphore_wait(barrier, 2 * sub_count - 1)
        for t in range(sub_count):
            signal(ready_sem.at[side], near_inner(t))
            signal(ready_sem.at[side], far_inner(t))

        for k in early[:1]:
            send(k, far_inner, sub_count)

        @pl.when(me < count - 1)
        def _():
            send_right()

        @pl.when(me > 0)
        def _():
            send_left()

        for k in early[:1] + audio_only + early[1:] + late:
            send(k, near_inner, sub_count)
        send_keep(early + audio_only + late)
        for k in early[1:]:
            send(k, far_inner, sub_count)
        pl.semaphore_wait(all_sem, 1)
        for k in early:
            send(k, far_outer, sub_count)
        for k in late:
            send(k, far_inner, sub_count)
            send(k, far_outer, sub_count)

    @pl.when(me == 0)
    def _():
        for j, array, near in near_pairs:
            near[0] = jnp.zeros(near.shape[1:], near.dtype)

    @pl.when(me == count - 1)
    def _():
        for j, array, near in near_pairs:
            near[2] = jnp.zeros(near.shape[1:], near.dtype)

    for copy in own:
        copy.wait()

    @pl.when(me > 0)
    def _():
        for j, array, near in near_pairs:
            near_copy(j, array, near, 0, me - 1).wait_recv()

    @pl.when(me < count - 1)
    def _():
        for j, array, near in near_pairs:
            near_copy(2 + j, array, near, 2, me + 1).wait_recv()

    spans = windows.shape[1]
    tile = (me * rows + lax.broadcasted_iota(jnp.int32, (rows, spans), 0)) // TILE_LEN
    bounds = windows[...]
    inside = (bounds[0:1, :] <= tile) & (tile < bounds[1:2, :])
    inside = jnp.where(inside, 1.0, 0.0).astype(jnp.bfloat16)
    seen = []
    for slot in range(3):
        stretch = lax.broadcasted_iota(jnp.int32, (spans, audio_rows), 1) // STRETCH_LEN
        stretch = stretch + (me + slot - 1) * (audio_rows // STRETCH_LEN)
        picks = stretch == lax.broadcasted_iota(jnp.int32, (spans, audio_rows), 0)
        picks = jnp.where(picks, 1.0, 0.0).astype(jnp.bfloat16)
        part = jnp.dot(inside, picks, preferred_element_type=jnp.float32)
        seen.append(jnp.concatenate([part] * (LANES // AUDIO_DIM), axis=0))

    for b in range(cross_q.shape[1] // LANES):
        lanes = slice(b * LANES, (b + 1) * LANES)
        stacked = lane_heads(local_cq[:, lanes])
        scores = []
        for slot in range(3):
            part = lax.dot_general(
                stacked,
                near_k[slot, :, lanes],
                (((1,), (1,)), ((), ())),
                preferred_element_type=jnp.float32,
            )
            scores.append(jnp.where(seen[slot] > 0.5, part, jnp.float32(-1e30)))
        peak = jnp.max(jnp.maximum(jnp.maximum(scores[0], scores[1]), scores[2]), axis=1, keepdims=True)
        factor = jnp.float32(audio_scaling * math.log2(math.e))
        weights = [jnp.exp2((part - peak) * factor) for part in scores]
        summed = jnp.sum(weights[0] + weights[1] + weights[2], axis=1, keepdims=True)
        mixed = sum(
            jnp.dot(
                weights[slot].astype(jnp.bfloat16),
                near_v[slot, :, lanes],
                preferred_element_type=jnp.float32,
            )
            for slot in range(3)
        )
        video_cross[:, lanes] = merge_lane_heads(mixed / summed, rows).astype(jnp.bfloat16)

    def run_blocks(k, steps, mix):
        def one(t, carry):
            mix(ways[k][2](t))

            @pl.when(t > 0)
            def _():
                outgoing(k, ways[k][2](t - 1)).start()

            return carry

        lax.fori_loop(0, steps, one, 0)
        kept(k).start()

    def part_copy(j, array, land):
        return pltpu.make_async_remote_copy(
            src_ref=array,
            dst_ref=land,
            send_sem=part_send.at[j],
            recv_sem=part_recv.at[j],
            device_id=device((me + half) % count),
            device_id_type=pl.DeviceIdType.MESH,
        )

    part_copies = [part_copy(0, far_part, got_part), part_copy(1, far_stat, got_stat)]
    stat_lane = lax.broadcasted_iota(jnp.int32, (audio_rows, LANES), 1)
    each = LANES // AUDIO_DIM

    def audio_parts(first_source, part, stat):
        def one(j, stats):
            queries = land_aq[first_source + j]
            for b in range(blocks_each):
                lanes = slice(b * LANES, (b + 1) * LANES)
                mixed, peak, summed = softmax_mix(
                    lane_heads(queries[:, lanes]), land_ck[:, lanes], land_cv[:, lanes], audio_scaling
                )
                part[j, :, lanes] = merge_lane_heads(mixed, audio_rows).astype(part.dtype)
                level = peak * jnp.float32(audio_scaling * math.log2(math.e)) + jnp.log2(summed)
                for i in range(each):
                    stats = jnp.where(
                        stat_lane == (j * blocks_each + b) * each + i,
                        level[i * audio_rows : (i + 1) * audio_rows],
                        stats,
                    )
            return stats

        stats = lax.fori_loop(0, half, one, jnp.zeros((audio_rows, LANES), jnp.float32))
        padded = jnp.concatenate(
            [stats, jnp.zeros((LANES - audio_rows, LANES), jnp.float32)], axis=0
        )
        stat[...] = padded.T[: stat.shape[0]]

    def merge_parts(peer):
        j = peer % half
        unpacked = []
        for stat in (own_stat, got_stat):
            rest = jnp.zeros((LANES - stat.shape[0], LANES), jnp.float32)
            unpacked.append(jnp.concatenate([stat[...], rest], axis=0).T[:audio_rows])
        for b in range(blocks_each):
            lanes = slice(b * LANES, (b + 1) * LANES)
            shares = []
            for i in range(each):
                picked = stat_lane == (j * blocks_each + b) * each + i
                mine = jnp.sum(jnp.where(picked, unpacked[0], 0.0), axis=1, keepdims=True)
                other = jnp.sum(jnp.where(picked, unpacked[1], 0.0), axis=1, keepdims=True)
                peak = jnp.maximum(mine, other)
                mine = jnp.exp2(mine - peak)
                other = jnp.exp2(other - peak)
                total = mine + other
                shares.append((mine / total, other / total))
            own_share, got_share = (
                merge_lane_heads(
                    jnp.concatenate(
                        [jnp.broadcast_to(s[w], (audio_rows, LANES)) for s in shares], axis=0
                    ),
                    audio_rows,
                )
                for w in range(2)
            )
            merged = own_part[j, :, lanes] * own_share
            merged = merged + got_part[j, :, lanes].astype(jnp.float32) * got_share
            mixed_a[j, :, lanes] = merged.astype(jnp.bfloat16)

    for h in range(video_each):
        for k in video_ways[h]:
            await_stream(k)

        def mix_video(source, h=h):
            mixed, peak, summed = softmax_mix(
                land_q[h, row(source), :], land_k[h], land_v[h], video_scaling
            )
            mixed_v[h, row(source), :] = mixed.astype(jnp.bfloat16)

        run_blocks(first + h, count, mix_video)
        if h == 0:
            for k in audio_ways:
                await_stream(k)
            audio_parts((1 - side) * half, far_part, far_stat)
            audio_parts(side * half, own_part, own_stat)
            for copy in part_copies:
                copy.start()
    for copy in part_copies:
        copy.wait()
    run_blocks(len(ways) - 1, half, merge_parts)

    for k in range(len(ways)):
        await_sent(k)
    for k in range(first, len(ways)):
        await_stream(k)

    @pl.when(me < count - 1)
    def _():
        for j, array, near in near_pairs:
            near_copy(j, array, near, 0, me + 1).wait_send()

    @pl.when(me > 0)
    def _():
        for j, array, near in near_pairs:
            near_copy(2 + j, array, near, 2, me - 1).wait_send()


def store_kernel(*refs):
    copies = [pltpu.make_async_copy(refs[i], refs[3 + i], refs[6].at[i]) for i in range(3)]
    for copy in copies:
        copy.start()
    for copy in copies:
        copy.wait()


def exchanged_body(count, sub_count, *arrays):
    vid_q, vid_k, vid_v, aud_q, cross_k, cross_v, cross_q, aud_k, aud_v, windows = arrays
    rows = vid_q.shape[0]
    audio_rows = aud_q.shape[0]
    video_each = vid_q.shape[1] // HEAD_DIM // count
    halves = count // 2
    width = aud_q.shape[1] // halves
    kinds = 4 * video_each + 4
    levels = -(-aud_q.shape[1] // AUDIO_DIM // 8) * 8
    half = jnp.bfloat16
    place = pl.BlockSpec(memory_space=pl.ANY)
    held = pl.pallas_call(
        partial(exchange_kernel, count, sub_count),
        out_shape=tuple(pltpu.VMEM(a.shape, half) for a in (vid_q, aud_q, cross_q)),
        in_specs=[place] * 9 + [pl.BlockSpec(memory_space=pltpu.VMEM)],
        out_specs=(pl.BlockSpec(memory_space=pltpu.VMEM),) * 3,
        scratch_shapes=[
            pltpu.VMEM((video_each, count * rows, HEAD_DIM), half),
            pltpu.VMEM((video_each, count * rows, HEAD_DIM), half),
            pltpu.VMEM((video_each, count * rows, HEAD_DIM), half),
            pltpu.VMEM((count, audio_rows, width), half),
            pltpu.VMEM((halves * rows, width), half),
            pltpu.VMEM((halves * rows, width), half),
            pltpu.VMEM((video_each, count * rows, HEAD_DIM), half),
            pltpu.VMEM((halves, audio_rows, width), half),
            pltpu.VMEM((halves, audio_rows, width), jnp.float32),
            pltpu.VMEM((levels, LANES), jnp.float32),
            pltpu.VMEM((halves, audio_rows, width), half),
            pltpu.VMEM((levels, LANES), jnp.float32),
            pltpu.VMEM((halves, audio_rows, width), half),
            pltpu.VMEM((levels, LANES), jnp.float32),
            pltpu.VMEM((3, audio_rows, aud_k.shape[1]), half),
            pltpu.VMEM((3, audio_rows, aud_k.shape[1]), half),
            pltpu.VMEM(cross_q.shape, half),
            pltpu.SemaphoreType.DMA((kinds,)),
            pltpu.SemaphoreType.DMA((kinds,)),
            pltpu.SemaphoreType.DMA((4,)),
            pltpu.SemaphoreType.DMA((4,)),
            pltpu.SemaphoreType.DMA((2,)),
            pltpu.SemaphoreType.DMA((2,)),
            pltpu.SemaphoreType.DMA((3,)),
            pltpu.SemaphoreType.REGULAR((2,)),
            pltpu.SemaphoreType.REGULAR,
        ],
        compiler_params=pltpu.CompilerParams(collective_id=0, has_side_effects=True),
        name="joint_attention",
    )(*arrays)
    return pl.pallas_call(
        store_kernel,
        out_shape=tuple(jax.ShapeDtypeStruct(a.shape, half) for a in (vid_q, aud_q, cross_q)),
        in_specs=[pl.BlockSpec(memory_space=pltpu.VMEM)] * 3,
        out_specs=(place, place, place),
        scratch_shapes=[pltpu.SemaphoreType.DMA((3,))],
        name="store_results",
    )(*[pltpu.with_memory_space_constraint(x, pltpu.VMEM) for x in held])


def body(*arrays):
    sub_count = lax.axis_size("sub")
    count = lax.axis_size("seq") * sub_count
    video_heads = arrays[0].shape[1] // HEAD_DIM
    audio_heads = arrays[3].shape[1] // AUDIO_DIM
    halved = count == 4 * sub_count and max(audio_heads, arrays[3].shape[0]) <= LANES
    if halved and video_heads % count == 0 and audio_heads % count == 0:
        return exchanged_body(count, sub_count, *arrays)
    return gathered_body(*arrays)


def solution(mesh):
    return jax.shard_map(
        body,
        mesh=mesh,
        in_specs=(
            P(("grp", "seq", "sub"), "head"),
            P(("grp", "seq", "sub"), "head"),
            P(("grp", "seq", "sub"), "head"),
            P(("grp", "seq", "sub"), "head"),
            P(("grp", "seq", "sub"), "head"),
            P(("grp", "seq", "sub"), "head"),
            P(("grp", "seq", "sub"), "head"),
            P(("grp", "seq", "sub"), "head"),
            P(("grp", "seq", "sub"), "head"),
            P(None, "grp"),
        ),
        out_specs=(
            P(("grp", "seq", "sub"), "head"),
            P(("grp", "seq", "sub"), "head"),
            P(("grp", "seq", "sub"), "head"),
        ),
        check_vma=False,
    )
```

```python
from functools import partial
import math

import jax
import jax.numpy as jnp
from jax import lax
from jax.experimental import pallas as pl
from jax.experimental.pallas import tpu as pltpu
from jax.sharding import PartitionSpec as P

HEAD_DIM = 128
AUDIO_DIM = 64
TILE_LEN = 32
STRETCH_LEN = 8


def extended(cells, sides, width):
    for axis, dim in sides:
        count = lax.axis_size(axis)
        ends = count - 1
        head = lax.slice_in_dim(cells, 0, width, axis=dim)
        tail = lax.slice_in_dim(cells, cells.shape[dim] - width, cells.shape[dim], axis=dim)
        cells = jnp.concatenate(
            [
                lax.ppermute(tail, axis, [(i, (i + 1) % count) for i in range(ends)]),
                cells,
                lax.ppermute(head, axis, [((i + 1) % count, i) for i in range(ends)]),
            ],
            axis=dim,
        )
    return cells


def start_state(query_count, head_count, head_size):
    running = jnp.full((head_count, query_count), -jnp.inf, jnp.float32)
    summed = jnp.zeros((head_count, query_count), jnp.float32)
    numerator = jnp.zeros((head_count, query_count, head_size), jnp.float32)
    return (running, summed, numerator)


def absorb(state_in, queries, key_rows, value_rows, head_count, scaling, visible):
    running, summed, numerator = state_in
    query_count = queries.shape[0]
    key_count = key_rows.shape[0]
    head_size = queries.shape[1] // head_count
    scores = (
        jnp.einsum(
            "qhe,khe->hqk",
            queries.reshape(query_count, head_count, head_size),
            key_rows.reshape(key_count, head_count, head_size),
            preferred_element_type=jnp.float32,
        )
        * scaling
    )
    if visible is not None:
        scores = jnp.where(visible[None], scores, jnp.float32(-1e30))
    newest = jnp.maximum(running, jnp.max(scores, axis=2))
    shrink = jnp.exp(running - newest)
    weights = jnp.exp(scores - newest[:, :, None])
    summed = summed * shrink + jnp.sum(weights, axis=2)
    numerator = numerator * shrink[:, :, None] + jnp.einsum(
        "hqk,khe->hqe",
        weights.astype(jnp.bfloat16),
        value_rows.reshape(key_count, head_count, head_size),
        preferred_element_type=jnp.float32,
    )
    return (newest, summed, numerator)


def block_split(total_rows):
    block_rows = total_rows
    while block_rows > 512 and block_rows % 2 == 0:
        block_rows = block_rows // 2
    return (block_rows, total_rows // block_rows)


def fold_keys(state_in, shards_in, offset, queries, head_count, scaling):
    key_rows, value_rows = shards_in
    block_rows, block_count = block_split(key_rows.shape[0])
    key_blocks = key_rows.reshape(block_count, block_rows, key_rows.shape[1])
    value_blocks = value_rows.reshape(block_count, block_rows, value_rows.shape[1])

    def one_block(state, paired):
        return (absorb(state, queries, paired[0], paired[1], head_count, scaling, None), None)

    result, unused = lax.scan(one_block, state_in, (key_blocks, value_blocks))
    return result


def normalize_heads(state_in):
    running, summed, numerator = state_in
    mixed = numerator / summed[:, :, None]
    return mixed.transpose(1, 0, 2).reshape(mixed.shape[1], -1).astype(jnp.bfloat16)


def gathered_body(vid_q, vid_k, vid_v, aud_q, cross_k, cross_v, cross_q, aud_k, aud_v, windows):
    video_heads = vid_q.shape[1] // HEAD_DIM
    video_scaling = 1.0 / math.sqrt(HEAD_DIM)
    audio_heads = aud_q.shape[1] // AUDIO_DIM
    audio_scaling = 1.0 / math.sqrt(AUDIO_DIM)
    moved_q, moved_k, moved_v = (
        lax.all_to_all(vid_q, "sub", split_axis=1, concat_axis=0, tiled=True),
        lax.all_to_all(vid_k, "sub", split_axis=1, concat_axis=0, tiled=True),
        lax.all_to_all(vid_v, "sub", split_axis=1, concat_axis=0, tiled=True),
    )
    pair_heads = video_heads // lax.axis_size("sub")
    folder = partial(fold_keys, queries=moved_q, head_count=pair_heads, scaling=video_scaling)
    state = folder(
        start_state(moved_q.shape[0], pair_heads, HEAD_DIM),
        (
            lax.all_gather(moved_k, "seq", axis=0, tiled=True),
            lax.all_gather(moved_v, "seq", axis=0, tiled=True),
        ),
        jnp.int32(0),
    )
    video_self = lax.all_to_all(
        normalize_heads(state), "sub", split_axis=0, concat_axis=1, tiled=True
    )
    folder = partial(fold_keys, queries=aud_q, head_count=audio_heads, scaling=audio_scaling)
    state = folder(
        start_state(aud_q.shape[0], audio_heads, AUDIO_DIM),
        (
            lax.all_gather(cross_k, ("seq", "sub"), axis=0, tiled=True),
            lax.all_gather(cross_v, ("seq", "sub"), axis=0, tiled=True),
        ),
        jnp.int32(0),
    )
    audio_out = normalize_heads(state)
    audio_rows = aud_k.shape[0]
    key_width = aud_k.shape[1]
    padded_rows = extended(
        jnp.concatenate((aud_k, aud_v), axis=1), ((("seq", "sub"), 0),), audio_rows
    )
    near_keys = padded_rows[:, :key_width]
    near_values = padded_rows[:, key_width:]
    position = lax.axis_index(("seq", "sub"))
    audio_index = (position - 1) * audio_rows + jnp.arange(padded_rows.shape[0], dtype=jnp.int32)
    stretch_index = audio_index // STRETCH_LEN
    stretch_ids = jnp.arange(windows.shape[1], dtype=jnp.int32)
    onehot = stretch_index[:, None] == stretch_ids[None, :]
    first_tile = jnp.sum(jnp.where(onehot, windows[0][None, :], 0), axis=1)
    after_tile = jnp.sum(jnp.where(onehot, windows[1][None, :], 0), axis=1)
    video_rows = cross_q.shape[0]
    video_tile = (position * video_rows + jnp.arange(video_rows, dtype=jnp.int32)) // TILE_LEN
    visible = (first_tile[None, :] <= video_tile[:, None]) & (
        video_tile[:, None] < after_tile[None, :]
    )
    state = absorb(
        start_state(video_rows, audio_heads, AUDIO_DIM),
        cross_q,
        near_keys,
        near_values,
        audio_heads,
        audio_scaling,
        visible,
    )
    video_cross = normalize_heads(state)
    return (video_self, audio_out, video_cross)


LANES = 128
AXES = ("seq", "sub")


def softmax_mix(queries, key_rows, value_rows, scaling):
    scores = lax.dot_general(
        queries, key_rows, (((1,), (1,)), ((), ())), preferred_element_type=jnp.float32
    )
    peak = jnp.max(scores, axis=1, keepdims=True)
    weights = jnp.exp2((scores - peak) * jnp.float32(scaling * math.log2(math.e)))
    summed = jnp.sum(weights, axis=1, keepdims=True)
    mixed = jnp.dot(
        weights.astype(jnp.bfloat16), value_rows, preferred_element_type=jnp.float32
    )
    return mixed / summed, peak, summed


def lane_heads(block):
    wide = block.astype(jnp.float32)
    lane = lax.broadcasted_iota(jnp.int32, wide.shape, 1) // AUDIO_DIM
    parts = [jnp.where(lane == i, wide, 0.0) for i in range(LANES // AUDIO_DIM)]
    return jnp.concatenate(parts, axis=0).astype(jnp.bfloat16)


def merge_lane_heads(stacked, rows):
    lane = lax.broadcasted_iota(jnp.int32, (rows, LANES), 1) // AUDIO_DIM
    merged = stacked[:rows]
    for i in range(1, LANES // AUDIO_DIM):
        merged = jnp.where(lane == i, stacked[i * rows : (i + 1) * rows], merged)
    return merged


def exchange_kernel(
    count,
    sub_count,
    vid_q,
    vid_k,
    vid_v,
    aud_q,
    cross_k,
    cross_v,
    cross_q,
    aud_k,
    aud_v,
    windows,
    video_self,
    audio_out,
    video_cross,
    land_q,
    land_k,
    land_v,
    land_aq,
    land_ck,
    land_cv,
    mixed_v,
    mixed_a,
    own_part,
    own_stat,
    far_part,
    far_stat,
    got_part,
    got_stat,
    near_k,
    near_v,
    local_cq,
    local_windows,
    send_sem,
    recv_sem,
    near_send,
    near_recv,
    part_send,
    part_recv,
    local_sem,
    ready_sem,
    all_sem,
):
    rows = vid_q.shape[0]
    audio_rows = aud_q.shape[0]
    video_each = vid_q.shape[1] // HEAD_DIM // count
    half = count // 2
    blocks_each = aud_q.shape[1] // LANES // half
    width = blocks_each * LANES
    video_scaling = 1.0 / math.sqrt(HEAD_DIM)
    audio_scaling = 1.0 / math.sqrt(AUDIO_DIM)
    me = lax.axis_index("seq") * sub_count + lax.axis_index("sub")

    side = me // half
    place = me % half

    def device(peer):
        return {"seq": peer // sub_count, "sub": peer % sub_count}

    def peer_at(t):
        return ((side + 1 - t // half) % 2) * half + (place + t + t // half) % half

    def peer_near(t):
        return side * half + (place + 1 + t) % half

    chip = me // sub_count
    core = me % sub_count
    inner = (me >= half - sub_count) & (me < half + sub_count)
    outer = jnp.logical_not(inner)

    def inner_of(which, t):
        return half - (1 - which) * sub_count + (core + t) % sub_count

    def outer_of(which, t):
        return which * (half + sub_count) + (core + t) % sub_count

    def core_peer(t):
        return chip * sub_count + (core + 1 + t) % sub_count

    def near_inner(t):
        return inner_of(side, t)

    def near_outer(t):
        return outer_of(side, t)

    def far_inner(t):
        return inner_of(1 - side, t)

    def far_outer(t):
        return outer_of(1 - side, t)

    def out_peer(t):
        turn = t // sub_count
        chips = count // sub_count
        there = jnp.where(turn == 1, chips // 2 - side, chip)
        there = jnp.where(turn == 0, (1 - side) * (chips - 1), there)
        there = jnp.where(turn == 2, 2 * (chip // 2) + 1 - chip % 2, there)
        shift = t + turn // (chips - 1)
        return there * sub_count + (core + shift) % sub_count

    def signal(semaphore, peer):
        pl.semaphore_signal(
            semaphore, inc=1, device_id=device(peer), device_id_type=pl.DeviceIdType.MESH
        )

    barrier = pltpu.get_barrier_semaphore()

    @pl.when(inner)
    def _():
        for t in range(sub_count):
            signal(barrier, far_inner(t))

    for t in range(sub_count - 1):
        signal(barrier, core_peer(t))

    own = [
        pltpu.make_async_copy(cross_q, local_cq, local_sem.at[0]),
        pltpu.make_async_copy(aud_k, near_k.at[1], local_sem.at[1]),
        pltpu.make_async_copy(aud_v, near_v.at[1], local_sem.at[2]),
        pltpu.make_async_copy(windows, local_windows, local_sem.at[3]),
    ]
    for copy in own:
        copy.start()

    def column(index):
        return pl.ds(pl.multiple_of(index * LANES, LANES), LANES)

    def row(index):
        return pl.ds(pl.multiple_of(index * rows, rows), rows)

    def columns(index):
        return pl.ds(pl.multiple_of(index * width, LANES), width)

    def video_way(array, land, h):
        return (
            lambda peer: array.at[:, column(peer * video_each + h)],
            lambda source: land.at[h, row(source), :],
            peer_at,
            count - 1,
            land.at[h],
            land.at[h, pl.ds(0, (count - 1) * rows), :],
        )

    def half_way(array, land):
        return (
            lambda peer: array.at[:, columns(peer % half)],
            lambda source: land.at[row(source % half), :],
            peer_near,
            half - 1,
            land,
            land.at[pl.ds(0, (half - 1) * rows), :],
        )

    ways = [
        (
            lambda peer: aud_q.at[:, columns(peer % half)],
            lambda source: land_aq.at[source],
            peer_at,
            count - 1,
            land_aq,
            land_aq.at[pl.ds(0, count - 1)],
        )
    ]
    audio_ways = [0]
    video_ways = []
    for h in range(video_each):
        video_ways.append(list(range(len(ways), len(ways) + 3)))
        for array, land in ((vid_k, land_k), (vid_v, land_v), (vid_q, land_q)):
            ways.append(video_way(array, land, h))
        if h == 0:
            for array, land in ((cross_k, land_ck), (cross_v, land_cv)):
                audio_ways.append(len(ways))
                ways.append(half_way(array, land))
    first = len(ways)
    early = audio_ways[:1] + video_ways[0]
    late = [k for kinds in video_ways[1:] for k in kinds]
    for h in range(video_each):
        ways.append(
            (
                lambda peer, h=h: mixed_v.at[h, row(peer), :],
                lambda source, h=h: video_self.at[:, column(source * video_each + h)],
                out_peer,
                count - 1,
                mixed_v.at[h],
                mixed_v.at[h, pl.ds(0, (count - 1) * rows), :],
            )
        )
    ways.append(
        (
            lambda peer: mixed_a.at[peer % half],
            lambda source: audio_out.at[:, columns(source % half)],
            peer_near,
            half - 1,
            mixed_a,
            mixed_a.at[pl.ds(0, half - 1)],
        )
    )

    def outgoing(k, peer):
        return pltpu.make_async_remote_copy(
            src_ref=ways[k][0](peer),
            dst_ref=ways[k][1](me),
            send_sem=send_sem.at[k],
            recv_sem=recv_sem.at[k],
            device_id=device(peer),
            device_id_type=pl.DeviceIdType.MESH,
        )

    def kept(k):
        return pltpu.make_async_copy(ways[k][0](me), ways[k][1](me), recv_sem.at[k])

    def await_stream(k):
        pltpu.make_async_copy(ways[k][4], ways[k][4], recv_sem.at[k]).wait()

    def await_sent(k):
        pltpu.make_async_copy(ways[k][5], ways[k][5], send_sem.at[k]).wait()

    def near_copy(j, array, near, side, peer):
        return pltpu.make_async_remote_copy(
            src_ref=array,
            dst_ref=near.at[side],
            send_sem=near_send.at[j],
            recv_sem=near_recv.at[j],
            device_id=device(peer),
            device_id_type=pl.DeviceIdType.MESH,
        )

    near_pairs = ((0, aud_k, near_k), (1, aud_v, near_v))

    def send_right():
        for j, array, near in near_pairs:
            near_copy(j, array, near, 0, me + 1).start()

    def send_left():
        for j, array, near in near_pairs:
            near_copy(2 + j, array, near, 2, me - 1).start()

    def send(k, peer_of, steps):
        def one(t, carry):
            outgoing(k, peer_of(t)).start()
            return carry

        lax.fori_loop(0, steps, one, 0)

    pair = sub_count - 1
    audio_only = audio_ways[1:]

    def send_keep(ks):
        for k in ks:
            send(k, core_peer, pair)
            kept(k).start()

    @pl.when(inner)
    def _():
        pl.semaphore_wait(barrier, 2 * sub_count - 1)
        for t in range(sub_count):
            signal(barrier, near_outer(t))
        for k in early:
            send(k, far_inner, sub_count)

        @pl.when(side == 0)
        def _():
            send_right()

            @pl.when(core > 0)
            def _():
                send_left()

        @pl.when(side == 1)
        def _():
            send_left()

            @pl.when(core < sub_count - 1)
            def _():
                send_right()

        send_keep(early[:1] + audio_only)
        pl.semaphore_wait(ready_sem.at[side], sub_count)

        @pl.when((side == 0) & (core == 0))
        def _():
            send_left()

        @pl.when((side == 1) & (core == sub_count - 1))
        def _():
            send_right()

        for k in early[:1] + audio_only + early[1:] + late:
            send(k, near_outer, sub_count)
        pl.semaphore_wait(ready_sem.at[1 - side], sub_count)
        signal(all_sem, near_outer(0))
        for k in early:
            send(k, far_outer, sub_count)
        for k in late:
            send(k, far_inner, sub_count)
        for k in late:
            send(k, far_outer, sub_count)
        send_keep(early[1:] + late)

    @pl.when(outer)
    def _():
        pl.semaphore_wait(barrier, 2 * sub_count - 1)
        for t in range(sub_count):
            signal(ready_sem.at[side], near_inner(t))
            signal(ready_sem.at[side], far_inner(t))

        for k in early[:1]:
            send(k, far_inner, sub_count)

        @pl.when(me < count - 1)
        def _():
            send_right()

        @pl.when(me > 0)
        def _():
            send_left()

        for k in early[:1] + audio_only:
            send(k, near_inner, sub_count)
        send_keep(early[:1] + audio_only)
        pl.semaphore_wait(all_sem, 1)
        for k in early[:1]:
            send(k, far_outer, sub_count)
        for k in early[1:] + late:
            send(k, near_inner, sub_count)
        for ks in (early[1:], late):
            for k in ks:
                send(k, far_outer, sub_count)
            for k in ks:
                send(k, far_inner, sub_count)
        send_keep(early[1:] + late)

    @pl.when(me == 0)
    def _():
        for j, array, near in near_pairs:
            near[0] = jnp.zeros(near.shape[1:], near.dtype)

    @pl.when(me == count - 1)
    def _():
        for j, array, near in near_pairs:
            near[2] = jnp.zeros(near.shape[1:], near.dtype)

    for copy in own:
        copy.wait()

    @pl.when(me > 0)
    def _():
        for j, array, near in near_pairs:
            near_copy(j, array, near, 0, me - 1).wait_recv()

    @pl.when(me < count - 1)
    def _():
        for j, array, near in near_pairs:
            near_copy(2 + j, array, near, 2, me + 1).wait_recv()

    spans = windows.shape[1]
    tile = (me * rows + lax.broadcasted_iota(jnp.int32, (rows, spans), 0)) // TILE_LEN
    bounds = local_windows[...]
    inside = (bounds[0:1, :] <= tile) & (tile < bounds[1:2, :])
    inside = jnp.where(inside, 1.0, 0.0).astype(jnp.bfloat16)
    seen = []
    for slot in range(3):
        stretch = lax.broadcasted_iota(jnp.int32, (spans, audio_rows), 1) // STRETCH_LEN
        stretch = stretch + (me + slot - 1) * (audio_rows // STRETCH_LEN)
        picks = stretch == lax.broadcasted_iota(jnp.int32, (spans, audio_rows), 0)
        picks = jnp.where(picks, 1.0, 0.0).astype(jnp.bfloat16)
        part = jnp.dot(inside, picks, preferred_element_type=jnp.float32)
        seen.append(jnp.concatenate([part] * (LANES // AUDIO_DIM), axis=0))

    for b in range(cross_q.shape[1] // LANES):
        lanes = slice(b * LANES, (b + 1) * LANES)
        stacked = lane_heads(local_cq[:, lanes])
        scores = []
        for slot in range(3):
            part = lax.dot_general(
                stacked,
                near_k[slot, :, lanes],
                (((1,), (1,)), ((), ())),
                preferred_element_type=jnp.float32,
            )
            scores.append(jnp.where(seen[slot] > 0.5, part, jnp.float32(-1e30)))
        peak = jnp.max(jnp.maximum(jnp.maximum(scores[0], scores[1]), scores[2]), axis=1, keepdims=True)
        factor = jnp.float32(audio_scaling * math.log2(math.e))
        weights = [jnp.exp2((part - peak) * factor) for part in scores]
        summed = jnp.sum(weights[0] + weights[1] + weights[2], axis=1, keepdims=True)
        mixed = sum(
            jnp.dot(
                weights[slot].astype(jnp.bfloat16),
                near_v[slot, :, lanes],
                preferred_element_type=jnp.float32,
            )
            for slot in range(3)
        )
        video_cross[:, lanes] = merge_lane_heads(mixed / summed, rows).astype(jnp.bfloat16)

    def run_blocks(k, steps, mix):
        def one(t, carry):
            mix(ways[k][2](t))

            @pl.when(t > 0)
            def _():
                outgoing(k, ways[k][2](t - 1)).start()

            return carry

        lax.fori_loop(0, steps, one, 0)
        kept(k).start()

    def part_copy(j, array, land):
        return pltpu.make_async_remote_copy(
            src_ref=array,
            dst_ref=land,
            send_sem=part_send.at[j],
            recv_sem=part_recv.at[j],
            device_id=device((me + half) % count),
            device_id_type=pl.DeviceIdType.MESH,
        )

    part_copies = [part_copy(0, far_part, got_part), part_copy(1, far_stat, got_stat)]
    stat_lane = lax.broadcasted_iota(jnp.int32, (audio_rows, LANES), 1)
    each = LANES // AUDIO_DIM

    def audio_parts(first_source, part, stat):
        def one(j, stats):
            queries = land_aq[first_source + j]
            for b in range(blocks_each):
                lanes = slice(b * LANES, (b + 1) * LANES)
                mixed, peak, summed = softmax_mix(
                    lane_heads(queries[:, lanes]), land_ck[:, lanes], land_cv[:, lanes], audio_scaling
                )
                part[j, :, lanes] = merge_lane_heads(mixed, audio_rows).astype(part.dtype)
                level = peak * jnp.float32(audio_scaling * math.log2(math.e)) + jnp.log2(summed)
                for i in range(each):
                    stats = jnp.where(
                        stat_lane == (j * blocks_each + b) * each + i,
                        level[i * audio_rows : (i + 1) * audio_rows],
                        stats,
                    )
            return stats

        stats = lax.fori_loop(0, half, one, jnp.zeros((audio_rows, LANES), jnp.float32))
        padded = jnp.concatenate(
            [stats, jnp.zeros((LANES - audio_rows, LANES), jnp.float32)], axis=0
        )
        stat[...] = padded.T[: stat.shape[0]]

    def merge_parts(peer):
        j = peer % half
        unpacked = []
        for stat in (own_stat, got_stat):
            rest = jnp.zeros((LANES - stat.shape[0], LANES), jnp.float32)
            unpacked.append(jnp.concatenate([stat[...], rest], axis=0).T[:audio_rows])
        for b in range(blocks_each):
            lanes = slice(b * LANES, (b + 1) * LANES)
            shares = []
            for i in range(each):
                picked = stat_lane == (j * blocks_each + b) * each + i
                mine = jnp.sum(jnp.where(picked, unpacked[0], 0.0), axis=1, keepdims=True)
                other = jnp.sum(jnp.where(picked, unpacked[1], 0.0), axis=1, keepdims=True)
                peak = jnp.maximum(mine, other)
                mine = jnp.exp2(mine - peak)
                other = jnp.exp2(other - peak)
                total = mine + other
                shares.append((mine / total, other / total))
            own_share, got_share = (
                merge_lane_heads(
                    jnp.concatenate(
                        [jnp.broadcast_to(s[w], (audio_rows, LANES)) for s in shares], axis=0
                    ),
                    audio_rows,
                )
                for w in range(2)
            )
            merged = own_part[j, :, lanes] * own_share
            merged = merged + got_part[j, :, lanes].astype(jnp.float32) * got_share
            mixed_a[j, :, lanes] = merged.astype(jnp.bfloat16)

    for k in audio_ways:
        await_stream(k)
    audio_parts((1 - side) * half, far_part, far_stat)
    audio_parts(side * half, own_part, own_stat)

    def mix_video(h, source):
        mixed, peak, summed = softmax_mix(
            land_q[h, row(source), :], land_k[h], land_v[h], video_scaling
        )
        mixed_v[h, row(source), :] = mixed.astype(jnp.bfloat16)

    for copy in part_copies:
        copy.start()
    for h in range(video_each):
        for k in video_ways[h]:
            await_stream(k)
        run_blocks(first + h, count, partial(mix_video, h))
    for copy in part_copies:
        copy.wait()
    run_blocks(len(ways) - 1, half, merge_parts)

    for k in range(len(ways)):
        await_sent(k)
    for k in range(first, len(ways)):
        await_stream(k)

    @pl.when(me < count - 1)
    def _():
        for j, array, near in near_pairs:
            near_copy(j, array, near, 0, me + 1).wait_send()

    @pl.when(me > 0)
    def _():
        for j, array, near in near_pairs:
            near_copy(2 + j, array, near, 2, me - 1).wait_send()


def store_kernel(*refs):
    copies = [pltpu.make_async_copy(refs[i], refs[3 + i], refs[6].at[i]) for i in range(3)]
    for copy in copies:
        copy.start()
    for copy in copies:
        copy.wait()


def exchanged_body(count, sub_count, *arrays):
    vid_q, vid_k, vid_v, aud_q, cross_k, cross_v, cross_q, aud_k, aud_v, windows = arrays
    rows = vid_q.shape[0]
    audio_rows = aud_q.shape[0]
    video_each = vid_q.shape[1] // HEAD_DIM // count
    halves = count // 2
    width = aud_q.shape[1] // halves
    kinds = 4 * video_each + 4
    levels = -(-aud_q.shape[1] // AUDIO_DIM // 8) * 8
    half = jnp.bfloat16
    place = pl.BlockSpec(memory_space=pl.ANY)
    held = pl.pallas_call(
        partial(exchange_kernel, count, sub_count),
        out_shape=tuple(pltpu.VMEM(a.shape, half) for a in (vid_q, aud_q, cross_q)),
        in_specs=[place] * 10,
        out_specs=(pl.BlockSpec(memory_space=pltpu.VMEM),) * 3,
        scratch_shapes=[
            pltpu.VMEM((video_each, count * rows, HEAD_DIM), half),
            pltpu.VMEM((video_each, count * rows, HEAD_DIM), half),
            pltpu.VMEM((video_each, count * rows, HEAD_DIM), half),
            pltpu.VMEM((count, audio_rows, width), half),
            pltpu.VMEM((halves * rows, width), half),
            pltpu.VMEM((halves * rows, width), half),
            pltpu.VMEM((video_each, count * rows, HEAD_DIM), half),
            pltpu.VMEM((halves, audio_rows, width), half),
            pltpu.VMEM((halves, audio_rows, width), jnp.float32),
            pltpu.VMEM((levels, LANES), jnp.float32),
            pltpu.VMEM((halves, audio_rows, width), half),
            pltpu.VMEM((levels, LANES), jnp.float32),
            pltpu.VMEM((halves, audio_rows, width), half),
            pltpu.VMEM((levels, LANES), jnp.float32),
            pltpu.VMEM((3, audio_rows, aud_k.shape[1]), half),
            pltpu.VMEM((3, audio_rows, aud_k.shape[1]), half),
            pltpu.VMEM(cross_q.shape, half),
            pltpu.VMEM(windows.shape, windows.dtype),
            pltpu.SemaphoreType.DMA((kinds,)),
            pltpu.SemaphoreType.DMA((kinds,)),
            pltpu.SemaphoreType.DMA((4,)),
            pltpu.SemaphoreType.DMA((4,)),
            pltpu.SemaphoreType.DMA((2,)),
            pltpu.SemaphoreType.DMA((2,)),
            pltpu.SemaphoreType.DMA((4,)),
            pltpu.SemaphoreType.REGULAR((2,)),
            pltpu.SemaphoreType.REGULAR,
        ],
        compiler_params=pltpu.CompilerParams(collective_id=0, has_side_effects=True),
        name="joint_attention",
    )(*arrays)
    return pl.pallas_call(
        store_kernel,
        out_shape=tuple(jax.ShapeDtypeStruct(a.shape, half) for a in (vid_q, aud_q, cross_q)),
        in_specs=[pl.BlockSpec(memory_space=pltpu.VMEM)] * 3,
        out_specs=(place, place, place),
        scratch_shapes=[pltpu.SemaphoreType.DMA((3,))],
        name="store_results",
    )(*[pltpu.with_memory_space_constraint(x, pltpu.VMEM) for x in held])


def body(*arrays):
    sub_count = lax.axis_size("sub")
    count = lax.axis_size("seq") * sub_count
    video_heads = arrays[0].shape[1] // HEAD_DIM
    audio_heads = arrays[3].shape[1] // AUDIO_DIM
    halved = count == 4 * sub_count and max(audio_heads, arrays[3].shape[0]) <= LANES
    if halved and video_heads % count == 0 and audio_heads % count == 0:
        return exchanged_body(count, sub_count, *arrays)
    return gathered_body(*arrays)


def solution(mesh):
    return jax.shard_map(
        body,
        mesh=mesh,
        in_specs=(
            P(("grp", "seq", "sub"), "head"),
            P(("grp", "seq", "sub"), "head"),
            P(("grp", "seq", "sub"), "head"),
            P(("grp", "seq", "sub"), "head"),
            P(("grp", "seq", "sub"), "head"),
            P(("grp", "seq", "sub"), "head"),
            P(("grp", "seq", "sub"), "head"),
            P(("grp", "seq", "sub"), "head"),
            P(("grp", "seq", "sub"), "head"),
            P(None, "grp"),
        ),
        out_specs=(
            P(("grp", "seq", "sub"), "head"),
            P(("grp", "seq", "sub"), "head"),
            P(("grp", "seq", "sub"), "head"),
        ),
        check_vma=False,
    )
```

```python
from functools import partial
import math

import jax
import jax.numpy as jnp
from jax import lax
from jax.experimental import pallas as pl
from jax.experimental.pallas import tpu as pltpu
from jax.sharding import PartitionSpec as P

HEAD_DIM = 128
AUDIO_DIM = 64
TILE_LEN = 32
STRETCH_LEN = 8


def extended(cells, sides, width):
    for axis, dim in sides:
        count = lax.axis_size(axis)
        ends = count - 1
        head = lax.slice_in_dim(cells, 0, width, axis=dim)
        tail = lax.slice_in_dim(cells, cells.shape[dim] - width, cells.shape[dim], axis=dim)
        cells = jnp.concatenate(
            [
                lax.ppermute(tail, axis, [(i, (i + 1) % count) for i in range(ends)]),
                cells,
                lax.ppermute(head, axis, [((i + 1) % count, i) for i in range(ends)]),
            ],
            axis=dim,
        )
    return cells


def start_state(query_count, head_count, head_size):
    running = jnp.full((head_count, query_count), -jnp.inf, jnp.float32)
    summed = jnp.zeros((head_count, query_count), jnp.float32)
    numerator = jnp.zeros((head_count, query_count, head_size), jnp.float32)
    return (running, summed, numerator)


def absorb(state_in, queries, key_rows, value_rows, head_count, scaling, visible):
    running, summed, numerator = state_in
    query_count = queries.shape[0]
    key_count = key_rows.shape[0]
    head_size = queries.shape[1] // head_count
    scores = (
        jnp.einsum(
            "qhe,khe->hqk",
            queries.reshape(query_count, head_count, head_size),
            key_rows.reshape(key_count, head_count, head_size),
            preferred_element_type=jnp.float32,
        )
        * scaling
    )
    if visible is not None:
        scores = jnp.where(visible[None], scores, jnp.float32(-1e30))
    newest = jnp.maximum(running, jnp.max(scores, axis=2))
    shrink = jnp.exp(running - newest)
    weights = jnp.exp(scores - newest[:, :, None])
    summed = summed * shrink + jnp.sum(weights, axis=2)
    numerator = numerator * shrink[:, :, None] + jnp.einsum(
        "hqk,khe->hqe",
        weights.astype(jnp.bfloat16),
        value_rows.reshape(key_count, head_count, head_size),
        preferred_element_type=jnp.float32,
    )
    return (newest, summed, numerator)


def block_split(total_rows):
    block_rows = total_rows
    while block_rows > 512 and block_rows % 2 == 0:
        block_rows = block_rows // 2
    return (block_rows, total_rows // block_rows)


def fold_keys(state_in, shards_in, offset, queries, head_count, scaling):
    key_rows, value_rows = shards_in
    block_rows, block_count = block_split(key_rows.shape[0])
    key_blocks = key_rows.reshape(block_count, block_rows, key_rows.shape[1])
    value_blocks = value_rows.reshape(block_count, block_rows, value_rows.shape[1])

    def one_block(state, paired):
        return (absorb(state, queries, paired[0], paired[1], head_count, scaling, None), None)

    result, unused = lax.scan(one_block, state_in, (key_blocks, value_blocks))
    return result


def normalize_heads(state_in):
    running, summed, numerator = state_in
    mixed = numerator / summed[:, :, None]
    return mixed.transpose(1, 0, 2).reshape(mixed.shape[1], -1).astype(jnp.bfloat16)


def gathered_body(vid_q, vid_k, vid_v, aud_q, cross_k, cross_v, cross_q, aud_k, aud_v, windows):
    video_heads = vid_q.shape[1] // HEAD_DIM
    video_scaling = 1.0 / math.sqrt(HEAD_DIM)
    audio_heads = aud_q.shape[1] // AUDIO_DIM
    audio_scaling = 1.0 / math.sqrt(AUDIO_DIM)
    moved_q, moved_k, moved_v = (
        lax.all_to_all(vid_q, "sub", split_axis=1, concat_axis=0, tiled=True),
        lax.all_to_all(vid_k, "sub", split_axis=1, concat_axis=0, tiled=True),
        lax.all_to_all(vid_v, "sub", split_axis=1, concat_axis=0, tiled=True),
    )
    pair_heads = video_heads // lax.axis_size("sub")
    folder = partial(fold_keys, queries=moved_q, head_count=pair_heads, scaling=video_scaling)
    state = folder(
        start_state(moved_q.shape[0], pair_heads, HEAD_DIM),
        (
            lax.all_gather(moved_k, "seq", axis=0, tiled=True),
            lax.all_gather(moved_v, "seq", axis=0, tiled=True),
        ),
        jnp.int32(0),
    )
    video_self = lax.all_to_all(
        normalize_heads(state), "sub", split_axis=0, concat_axis=1, tiled=True
    )
    folder = partial(fold_keys, queries=aud_q, head_count=audio_heads, scaling=audio_scaling)
    state = folder(
        start_state(aud_q.shape[0], audio_heads, AUDIO_DIM),
        (
            lax.all_gather(cross_k, ("seq", "sub"), axis=0, tiled=True),
            lax.all_gather(cross_v, ("seq", "sub"), axis=0, tiled=True),
        ),
        jnp.int32(0),
    )
    audio_out = normalize_heads(state)
    audio_rows = aud_k.shape[0]
    key_width = aud_k.shape[1]
    padded_rows = extended(
        jnp.concatenate((aud_k, aud_v), axis=1), ((("seq", "sub"), 0),), audio_rows
    )
    near_keys = padded_rows[:, :key_width]
    near_values = padded_rows[:, key_width:]
    position = lax.axis_index(("seq", "sub"))
    audio_index = (position - 1) * audio_rows + jnp.arange(padded_rows.shape[0], dtype=jnp.int32)
    stretch_index = audio_index // STRETCH_LEN
    stretch_ids = jnp.arange(windows.shape[1], dtype=jnp.int32)
    onehot = stretch_index[:, None] == stretch_ids[None, :]
    first_tile = jnp.sum(jnp.where(onehot, windows[0][None, :], 0), axis=1)
    after_tile = jnp.sum(jnp.where(onehot, windows[1][None, :], 0), axis=1)
    video_rows = cross_q.shape[0]
    video_tile = (position * video_rows + jnp.arange(video_rows, dtype=jnp.int32)) // TILE_LEN
    visible = (first_tile[None, :] <= video_tile[:, None]) & (
        video_tile[:, None] < after_tile[None, :]
    )
    state = absorb(
        start_state(video_rows, audio_heads, AUDIO_DIM),
        cross_q,
        near_keys,
        near_values,
        audio_heads,
        audio_scaling,
        visible,
    )
    video_cross = normalize_heads(state)
    return (video_self, audio_out, video_cross)


LANES = 128
AXES = ("seq", "sub")


def softmax_mix(queries, key_rows, value_rows, scaling):
    scores = lax.dot_general(
        queries, key_rows, (((1,), (1,)), ((), ())), preferred_element_type=jnp.float32
    )
    peak = jnp.max(scores, axis=1, keepdims=True)
    weights = jnp.exp2((scores - peak) * jnp.float32(scaling * math.log2(math.e)))
    summed = jnp.sum(weights, axis=1, keepdims=True)
    mixed = jnp.dot(
        weights.astype(jnp.bfloat16), value_rows, preferred_element_type=jnp.float32
    )
    return mixed / summed, peak, summed


def lane_heads(block):
    wide = block.astype(jnp.float32)
    lane = lax.broadcasted_iota(jnp.int32, wide.shape, 1) // AUDIO_DIM
    parts = [jnp.where(lane == i, wide, 0.0) for i in range(LANES // AUDIO_DIM)]
    return jnp.concatenate(parts, axis=0).astype(jnp.bfloat16)


def merge_lane_heads(stacked, rows):
    lane = lax.broadcasted_iota(jnp.int32, (rows, LANES), 1) // AUDIO_DIM
    merged = stacked[:rows]
    for i in range(1, LANES // AUDIO_DIM):
        merged = jnp.where(lane == i, stacked[i * rows : (i + 1) * rows], merged)
    return merged


def exchange_kernel(
    count,
    sub_count,
    vid_q,
    vid_k,
    vid_v,
    aud_q,
    cross_k,
    cross_v,
    cross_q,
    aud_k,
    aud_v,
    windows,
    video_self,
    audio_out,
    video_cross,
    land,
    land_aq,
    land_c,
    mixed_v,
    mixed_a,
    own_part,
    own_stat,
    far_part,
    far_stat,
    got_part,
    got_stat,
    near_k,
    near_v,
    local_cq,
    local_windows,
    send_sem,
    recv_sem,
    near_send,
    near_recv,
    part_send,
    part_recv,
    local_sem,
    ready_sem,
    all_sem,
):
    rows = vid_q.shape[0]
    audio_rows = aud_q.shape[0]
    video_each = vid_q.shape[1] // HEAD_DIM // count
    half = count // 2
    blocks_each = aud_q.shape[1] // LANES // half
    width = blocks_each * LANES
    video_scaling = 1.0 / math.sqrt(HEAD_DIM)
    audio_scaling = 1.0 / math.sqrt(AUDIO_DIM)
    me = lax.axis_index("seq") * sub_count + lax.axis_index("sub")

    side = me // half
    place = me % half

    def device(peer):
        return {"seq": peer // sub_count, "sub": peer % sub_count}

    def peer_near(t):
        return side * half + (place + 1 + t) % half

    chip = me // sub_count
    core = me % sub_count
    inner = (me >= half - sub_count) & (me < half + sub_count)
    outer = jnp.logical_not(inner)

    def inner_of(which, t):
        return half - (1 - which) * sub_count + (core + t) % sub_count

    def outer_of(which, t):
        return which * (half + sub_count) + (core + t) % sub_count

    def core_peer(t):
        return chip * sub_count + (core + 1 + t) % sub_count

    def near_inner(t):
        return inner_of(side, t)

    def near_outer(t):
        return outer_of(side, t)

    def far_inner(t):
        return inner_of(1 - side, t)

    def far_outer(t):
        return outer_of(1 - side, t)

    def out_peer(t):
        turn = t // sub_count
        chips = count // sub_count
        there = jnp.where(turn == side, chips // 2 - side, chip)
        there = jnp.where(turn == 1 - side, (1 - side) * (chips - 1), there)
        there = jnp.where(turn == 2, 2 * (chip // 2) + 1 - chip % 2, there)
        shift = t + turn // (chips - 1)
        return there * sub_count + (core + shift) % sub_count

    def signal(semaphore, peer):
        pl.semaphore_signal(
            semaphore, inc=1, device_id=device(peer), device_id_type=pl.DeviceIdType.MESH
        )

    barrier = pltpu.get_barrier_semaphore()

    @pl.when(inner)
    def _():
        for t in range(sub_count):
            signal(barrier, far_inner(t))

    for t in range(sub_count - 1):
        signal(barrier, core_peer(t))

    own = [
        pltpu.make_async_copy(cross_q, local_cq, local_sem.at[0]),
        pltpu.make_async_copy(aud_k, near_k.at[1], local_sem.at[1]),
        pltpu.make_async_copy(aud_v, near_v.at[1], local_sem.at[2]),
        pltpu.make_async_copy(windows, local_windows, local_sem.at[3]),
    ]
    for copy in own:
        copy.start()

    def column(index):
        return pl.ds(pl.multiple_of(index * LANES, LANES), LANES)

    def row(index):
        return pl.ds(pl.multiple_of(index * rows, rows), rows)

    def columns(index):
        return pl.ds(pl.multiple_of(index * width, LANES), width)

    def video_way(array, which, h):
        return (
            lambda peer: array.at[:, column(peer * video_each + h)],
            lambda source: land.at[which, h, row(source), :],
            2,
            4 + h,
        )

    def half_way(array, which):
        return (
            lambda peer: array.at[:, columns(peer % half)],
            lambda source: land_c.at[which, row(source % half), :],
            1,
            1,
        )

    ways = [
        (
            lambda peer: aud_q.at[:, columns(peer % half)],
            lambda source: land_aq.at[source],
            0,
            0,
        )
    ]
    audio_ways = [0]
    video_ways = []
    for h in range(video_each):
        video_ways.append(list(range(len(ways), len(ways) + 3)))
        for which, array in enumerate((vid_k, vid_v, vid_q)):
            ways.append(video_way(array, which, h))
        if h == 0:
            for which, array in enumerate((cross_k, cross_v)):
                audio_ways.append(len(ways))
                ways.append(half_way(array, which))
    first = len(ways)
    early = audio_ways[:1] + video_ways[0]
    late = [k for kinds in video_ways[1:] for k in kinds]
    for h in range(video_each):
        ways.append(
            (
                lambda peer, h=h: mixed_v.at[h, row(peer), :],
                lambda source, h=h: video_self.at[:, column(source * video_each + h)],
                3,
                2,
            )
        )
    ways.append(
        (
            lambda peer: mixed_a.at[peer % half],
            lambda source: audio_out.at[:, columns(source % half)],
            4,
            3,
        )
    )
    sent = (
        land_aq.at[pl.ds(0, count - 1)],
        land_c.at[:, pl.ds(0, (half - 1) * rows), :],
        land.at[:, :, pl.ds(0, (count - 1) * rows), :],
        mixed_v.at[:, pl.ds(0, (count - 1) * rows), :],
        mixed_a.at[pl.ds(0, half - 1)],
    )
    landed = [land_aq, land_c, video_self, audio_out]
    landed += [land.at[:, h] for h in range(video_each)]

    def outgoing(k, peer):
        return pltpu.make_async_remote_copy(
            src_ref=ways[k][0](peer),
            dst_ref=ways[k][1](me),
            send_sem=send_sem.at[ways[k][2]],
            recv_sem=recv_sem.at[ways[k][3]],
            device_id=device(peer),
            device_id_type=pl.DeviceIdType.MESH,
        )

    def kept(k):
        return pltpu.make_async_copy(ways[k][0](me), ways[k][1](me), recv_sem.at[ways[k][3]])

    def await_landed(i):
        pltpu.make_async_copy(landed[i], landed[i], recv_sem.at[i]).wait()

    def await_sent(i):
        pltpu.make_async_copy(sent[i], sent[i], send_sem.at[i]).wait()

    def near_copy(array, near, slot, peer):
        return pltpu.make_async_remote_copy(
            src_ref=array,
            dst_ref=near.at[slot],
            send_sem=near_send.at[slot // 2],
            recv_sem=near_recv.at[slot // 2],
            device_id=device(peer),
            device_id_type=pl.DeviceIdType.MESH,
        )

    near_pairs = ((aud_k, near_k), (aud_v, near_v))

    def send_right():
        for array, near in near_pairs:
            near_copy(array, near, 0, me + 1).start()

    def send_left():
        for array, near in near_pairs:
            near_copy(array, near, 2, me - 1).start()

    def await_near(semaphore):
        both = near_k.at[pl.ds(0, 2)]
        pltpu.make_async_copy(both, both, semaphore).wait()

    def send(k, peer_of, steps):
        def one(t, carry):
            outgoing(k, peer_of(t)).start()
            return carry

        lax.fori_loop(0, steps, one, 0)

    pair = sub_count - 1
    audio_only = audio_ways[1:]

    def send_keep(ks):
        for k in ks:
            send(k, core_peer, pair)
            kept(k).start()

    @pl.when(inner)
    def _():
        pl.semaphore_wait(barrier, 2 * sub_count - 1)
        for t in range(sub_count):
            signal(barrier, near_outer(t))
        for k in early:
            send(k, far_inner, sub_count)

        @pl.when(side == 0)
        def _():
            send_right()

            @pl.when(core > 0)
            def _():
                send_left()

        @pl.when(side == 1)
        def _():
            send_left()

            @pl.when(core < sub_count - 1)
            def _():
                send_right()

        send_keep(early[:1] + audio_only)
        pl.semaphore_wait(ready_sem.at[side], sub_count)

        @pl.when((side == 0) & (core == 0))
        def _():
            send_left()

        @pl.when((side == 1) & (core == sub_count - 1))
        def _():
            send_right()

        for k in early[:1] + audio_only + early[1:] + late:
            send(k, near_outer, sub_count)
        pl.semaphore_wait(ready_sem.at[1 - side], sub_count)
        signal(all_sem, near_outer(0))
        for k in early:
            send(k, far_outer, sub_count)
        for k in late:
            send(k, far_inner, sub_count)
        for k in late:
            send(k, far_outer, sub_count)
        send_keep(early[1:] + late)

    @pl.when(outer)
    def _():
        pl.semaphore_wait(barrier, 2 * sub_count - 1)
        for t in range(sub_count):
            signal(ready_sem.at[side], near_inner(t))
            signal(ready_sem.at[side], far_inner(t))

        for k in early[:1]:
            send(k, far_inner, sub_count)

        @pl.when(me < count - 1)
        def _():
            send_right()

        @pl.when(me > 0)
        def _():
            send_left()

        for k in early[:1] + audio_only:
            send(k, near_inner, sub_count)
        send_keep(early[:1] + audio_only)
        pl.semaphore_wait(all_sem, 1)
        for k in early[:1]:
            send(k, far_outer, sub_count)
        for k in early[1:] + late:
            send(k, near_inner, sub_count)
        for ks in (early[1:], late):
            for k in ks:
                send(k, far_outer, sub_count)
            for k in ks:
                send(k, far_inner, sub_count)
        send_keep(early[1:] + late)

    @pl.when(me == 0)
    def _():
        for array, near in near_pairs:
            near[0] = jnp.zeros(near.shape[1:], near.dtype)

    @pl.when(me == count - 1)
    def _():
        for array, near in near_pairs:
            near[2] = jnp.zeros(near.shape[1:], near.dtype)

    for copy in own:
        copy.wait()

    @pl.when(me > 0)
    def _():
        await_near(near_recv.at[0])

    @pl.when(me < count - 1)
    def _():
        await_near(near_recv.at[1])

    spans = windows.shape[1]
    tile = (me * rows + lax.broadcasted_iota(jnp.int32, (rows, spans), 0)) // TILE_LEN
    bounds = local_windows[...]
    inside = (bounds[0:1, :] <= tile) & (tile < bounds[1:2, :])
    inside = jnp.where(inside, 1.0, 0.0).astype(jnp.bfloat16)
    seen = []
    for slot in range(3):
        stretch = lax.broadcasted_iota(jnp.int32, (spans, audio_rows), 1) // STRETCH_LEN
        stretch = stretch + (me + slot - 1) * (audio_rows // STRETCH_LEN)
        picks = stretch == lax.broadcasted_iota(jnp.int32, (spans, audio_rows), 0)
        picks = jnp.where(picks, 1.0, 0.0).astype(jnp.bfloat16)
        part = jnp.dot(inside, picks, preferred_element_type=jnp.float32)
        seen.append(jnp.concatenate([part] * (LANES // AUDIO_DIM), axis=0))

    for b in range(cross_q.shape[1] // LANES):
        lanes = slice(b * LANES, (b + 1) * LANES)
        stacked = lane_heads(local_cq[:, lanes])
        scores = []
        for slot in range(3):
            part = lax.dot_general(
                stacked,
                near_k[slot, :, lanes],
                (((1,), (1,)), ((), ())),
                preferred_element_type=jnp.float32,
            )
            scores.append(jnp.where(seen[slot] > 0.5, part, jnp.float32(-1e30)))
        peak = jnp.max(jnp.maximum(jnp.maximum(scores[0], scores[1]), scores[2]), axis=1, keepdims=True)
        factor = jnp.float32(audio_scaling * math.log2(math.e))
        weights = [jnp.exp2((part - peak) * factor) for part in scores]
        summed = jnp.sum(weights[0] + weights[1] + weights[2], axis=1, keepdims=True)
        mixed = sum(
            jnp.dot(
                weights[slot].astype(jnp.bfloat16),
                near_v[slot, :, lanes],
                preferred_element_type=jnp.float32,
            )
            for slot in range(3)
        )
        video_cross[:, lanes] = merge_lane_heads(mixed / summed, rows).astype(jnp.bfloat16)

    def part_copy(j, array, land):
        return pltpu.make_async_remote_copy(
            src_ref=array,
            dst_ref=land,
            send_sem=part_send.at[j],
            recv_sem=part_recv.at[j],
            device_id=device((me + half) % count),
            device_id_type=pl.DeviceIdType.MESH,
        )

    part_copies = [part_copy(0, far_part, got_part), part_copy(1, far_stat, got_stat)]
    stat_lane = lax.broadcasted_iota(jnp.int32, (audio_rows, LANES), 1)
    each = LANES // AUDIO_DIM

    def audio_parts(first_source, part, stat):
        def one(j, stats):
            queries = land_aq[first_source + j]
            for b in range(blocks_each):
                lanes = slice(b * LANES, (b + 1) * LANES)
                mixed, peak, summed = softmax_mix(
                    lane_heads(queries[:, lanes]), land_c[0, :, lanes], land_c[1, :, lanes], audio_scaling
                )
                part[j, :, lanes] = merge_lane_heads(mixed, audio_rows).astype(part.dtype)
                level = peak * jnp.float32(audio_scaling * math.log2(math.e)) + jnp.log2(summed)
                for i in range(each):
                    stats = jnp.where(
                        stat_lane == (j * blocks_each + b) * each + i,
                        level[i * audio_rows : (i + 1) * audio_rows],
                        stats,
                    )
            return stats

        stats = lax.fori_loop(0, half, one, jnp.zeros((audio_rows, LANES), jnp.float32))
        padded = jnp.concatenate(
            [stats, jnp.zeros((LANES - audio_rows, LANES), jnp.float32)], axis=0
        )
        stat[...] = padded.T[: stat.shape[0]]

    def merge_parts(peer):
        j = peer % half
        unpacked = []
        for stat in (own_stat, got_stat):
            rest = jnp.zeros((LANES - stat.shape[0], LANES), jnp.float32)
            unpacked.append(jnp.concatenate([stat[...], rest], axis=0).T[:audio_rows])
        for b in range(blocks_each):
            lanes = slice(b * LANES, (b + 1) * LANES)
            shares = []
            for i in range(each):
                picked = stat_lane == (j * blocks_each + b) * each + i
                mine = jnp.sum(jnp.where(picked, unpacked[0], 0.0), axis=1, keepdims=True)
                other = jnp.sum(jnp.where(picked, unpacked[1], 0.0), axis=1, keepdims=True)
                peak = jnp.maximum(mine, other)
                mine = jnp.exp2(mine - peak)
                other = jnp.exp2(other - peak)
                total = mine + other
                shares.append((mine / total, other / total))
            own_share, got_share = (
                merge_lane_heads(
                    jnp.concatenate(
                        [jnp.broadcast_to(s[w], (audio_rows, LANES)) for s in shares], axis=0
                    ),
                    audio_rows,
                )
                for w in range(2)
            )
            merged = own_part[j, :, lanes] * own_share
            merged = merged + got_part[j, :, lanes].astype(jnp.float32) * got_share
            mixed_a[j, :, lanes] = merged.astype(jnp.bfloat16)

    await_landed(0)
    await_landed(1)
    audio_parts((1 - side) * half, far_part, far_stat)
    audio_parts(side * half, own_part, own_stat)

    def mix_video(h, source):
        mixed, peak, summed = softmax_mix(
            land[2, h, row(source), :], land[0, h], land[1, h], video_scaling
        )
        mixed_v[h, row(source), :] = mixed.astype(jnp.bfloat16)

    for copy in part_copies:
        copy.start()
    for h in range(video_each):
        await_landed(4 + h)
        last = h == video_each - 1

        def one(t, carry, h=h, last=last):
            mix_video(h, out_peer(t))
            held = jnp.logical_and(((side == 1) | inner), (t - 1) // sub_count == 1)
            now = t > 0
            if not last:
                now = now & jnp.logical_not(held)

            @pl.when(now)
            def _():
                outgoing(first + h, out_peer(t - 1)).start()

            if last:

                @pl.when((t == sub_count) & ((side == 1) | inner))
                def _():
                    for earlier in range(h):
                        for i in range(sub_count):
                            outgoing(first + earlier, out_peer(sub_count + i)).start()

            return carry

        lax.fori_loop(0, count, one, 0)
        kept(first + h).start()
    for copy in part_copies:
        copy.wait()
    merged = len(ways) - 1

    def one_merge(t, carry):
        merge_parts(peer_near(t))

        @pl.when(t < half - 1)
        def _():
            outgoing(merged, peer_near(t)).start()

        return carry

    lax.fori_loop(0, half, one_merge, 0)
    kept(merged).start()

    for i in range(len(sent)):
        await_sent(i)
    await_landed(2)
    await_landed(3)

    @pl.when(me < count - 1)
    def _():
        await_near(near_send.at[0])

    @pl.when(me > 0)
    def _():
        await_near(near_send.at[1])


def store_kernel(*refs):
    copies = [pltpu.make_async_copy(refs[i], refs[3 + i], refs[6].at[i]) for i in range(3)]
    for copy in copies:
        copy.start()
    for copy in copies:
        copy.wait()


def exchanged_body(count, sub_count, *arrays):
    vid_q, vid_k, vid_v, aud_q, cross_k, cross_v, cross_q, aud_k, aud_v, windows = arrays
    rows = vid_q.shape[0]
    audio_rows = aud_q.shape[0]
    video_each = vid_q.shape[1] // HEAD_DIM // count
    halves = count // 2
    width = aud_q.shape[1] // halves
    levels = -(-aud_q.shape[1] // AUDIO_DIM // 8) * 8
    half = jnp.bfloat16
    place = pl.BlockSpec(memory_space=pl.ANY)
    held = pl.pallas_call(
        partial(exchange_kernel, count, sub_count),
        out_shape=tuple(pltpu.VMEM(a.shape, half) for a in (vid_q, aud_q, cross_q)),
        in_specs=[place] * 10,
        out_specs=(pl.BlockSpec(memory_space=pltpu.VMEM),) * 3,
        scratch_shapes=[
            pltpu.VMEM((3, video_each, count * rows, HEAD_DIM), half),
            pltpu.VMEM((count, audio_rows, width), half),
            pltpu.VMEM((2, halves * rows, width), half),
            pltpu.VMEM((video_each, count * rows, HEAD_DIM), half),
            pltpu.VMEM((halves, audio_rows, width), half),
            pltpu.VMEM((halves, audio_rows, width), jnp.float32),
            pltpu.VMEM((levels, LANES), jnp.float32),
            pltpu.VMEM((halves, audio_rows, width), half),
            pltpu.VMEM((levels, LANES), jnp.float32),
            pltpu.VMEM((halves, audio_rows, width), half),
            pltpu.VMEM((levels, LANES), jnp.float32),
            pltpu.VMEM((3, audio_rows, aud_k.shape[1]), half),
            pltpu.VMEM((3, audio_rows, aud_k.shape[1]), half),
            pltpu.VMEM(cross_q.shape, half),
            pltpu.VMEM(windows.shape, windows.dtype),
            pltpu.SemaphoreType.DMA((5,)),
            pltpu.SemaphoreType.DMA((4 + video_each,)),
            pltpu.SemaphoreType.DMA((2,)),
            pltpu.SemaphoreType.DMA((2,)),
            pltpu.SemaphoreType.DMA((2,)),
            pltpu.SemaphoreType.DMA((2,)),
            pltpu.SemaphoreType.DMA((4,)),
            pltpu.SemaphoreType.REGULAR((2,)),
            pltpu.SemaphoreType.REGULAR,
        ],
        compiler_params=pltpu.CompilerParams(collective_id=0, has_side_effects=True),
        name="joint_attention",
    )(*arrays)
    return pl.pallas_call(
        store_kernel,
        out_shape=tuple(jax.ShapeDtypeStruct(a.shape, half) for a in (vid_q, aud_q, cross_q)),
        in_specs=[pl.BlockSpec(memory_space=pltpu.VMEM)] * 3,
        out_specs=(place, place, place),
        scratch_shapes=[pltpu.SemaphoreType.DMA((3,))],
        name="store_results",
    )(*[pltpu.with_memory_space_constraint(x, pltpu.VMEM) for x in held])


def body(*arrays):
    sub_count = lax.axis_size("sub")
    count = lax.axis_size("seq") * sub_count
    video_heads = arrays[0].shape[1] // HEAD_DIM
    audio_heads = arrays[3].shape[1] // AUDIO_DIM
    halved = count == 4 * sub_count and max(audio_heads, arrays[3].shape[0]) <= LANES
    if halved and video_heads % count == 0 and audio_heads % count == 0:
        return exchanged_body(count, sub_count, *arrays)
    return gathered_body(*arrays)


def solution(mesh):
    return jax.shard_map(
        body,
        mesh=mesh,
        in_specs=(
            P(("grp", "seq", "sub"), "head"),
            P(("grp", "seq", "sub"), "head"),
            P(("grp", "seq", "sub"), "head"),
            P(("grp", "seq", "sub"), "head"),
            P(("grp", "seq", "sub"), "head"),
            P(("grp", "seq", "sub"), "head"),
            P(("grp", "seq", "sub"), "head"),
            P(("grp", "seq", "sub"), "head"),
            P(("grp", "seq", "sub"), "head"),
            P(None, "grp"),
        ),
        out_specs=(
            P(("grp", "seq", "sub"), "head"),
            P(("grp", "seq", "sub"), "head"),
            P(("grp", "seq", "sub"), "head"),
        ),
        check_vma=False,
    )
```

```python
from functools import partial
import math

import jax
import jax.numpy as jnp
from jax import lax
from jax.experimental import pallas as pl
from jax.experimental.pallas import tpu as pltpu
from jax.sharding import PartitionSpec as P

HEAD_DIM = 128
AUDIO_DIM = 64
TILE_LEN = 32
STRETCH_LEN = 8


def extended(cells, sides, width):
    for axis, dim in sides:
        count = lax.axis_size(axis)
        ends = count - 1
        head = lax.slice_in_dim(cells, 0, width, axis=dim)
        tail = lax.slice_in_dim(cells, cells.shape[dim] - width, cells.shape[dim], axis=dim)
        cells = jnp.concatenate(
            [
                lax.ppermute(tail, axis, [(i, (i + 1) % count) for i in range(ends)]),
                cells,
                lax.ppermute(head, axis, [((i + 1) % count, i) for i in range(ends)]),
            ],
            axis=dim,
        )
    return cells


def start_state(query_count, head_count, head_size):
    running = jnp.full((head_count, query_count), -jnp.inf, jnp.float32)
    summed = jnp.zeros((head_count, query_count), jnp.float32)
    numerator = jnp.zeros((head_count, query_count, head_size), jnp.float32)
    return (running, summed, numerator)


def absorb(state_in, queries, key_rows, value_rows, head_count, scaling, visible):
    running, summed, numerator = state_in
    query_count = queries.shape[0]
    key_count = key_rows.shape[0]
    head_size = queries.shape[1] // head_count
    scores = (
        jnp.einsum(
            "qhe,khe->hqk",
            queries.reshape(query_count, head_count, head_size),
            key_rows.reshape(key_count, head_count, head_size),
            preferred_element_type=jnp.float32,
        )
        * scaling
    )
    if visible is not None:
        scores = jnp.where(visible[None], scores, jnp.float32(-1e30))
    newest = jnp.maximum(running, jnp.max(scores, axis=2))
    shrink = jnp.exp(running - newest)
    weights = jnp.exp(scores - newest[:, :, None])
    summed = summed * shrink + jnp.sum(weights, axis=2)
    numerator = numerator * shrink[:, :, None] + jnp.einsum(
        "hqk,khe->hqe",
        weights.astype(jnp.bfloat16),
        value_rows.reshape(key_count, head_count, head_size),
        preferred_element_type=jnp.float32,
    )
    return (newest, summed, numerator)


def block_split(total_rows):
    block_rows = total_rows
    while block_rows > 512 and block_rows % 2 == 0:
        block_rows = block_rows // 2
    return (block_rows, total_rows // block_rows)


def fold_keys(state_in, shards_in, offset, queries, head_count, scaling):
    key_rows, value_rows = shards_in
    block_rows, block_count = block_split(key_rows.shape[0])
    key_blocks = key_rows.reshape(block_count, block_rows, key_rows.shape[1])
    value_blocks = value_rows.reshape(block_count, block_rows, value_rows.shape[1])

    def one_block(state, paired):
        return (absorb(state, queries, paired[0], paired[1], head_count, scaling, None), None)

    result, unused = lax.scan(one_block, state_in, (key_blocks, value_blocks))
    return result


def normalize_heads(state_in):
    running, summed, numerator = state_in
    mixed = numerator / summed[:, :, None]
    return mixed.transpose(1, 0, 2).reshape(mixed.shape[1], -1).astype(jnp.bfloat16)


def gathered_body(vid_q, vid_k, vid_v, aud_q, cross_k, cross_v, cross_q, aud_k, aud_v, windows):
    video_heads = vid_q.shape[1] // HEAD_DIM
    video_scaling = 1.0 / math.sqrt(HEAD_DIM)
    audio_heads = aud_q.shape[1] // AUDIO_DIM
    audio_scaling = 1.0 / math.sqrt(AUDIO_DIM)
    moved_q, moved_k, moved_v = (
        lax.all_to_all(vid_q, "sub", split_axis=1, concat_axis=0, tiled=True),
        lax.all_to_all(vid_k, "sub", split_axis=1, concat_axis=0, tiled=True),
        lax.all_to_all(vid_v, "sub", split_axis=1, concat_axis=0, tiled=True),
    )
    pair_heads = video_heads // lax.axis_size("sub")
    folder = partial(fold_keys, queries=moved_q, head_count=pair_heads, scaling=video_scaling)
    state = folder(
        start_state(moved_q.shape[0], pair_heads, HEAD_DIM),
        (
            lax.all_gather(moved_k, "seq", axis=0, tiled=True),
            lax.all_gather(moved_v, "seq", axis=0, tiled=True),
        ),
        jnp.int32(0),
    )
    video_self = lax.all_to_all(
        normalize_heads(state), "sub", split_axis=0, concat_axis=1, tiled=True
    )
    folder = partial(fold_keys, queries=aud_q, head_count=audio_heads, scaling=audio_scaling)
    state = folder(
        start_state(aud_q.shape[0], audio_heads, AUDIO_DIM),
        (
            lax.all_gather(cross_k, ("seq", "sub"), axis=0, tiled=True),
            lax.all_gather(cross_v, ("seq", "sub"), axis=0, tiled=True),
        ),
        jnp.int32(0),
    )
    audio_out = normalize_heads(state)
    audio_rows = aud_k.shape[0]
    key_width = aud_k.shape[1]
    padded_rows = extended(
        jnp.concatenate((aud_k, aud_v), axis=1), ((("seq", "sub"), 0),), audio_rows
    )
    near_keys = padded_rows[:, :key_width]
    near_values = padded_rows[:, key_width:]
    position = lax.axis_index(("seq", "sub"))
    audio_index = (position - 1) * audio_rows + jnp.arange(padded_rows.shape[0], dtype=jnp.int32)
    stretch_index = audio_index // STRETCH_LEN
    stretch_ids = jnp.arange(windows.shape[1], dtype=jnp.int32)
    onehot = stretch_index[:, None] == stretch_ids[None, :]
    first_tile = jnp.sum(jnp.where(onehot, windows[0][None, :], 0), axis=1)
    after_tile = jnp.sum(jnp.where(onehot, windows[1][None, :], 0), axis=1)
    video_rows = cross_q.shape[0]
    video_tile = (position * video_rows + jnp.arange(video_rows, dtype=jnp.int32)) // TILE_LEN
    visible = (first_tile[None, :] <= video_tile[:, None]) & (
        video_tile[:, None] < after_tile[None, :]
    )
    state = absorb(
        start_state(video_rows, audio_heads, AUDIO_DIM),
        cross_q,
        near_keys,
        near_values,
        audio_heads,
        audio_scaling,
        visible,
    )
    video_cross = normalize_heads(state)
    return (video_self, audio_out, video_cross)


LANES = 128
AXES = ("seq", "sub")


def softmax_mix(queries, key_rows, value_rows, scaling):
    scores = lax.dot_general(
        queries, key_rows, (((1,), (1,)), ((), ())), preferred_element_type=jnp.float32
    )
    peak = jnp.max(scores, axis=1, keepdims=True)
    weights = jnp.exp2((scores - peak) * jnp.float32(scaling * math.log2(math.e)))
    summed = jnp.sum(weights, axis=1, keepdims=True)
    mixed = jnp.dot(
        weights.astype(jnp.bfloat16), value_rows, preferred_element_type=jnp.float32
    )
    return mixed / summed, peak, summed


def lane_heads(block):
    wide = block.astype(jnp.float32)
    lane = lax.broadcasted_iota(jnp.int32, wide.shape, 1) // AUDIO_DIM
    parts = [jnp.where(lane == i, wide, 0.0) for i in range(LANES // AUDIO_DIM)]
    return jnp.concatenate(parts, axis=0).astype(jnp.bfloat16)


def merge_lane_heads(stacked, rows):
    lane = lax.broadcasted_iota(jnp.int32, (rows, LANES), 1) // AUDIO_DIM
    merged = stacked[:rows]
    for i in range(1, LANES // AUDIO_DIM):
        merged = jnp.where(lane == i, stacked[i * rows : (i + 1) * rows], merged)
    return merged


def exchange_kernel(
    count,
    sub_count,
    vid_q,
    vid_k,
    vid_v,
    aud_q,
    cross_k,
    cross_v,
    cross_q,
    aud_k,
    aud_v,
    windows,
    video_self,
    audio_out,
    video_cross,
    land,
    land_aq,
    land_c,
    mixed_v,
    mixed_a,
    own_part,
    own_stat,
    far_part,
    far_stat,
    got_part,
    got_stat,
    near_k,
    near_v,
    local_cq,
    local_windows,
    send_sem,
    recv_sem,
    near_send,
    near_recv,
    part_send,
    part_recv,
    local_sem,
    ready_sem,
    all_sem,
):
    rows = vid_q.shape[0]
    audio_rows = aud_q.shape[0]
    video_each = vid_q.shape[1] // HEAD_DIM // count
    half = count // 2
    blocks_each = aud_q.shape[1] // LANES // half
    width = blocks_each * LANES
    video_scaling = 1.0 / math.sqrt(HEAD_DIM)
    audio_scaling = 1.0 / math.sqrt(AUDIO_DIM)
    me = lax.axis_index("seq") * sub_count + lax.axis_index("sub")

    side = me // half
    place = me % half

    def device(peer):
        return {"seq": peer // sub_count, "sub": peer % sub_count}

    def peer_near(t):
        return side * half + (place + 1 + t) % half

    chip = me // sub_count
    core = me % sub_count
    inner = (me >= half - sub_count) & (me < half + sub_count)
    outer = jnp.logical_not(inner)

    def inner_of(which, t):
        return half - (1 - which) * sub_count + (core + t) % sub_count

    def outer_of(which, t):
        return which * (half + sub_count) + (core + t) % sub_count

    def core_peer(t):
        return chip * sub_count + (core + 1 + t) % sub_count

    def near_inner(t):
        return inner_of(side, t)

    def near_outer(t):
        return outer_of(side, t)

    def far_inner(t):
        return inner_of(1 - side, t)

    def far_outer(t):
        return outer_of(1 - side, t)

    def out_peer(t):
        turn = t // sub_count
        chips = count // sub_count
        there = jnp.where(turn == side, chips // 2 - side, chip)
        there = jnp.where(turn == 1 - side, (1 - side) * (chips - 1), there)
        there = jnp.where(turn == 2, 2 * (chip // 2) + 1 - chip % 2, there)
        shift = t + turn // (chips - 1)
        return there * sub_count + (core + shift) % sub_count

    def signal(semaphore, peer):
        pl.semaphore_signal(
            semaphore, inc=1, device_id=device(peer), device_id_type=pl.DeviceIdType.MESH
        )

    barrier = pltpu.get_barrier_semaphore()

    @pl.when(inner)
    def _():
        for t in range(sub_count):
            signal(barrier, far_inner(t))

    for t in range(sub_count - 1):
        signal(barrier, core_peer(t))

    own = [
        pltpu.make_async_copy(cross_q, local_cq, local_sem.at[0]),
        pltpu.make_async_copy(aud_k, near_k.at[1], local_sem.at[1]),
        pltpu.make_async_copy(aud_v, near_v.at[1], local_sem.at[2]),
        pltpu.make_async_copy(windows, local_windows, local_sem.at[3]),
    ]
    for copy in own:
        copy.start()

    def column(index):
        return pl.ds(pl.multiple_of(index * LANES, LANES), LANES)

    def row(index):
        return pl.ds(pl.multiple_of(index * rows, rows), rows)

    def columns(index):
        return pl.ds(pl.multiple_of(index * width, LANES), width)

    def video_way(array, which, h):
        return (
            lambda peer: array.at[:, column(peer * video_each + h)],
            lambda source: land.at[which, h, row(source), :],
            2,
            4 + h,
        )

    def half_way(array, which):
        return (
            lambda peer: array.at[:, columns(peer % half)],
            lambda source: land_c.at[which, row(source % half), :],
            1,
            1,
        )

    ways = [
        (
            lambda peer: aud_q.at[:, columns(peer % half)],
            lambda source: land_aq.at[source],
            0,
            0,
        )
    ]
    audio_ways = [0]
    video_ways = []
    for h in range(video_each):
        video_ways.append(list(range(len(ways), len(ways) + 3)))
        for which, array in enumerate((vid_k, vid_v, vid_q)):
            ways.append(video_way(array, which, h))
        if h == 0:
            for which, array in enumerate((cross_k, cross_v)):
                audio_ways.append(len(ways))
                ways.append(half_way(array, which))
    first = len(ways)
    early = audio_ways[:1] + video_ways[0]
    late = [k for kinds in video_ways[1:] for k in kinds]
    for h in range(video_each):
        ways.append(
            (
                lambda peer, h=h: mixed_v.at[h, row(peer), :],
                lambda source, h=h: video_self.at[:, column(source * video_each + h)],
                3,
                2,
            )
        )
    ways.append(
        (
            lambda peer: mixed_a.at[peer % half],
            lambda source: audio_out.at[:, columns(source % half)],
            4,
            3,
        )
    )
    sent = (
        land_aq.at[pl.ds(0, count - 1)],
        land_c.at[:, pl.ds(0, (half - 1) * rows), :],
        land.at[:, :, pl.ds(0, (count - 1) * rows), :],
        mixed_v.at[:, pl.ds(0, (count - 1) * rows), :],
        mixed_a.at[pl.ds(0, half - 1)],
    )
    landed = [land_aq, land_c, video_self, audio_out]
    landed += [land.at[:, h] for h in range(video_each)]

    def outgoing(k, peer):
        return pltpu.make_async_remote_copy(
            src_ref=ways[k][0](peer),
            dst_ref=ways[k][1](me),
            send_sem=send_sem.at[ways[k][2]],
            recv_sem=recv_sem.at[ways[k][3]],
            device_id=device(peer),
            device_id_type=pl.DeviceIdType.MESH,
        )

    def kept(k):
        return pltpu.make_async_copy(ways[k][0](me), ways[k][1](me), recv_sem.at[ways[k][3]])

    def await_landed(i):
        pltpu.make_async_copy(landed[i], landed[i], recv_sem.at[i]).wait()

    def await_sent(i):
        pltpu.make_async_copy(sent[i], sent[i], send_sem.at[i]).wait()

    def near_copy(array, near, slot, peer):
        return pltpu.make_async_remote_copy(
            src_ref=array,
            dst_ref=near.at[slot],
            send_sem=near_send.at[slot // 2],
            recv_sem=near_recv.at[slot // 2],
            device_id=device(peer),
            device_id_type=pl.DeviceIdType.MESH,
        )

    near_pairs = ((aud_k, near_k), (aud_v, near_v))

    def send_right():
        for array, near in near_pairs:
            near_copy(array, near, 0, me + 1).start()

    def send_left():
        for array, near in near_pairs:
            near_copy(array, near, 2, me - 1).start()

    def await_near(semaphore):
        both = near_k.at[pl.ds(0, 2)]
        pltpu.make_async_copy(both, both, semaphore).wait()

    def send(k, peer_of, steps):
        def one(t, carry):
            outgoing(k, peer_of(t)).start()
            return carry

        lax.fori_loop(0, steps, one, 0)

    pair = sub_count - 1
    audio_only = audio_ways[1:]

    def send_keep(ks):
        for k in ks:
            send(k, core_peer, pair)
            kept(k).start()

    @pl.when(inner)
    def _():
        pl.semaphore_wait(barrier, 2 * sub_count - 1)
        for t in range(sub_count):
            signal(barrier, near_outer(t))
        for k in early:
            send(k, far_inner, sub_count)

        @pl.when(side == 0)
        def _():
            send_right()

            @pl.when(core > 0)
            def _():
                send_left()

        @pl.when(side == 1)
        def _():
            send_left()

            @pl.when(core < sub_count - 1)
            def _():
                send_right()

        send_keep(early[:1] + audio_only)
        pl.semaphore_wait(ready_sem.at[side], sub_count)

        @pl.when((side == 0) & (core == 0))
        def _():
            send_left()

        @pl.when((side == 1) & (core == sub_count - 1))
        def _():
            send_right()

        for k in early[:1] + audio_only + early[1:] + late:
            send(k, near_outer, sub_count)
        pl.semaphore_wait(ready_sem.at[1 - side], sub_count)
        signal(all_sem, near_outer(0))
        for k in early:
            send(k, far_outer, sub_count)
        for k in late:
            send(k, far_inner, sub_count)
        for k in late:
            send(k, far_outer, sub_count)
        send_keep(early[1:] + late)

    @pl.when(outer)
    def _():
        pl.semaphore_wait(barrier, 2 * sub_count - 1)
        for t in range(sub_count):
            signal(ready_sem.at[side], near_inner(t))
            signal(ready_sem.at[side], far_inner(t))

        for k in early[:1]:
            send(k, far_inner, sub_count)

        @pl.when(me < count - 1)
        def _():
            send_right()

        @pl.when(me > 0)
        def _():
            send_left()

        for k in early[:1] + audio_only:
            send(k, near_inner, sub_count)
        send_keep(early[:1] + audio_only)
        pl.semaphore_wait(all_sem, 1)
        for k in early[:1]:
            send(k, far_outer, sub_count)
        for k in early[1:] + late:
            send(k, near_inner, sub_count)
        for ks in (early[1:], late):
            for k in ks:
                send(k, far_outer, sub_count)
            for k in ks:
                send(k, far_inner, sub_count)
        send_keep(early[1:] + late)

    @pl.when(me == 0)
    def _():
        for array, near in near_pairs:
            near[0] = jnp.zeros(near.shape[1:], near.dtype)

    @pl.when(me == count - 1)
    def _():
        for array, near in near_pairs:
            near[2] = jnp.zeros(near.shape[1:], near.dtype)

    for copy in own:
        copy.wait()

    @pl.when(me > 0)
    def _():
        await_near(near_recv.at[0])

    @pl.when(me < count - 1)
    def _():
        await_near(near_recv.at[1])

    spans = windows.shape[1]
    tile = (me * rows + lax.broadcasted_iota(jnp.int32, (rows, spans), 0)) // TILE_LEN
    bounds = local_windows[...]
    inside = (bounds[0:1, :] <= tile) & (tile < bounds[1:2, :])
    inside = jnp.where(inside, 1.0, 0.0).astype(jnp.bfloat16)
    seen = []
    for slot in range(3):
        stretch = lax.broadcasted_iota(jnp.int32, (spans, audio_rows), 1) // STRETCH_LEN
        stretch = stretch + (me + slot - 1) * (audio_rows // STRETCH_LEN)
        picks = stretch == lax.broadcasted_iota(jnp.int32, (spans, audio_rows), 0)
        picks = jnp.where(picks, 1.0, 0.0).astype(jnp.bfloat16)
        part = jnp.dot(inside, picks, preferred_element_type=jnp.float32)
        seen.append(jnp.concatenate([part] * (LANES // AUDIO_DIM), axis=0))

    for b in range(cross_q.shape[1] // LANES):
        lanes = slice(b * LANES, (b + 1) * LANES)
        stacked = lane_heads(local_cq[:, lanes])
        scores = []
        for slot in range(3):
            part = lax.dot_general(
                stacked,
                near_k[slot, :, lanes],
                (((1,), (1,)), ((), ())),
                preferred_element_type=jnp.float32,
            )
            scores.append(jnp.where(seen[slot] > 0.5, part, jnp.float32(-1e30)))
        peak = jnp.max(jnp.maximum(jnp.maximum(scores[0], scores[1]), scores[2]), axis=1, keepdims=True)
        factor = jnp.float32(audio_scaling * math.log2(math.e))
        weights = [jnp.exp2((part - peak) * factor) for part in scores]
        summed = jnp.sum(weights[0] + weights[1] + weights[2], axis=1, keepdims=True)
        mixed = sum(
            jnp.dot(
                weights[slot].astype(jnp.bfloat16),
                near_v[slot, :, lanes],
                preferred_element_type=jnp.float32,
            )
            for slot in range(3)
        )
        video_cross[:, lanes] = merge_lane_heads(mixed / summed, rows).astype(jnp.bfloat16)

    def part_copy(j, array, land):
        return pltpu.make_async_remote_copy(
            src_ref=array,
            dst_ref=land,
            send_sem=part_send.at[j],
            recv_sem=part_recv.at[j],
            device_id=device((me + half) % count),
            device_id_type=pl.DeviceIdType.MESH,
        )

    part_copies = [part_copy(0, far_part, got_part), part_copy(1, far_stat, got_stat)]
    each = LANES // AUDIO_DIM
    levels = half * blocks_each * each
    folds = level_folds(levels, audio_rows)
    span = LANES // folds
    stat_row = lax.broadcasted_iota(jnp.int32, (LANES, LANES), 0) // span
    stat_lane = lax.broadcasted_iota(jnp.int32, (LANES, LANES), 1)

    def audio_parts(first_source, part, stat):
        def one(j, stats):
            queries = land_aq[first_source + j]
            for b in range(blocks_each):
                lanes = slice(b * LANES, (b + 1) * LANES)
                mixed, peak, summed = softmax_mix(
                    lane_heads(queries[:, lanes]), land_c[0, :, lanes], land_c[1, :, lanes], audio_scaling
                )
                part[j, :, lanes] = merge_lane_heads(mixed, audio_rows).astype(part.dtype)
                level = peak * jnp.float32(audio_scaling * math.log2(math.e)) + jnp.log2(summed)
                rest = jnp.zeros((span - audio_rows, 1), jnp.float32)
                for i in range(each):
                    index = (j * blocks_each + b) * each + i
                    picked = stat_lane * folds + stat_row == index
                    held = level[i * audio_rows : (i + 1) * audio_rows]
                    stats = jnp.where(picked, jnp.concatenate([held, rest] * folds, axis=0), stats)
            return stats

        stats = lax.fori_loop(0, half, one, jnp.zeros((LANES, LANES), jnp.float32))
        stat[...] = stats.T[: stat.shape[0]]

    def merge_parts(peer):
        j = peer % half
        unpacked = []
        for stat in (own_stat, got_stat):
            rest = jnp.zeros((LANES - stat.shape[0], LANES), jnp.float32)
            unpacked.append(jnp.concatenate([stat[...], rest], axis=0).T)
        for b in range(blocks_each):
            lanes = slice(b * LANES, (b + 1) * LANES)
            shares = []
            for i in range(each):
                picked = stat_lane * folds + stat_row == (j * blocks_each + b) * each + i
                mine, other = (
                    sum(kept_rows[g * span : g * span + audio_rows] for g in range(folds))
                    for kept_rows in (
                        jnp.sum(jnp.where(picked, wide, 0.0), axis=1, keepdims=True)
                        for wide in unpacked
                    )
                )
                peak = jnp.maximum(mine, other)
                mine = jnp.exp2(mine - peak)
                other = jnp.exp2(other - peak)
                total = mine + other
                shares.append((mine / total, other / total))
            own_share, got_share = (
                merge_lane_heads(
                    jnp.concatenate(
                        [jnp.broadcast_to(s[w], (audio_rows, LANES)) for s in shares], axis=0
                    ),
                    audio_rows,
                )
                for w in range(2)
            )
            merged = own_part[j, :, lanes] * own_share
            merged = merged + got_part[j, :, lanes].astype(jnp.float32) * got_share
            mixed_a[j, :, lanes] = merged.astype(jnp.bfloat16)

    await_landed(0)
    await_landed(1)
    audio_parts((1 - side) * half, far_part, far_stat)
    audio_parts(side * half, own_part, own_stat)

    def mix_video(h, source):
        mixed, peak, summed = softmax_mix(
            land[2, h, row(source), :], land[0, h], land[1, h], video_scaling
        )
        mixed_v[h, row(source), :] = mixed.astype(jnp.bfloat16)

    for copy in part_copies:
        copy.start()

    def gated(turn):
        return inner & (turn == 0)

    def delayed(turn):
        return (inner | (side == 1)) & (turn == 1)

    def send_held(condition):
        for earlier in range(video_each - 1):
            for i in range(2 * sub_count):

                @pl.when(condition(i // sub_count))
                def _():
                    outgoing(first + earlier, out_peer(i)).start()

    for h in range(video_each):
        await_landed(4 + h)
        last = h == video_each - 1
        if last:
            send_held(gated)

        def one(t, carry, h=h, last=last):
            mix_video(h, out_peer(t))
            now = t > 0
            if not last:
                turn = (t - 1) // sub_count
                now = now & jnp.logical_not(gated(turn) | delayed(turn))

            @pl.when(now)
            def _():
                outgoing(first + h, out_peer(t - 1)).start()

            if last:

                @pl.when(t == sub_count)
                def _():
                    send_held(delayed)

            return carry

        lax.fori_loop(0, count, one, 0)
        kept(first + h).start()
    for copy in part_copies:
        copy.wait()
    merged = len(ways) - 1

    def one_merge(t, carry):
        merge_parts(peer_near(t))

        @pl.when(t < half - 1)
        def _():
            outgoing(merged, peer_near(t)).start()

        return carry

    lax.fori_loop(0, half, one_merge, 0)
    kept(merged).start()

    for i in range(len(sent)):
        await_sent(i)
    await_landed(2)
    await_landed(3)

    @pl.when(me < count - 1)
    def _():
        await_near(near_send.at[0])

    @pl.when(me > 0)
    def _():
        await_near(near_send.at[1])


def level_folds(levels, audio_rows):
    folds = 1
    while levels % (2 * folds) == 0 and levels > 8 * folds and LANES >= 2 * folds * audio_rows:
        folds = 2 * folds
    return folds


def store_kernel(*refs):
    copies = [pltpu.make_async_copy(refs[i], refs[3 + i], refs[6].at[i]) for i in range(3)]
    for copy in copies:
        copy.start()
    for copy in copies:
        copy.wait()


def exchanged_body(count, sub_count, *arrays):
    vid_q, vid_k, vid_v, aud_q, cross_k, cross_v, cross_q, aud_k, aud_v, windows = arrays
    rows = vid_q.shape[0]
    audio_rows = aud_q.shape[0]
    video_each = vid_q.shape[1] // HEAD_DIM // count
    halves = count // 2
    width = aud_q.shape[1] // halves
    levels = aud_q.shape[1] // AUDIO_DIM
    levels = -(-levels // level_folds(levels, audio_rows) // 8) * 8
    half = jnp.bfloat16
    place = pl.BlockSpec(memory_space=pl.ANY)
    held = pl.pallas_call(
        partial(exchange_kernel, count, sub_count),
        out_shape=tuple(pltpu.VMEM(a.shape, half) for a in (vid_q, aud_q, cross_q)),
        in_specs=[place] * 10,
        out_specs=(pl.BlockSpec(memory_space=pltpu.VMEM),) * 3,
        scratch_shapes=[
            pltpu.VMEM((3, video_each, count * rows, HEAD_DIM), half),
            pltpu.VMEM((count, audio_rows, width), half),
            pltpu.VMEM((2, halves * rows, width), half),
            pltpu.VMEM((video_each, count * rows, HEAD_DIM), half),
            pltpu.VMEM((halves, audio_rows, width), half),
            pltpu.VMEM((halves, audio_rows, width), jnp.float32),
            pltpu.VMEM((levels, LANES), jnp.float32),
            pltpu.VMEM((halves, audio_rows, width), half),
            pltpu.VMEM((levels, LANES), jnp.float32),
            pltpu.VMEM((halves, audio_rows, width), half),
            pltpu.VMEM((levels, LANES), jnp.float32),
            pltpu.VMEM((3, audio_rows, aud_k.shape[1]), half),
            pltpu.VMEM((3, audio_rows, aud_k.shape[1]), half),
            pltpu.VMEM(cross_q.shape, half),
            pltpu.VMEM(windows.shape, windows.dtype),
            pltpu.SemaphoreType.DMA((5,)),
            pltpu.SemaphoreType.DMA((4 + video_each,)),
            pltpu.SemaphoreType.DMA((2,)),
            pltpu.SemaphoreType.DMA((2,)),
            pltpu.SemaphoreType.DMA((2,)),
            pltpu.SemaphoreType.DMA((2,)),
            pltpu.SemaphoreType.DMA((4,)),
            pltpu.SemaphoreType.REGULAR((2,)),
            pltpu.SemaphoreType.REGULAR,
        ],
        compiler_params=pltpu.CompilerParams(collective_id=0, has_side_effects=True),
        name="joint_attention",
    )(*arrays)
    return pl.pallas_call(
        store_kernel,
        out_shape=tuple(jax.ShapeDtypeStruct(a.shape, half) for a in (vid_q, aud_q, cross_q)),
        in_specs=[pl.BlockSpec(memory_space=pltpu.VMEM)] * 3,
        out_specs=(place, place, place),
        scratch_shapes=[pltpu.SemaphoreType.DMA((3,))],
        name="store_results",
    )(*[pltpu.with_memory_space_constraint(x, pltpu.VMEM) for x in held])


def body(*arrays):
    sub_count = lax.axis_size("sub")
    count = lax.axis_size("seq") * sub_count
    video_heads = arrays[0].shape[1] // HEAD_DIM
    audio_heads = arrays[3].shape[1] // AUDIO_DIM
    halved = count == 4 * sub_count and max(audio_heads, arrays[3].shape[0]) <= LANES
    if halved and video_heads % count == 0 and audio_heads % count == 0:
        return exchanged_body(count, sub_count, *arrays)
    return gathered_body(*arrays)


def solution(mesh):
    return jax.shard_map(
        body,
        mesh=mesh,
        in_specs=(
            P(("grp", "seq", "sub"), "head"),
            P(("grp", "seq", "sub"), "head"),
            P(("grp", "seq", "sub"), "head"),
            P(("grp", "seq", "sub"), "head"),
            P(("grp", "seq", "sub"), "head"),
            P(("grp", "seq", "sub"), "head"),
            P(("grp", "seq", "sub"), "head"),
            P(("grp", "seq", "sub"), "head"),
            P(("grp", "seq", "sub"), "head"),
            P(None, "grp"),
        ),
        out_specs=(
            P(("grp", "seq", "sub"), "head"),
            P(("grp", "seq", "sub"), "head"),
            P(("grp", "seq", "sub"), "head"),
        ),
        check_vma=False,
    )
```

```python
from functools import partial
import math

import jax
import jax.numpy as jnp
from jax import lax
from jax.experimental import pallas as pl
from jax.experimental.pallas import tpu as pltpu
from jax.sharding import PartitionSpec as P

HEAD_DIM = 128
AUDIO_DIM = 64
TILE_LEN = 32
STRETCH_LEN = 8


def extended(cells, sides, width):
    for axis, dim in sides:
        count = lax.axis_size(axis)
        ends = count - 1
        head = lax.slice_in_dim(cells, 0, width, axis=dim)
        tail = lax.slice_in_dim(cells, cells.shape[dim] - width, cells.shape[dim], axis=dim)
        cells = jnp.concatenate(
            [
                lax.ppermute(tail, axis, [(i, (i + 1) % count) for i in range(ends)]),
                cells,
                lax.ppermute(head, axis, [((i + 1) % count, i) for i in range(ends)]),
            ],
            axis=dim,
        )
    return cells


def start_state(query_count, head_count, head_size):
    running = jnp.full((head_count, query_count), -jnp.inf, jnp.float32)
    summed = jnp.zeros((head_count, query_count), jnp.float32)
    numerator = jnp.zeros((head_count, query_count, head_size), jnp.float32)
    return (running, summed, numerator)


def absorb(state_in, queries, key_rows, value_rows, head_count, scaling, visible):
    running, summed, numerator = state_in
    query_count = queries.shape[0]
    key_count = key_rows.shape[0]
    head_size = queries.shape[1] // head_count
    scores = (
        jnp.einsum(
            "qhe,khe->hqk",
            queries.reshape(query_count, head_count, head_size),
            key_rows.reshape(key_count, head_count, head_size),
            preferred_element_type=jnp.float32,
        )
        * scaling
    )
    if visible is not None:
        scores = jnp.where(visible[None], scores, jnp.float32(-1e30))
    newest = jnp.maximum(running, jnp.max(scores, axis=2))
    shrink = jnp.exp(running - newest)
    weights = jnp.exp(scores - newest[:, :, None])
    summed = summed * shrink + jnp.sum(weights, axis=2)
    numerator = numerator * shrink[:, :, None] + jnp.einsum(
        "hqk,khe->hqe",
        weights.astype(jnp.bfloat16),
        value_rows.reshape(key_count, head_count, head_size),
        preferred_element_type=jnp.float32,
    )
    return (newest, summed, numerator)


def block_split(total_rows):
    block_rows = total_rows
    while block_rows > 512 and block_rows % 2 == 0:
        block_rows = block_rows // 2
    return (block_rows, total_rows // block_rows)


def fold_keys(state_in, shards_in, offset, queries, head_count, scaling):
    key_rows, value_rows = shards_in
    block_rows, block_count = block_split(key_rows.shape[0])
    key_blocks = key_rows.reshape(block_count, block_rows, key_rows.shape[1])
    value_blocks = value_rows.reshape(block_count, block_rows, value_rows.shape[1])

    def one_block(state, paired):
        return (absorb(state, queries, paired[0], paired[1], head_count, scaling, None), None)

    result, unused = lax.scan(one_block, state_in, (key_blocks, value_blocks))
    return result


def normalize_heads(state_in):
    running, summed, numerator = state_in
    mixed = numerator / summed[:, :, None]
    return mixed.transpose(1, 0, 2).reshape(mixed.shape[1], -1).astype(jnp.bfloat16)


def gathered_body(vid_q, vid_k, vid_v, aud_q, cross_k, cross_v, cross_q, aud_k, aud_v, windows):
    video_heads = vid_q.shape[1] // HEAD_DIM
    video_scaling = 1.0 / math.sqrt(HEAD_DIM)
    audio_heads = aud_q.shape[1] // AUDIO_DIM
    audio_scaling = 1.0 / math.sqrt(AUDIO_DIM)
    moved_q, moved_k, moved_v = (
        lax.all_to_all(vid_q, "sub", split_axis=1, concat_axis=0, tiled=True),
        lax.all_to_all(vid_k, "sub", split_axis=1, concat_axis=0, tiled=True),
        lax.all_to_all(vid_v, "sub", split_axis=1, concat_axis=0, tiled=True),
    )
    pair_heads = video_heads // lax.axis_size("sub")
    folder = partial(fold_keys, queries=moved_q, head_count=pair_heads, scaling=video_scaling)
    state = folder(
        start_state(moved_q.shape[0], pair_heads, HEAD_DIM),
        (
            lax.all_gather(moved_k, "seq", axis=0, tiled=True),
            lax.all_gather(moved_v, "seq", axis=0, tiled=True),
        ),
        jnp.int32(0),
    )
    video_self = lax.all_to_all(
        normalize_heads(state), "sub", split_axis=0, concat_axis=1, tiled=True
    )
    folder = partial(fold_keys, queries=aud_q, head_count=audio_heads, scaling=audio_scaling)
    state = folder(
        start_state(aud_q.shape[0], audio_heads, AUDIO_DIM),
        (
            lax.all_gather(cross_k, ("seq", "sub"), axis=0, tiled=True),
            lax.all_gather(cross_v, ("seq", "sub"), axis=0, tiled=True),
        ),
        jnp.int32(0),
    )
    audio_out = normalize_heads(state)
    audio_rows = aud_k.shape[0]
    key_width = aud_k.shape[1]
    padded_rows = extended(
        jnp.concatenate((aud_k, aud_v), axis=1), ((("seq", "sub"), 0),), audio_rows
    )
    near_keys = padded_rows[:, :key_width]
    near_values = padded_rows[:, key_width:]
    position = lax.axis_index(("seq", "sub"))
    audio_index = (position - 1) * audio_rows + jnp.arange(padded_rows.shape[0], dtype=jnp.int32)
    stretch_index = audio_index // STRETCH_LEN
    stretch_ids = jnp.arange(windows.shape[1], dtype=jnp.int32)
    onehot = stretch_index[:, None] == stretch_ids[None, :]
    first_tile = jnp.sum(jnp.where(onehot, windows[0][None, :], 0), axis=1)
    after_tile = jnp.sum(jnp.where(onehot, windows[1][None, :], 0), axis=1)
    video_rows = cross_q.shape[0]
    video_tile = (position * video_rows + jnp.arange(video_rows, dtype=jnp.int32)) // TILE_LEN
    visible = (first_tile[None, :] <= video_tile[:, None]) & (
        video_tile[:, None] < after_tile[None, :]
    )
    state = absorb(
        start_state(video_rows, audio_heads, AUDIO_DIM),
        cross_q,
        near_keys,
        near_values,
        audio_heads,
        audio_scaling,
        visible,
    )
    video_cross = normalize_heads(state)
    return (video_self, audio_out, video_cross)


LANES = 128
AXES = ("seq", "sub")


def softmax_mix(queries, key_rows, value_rows, scaling):
    scores = lax.dot_general(
        queries, key_rows, (((1,), (1,)), ((), ())), preferred_element_type=jnp.float32
    )
    peak = jnp.max(scores, axis=1, keepdims=True)
    weights = jnp.exp2((scores - peak) * jnp.float32(scaling * math.log2(math.e)))
    summed = jnp.sum(weights, axis=1, keepdims=True)
    mixed = jnp.dot(
        weights.astype(jnp.bfloat16), value_rows, preferred_element_type=jnp.float32
    )
    return mixed / summed, peak, summed


def lane_heads(block):
    wide = block.astype(jnp.float32)
    lane = lax.broadcasted_iota(jnp.int32, wide.shape, 1) // AUDIO_DIM
    parts = [jnp.where(lane == i, wide, 0.0) for i in range(LANES // AUDIO_DIM)]
    return jnp.concatenate(parts, axis=0).astype(jnp.bfloat16)


def merge_lane_heads(stacked, rows):
    lane = lax.broadcasted_iota(jnp.int32, (rows, LANES), 1) // AUDIO_DIM
    merged = stacked[:rows]
    for i in range(1, LANES // AUDIO_DIM):
        merged = jnp.where(lane == i, stacked[i * rows : (i + 1) * rows], merged)
    return merged


def exchange_kernel(
    count,
    sub_count,
    vid_q,
    vid_k,
    vid_v,
    aud_q,
    cross_k,
    cross_v,
    cross_q,
    aud_k,
    aud_v,
    windows,
    video_self,
    audio_out,
    video_cross,
    land,
    land_aq,
    land_c,
    mixed_v,
    mixed_a,
    own_part,
    own_stat,
    far_part,
    far_stat,
    got_part,
    got_stat,
    near_k,
    near_v,
    local_cq,
    local_windows,
    send_sem,
    recv_sem,
    near_send,
    near_recv,
    part_send,
    part_recv,
    local_sem,
    ready_sem,
    all_sem,
):
    rows = vid_q.shape[0]
    audio_rows = aud_q.shape[0]
    video_each = vid_q.shape[1] // HEAD_DIM // count
    half = count // 2
    blocks_each = aud_q.shape[1] // LANES // half
    width = blocks_each * LANES
    video_scaling = 1.0 / math.sqrt(HEAD_DIM)
    audio_scaling = 1.0 / math.sqrt(AUDIO_DIM)
    me = lax.axis_index("seq") * sub_count + lax.axis_index("sub")

    side = me // half
    place = me % half

    def device(peer):
        return {"seq": peer // sub_count, "sub": peer % sub_count}

    def peer_near(t):
        return side * half + (place + 1 + t) % half

    chip = me // sub_count
    core = me % sub_count
    inner = (me >= half - sub_count) & (me < half + sub_count)
    outer = jnp.logical_not(inner)

    def inner_of(which, t):
        return half - (1 - which) * sub_count + (core + t) % sub_count

    def outer_of(which, t):
        return which * (half + sub_count) + (core + t) % sub_count

    def core_peer(t):
        return chip * sub_count + (core + 1 + t) % sub_count

    def near_inner(t):
        return inner_of(side, t)

    def near_outer(t):
        return outer_of(side, t)

    def far_inner(t):
        return inner_of(1 - side, t)

    def far_outer(t):
        return outer_of(1 - side, t)

    def last_peer(t):
        turn = t // sub_count
        kind = turn
        for i, k in enumerate((0, 1, 2)):
            kind = jnp.where(outer & (turn == i), k, kind)
        return out_peer(kind * sub_count + t % sub_count)

    def out_peer(t):
        turn = t // sub_count
        chips = count // sub_count
        there = jnp.where(turn == side, chips // 2 - side, chip)
        there = jnp.where(turn == 1 - side, (1 - side) * (chips - 1), there)
        there = jnp.where(turn == 2, 2 * (chip // 2) + 1 - chip % 2, there)
        shift = t + turn // (chips - 1)
        return there * sub_count + (core + shift) % sub_count

    def signal(semaphore, peer):
        pl.semaphore_signal(
            semaphore, inc=1, device_id=device(peer), device_id_type=pl.DeviceIdType.MESH
        )

    barrier = pltpu.get_barrier_semaphore()

    @pl.when(inner)
    def _():
        for t in range(sub_count):
            signal(barrier, far_inner(t))

    for t in range(sub_count - 1):
        signal(barrier, core_peer(t))

    own = [
        pltpu.make_async_copy(cross_q, local_cq, local_sem.at[0]),
        pltpu.make_async_copy(aud_k, near_k.at[1], local_sem.at[1]),
        pltpu.make_async_copy(aud_v, near_v.at[1], local_sem.at[2]),
        pltpu.make_async_copy(windows, local_windows, local_sem.at[3]),
    ]
    for copy in own:
        copy.start()

    def column(index):
        return pl.ds(pl.multiple_of(index * LANES, LANES), LANES)

    def row(index):
        return pl.ds(pl.multiple_of(index * rows, rows), rows)

    def columns(index):
        return pl.ds(pl.multiple_of(index * width, LANES), width)

    def video_way(array, which, h):
        return (
            lambda peer: array.at[:, column(peer * video_each + h)],
            lambda source: land.at[which, h, row(source), :],
            2,
            4 + h,
        )

    def half_way(array, which):
        return (
            lambda peer: array.at[:, columns(peer % half)],
            lambda source: land_c.at[which, row(source % half), :],
            1,
            1,
        )

    ways = [
        (
            lambda peer: aud_q.at[:, columns(peer % half)],
            lambda source: land_aq.at[source],
            0,
            0,
        )
    ]
    audio_ways = [0]
    video_ways = []
    for h in range(video_each):
        video_ways.append(list(range(len(ways), len(ways) + 3)))
        for which, array in enumerate((vid_k, vid_v, vid_q)):
            ways.append(video_way(array, which, h))
        if h == 0:
            for which, array in enumerate((cross_k, cross_v)):
                audio_ways.append(len(ways))
                ways.append(half_way(array, which))
    first = len(ways)
    early = audio_ways[:1] + video_ways[0]
    late = [k for kinds in video_ways[1:] for k in kinds]
    for h in range(video_each):
        ways.append(
            (
                lambda peer, h=h: mixed_v.at[h, row(peer), :],
                lambda source, h=h: video_self.at[:, column(source * video_each + h)],
                3,
                2,
            )
        )
    ways.append(
        (
            lambda peer: mixed_a.at[peer % half],
            lambda source: audio_out.at[:, columns(source % half)],
            4,
            3,
        )
    )
    sent = (
        land_aq.at[pl.ds(0, count - 1)],
        land_c.at[:, pl.ds(0, (half - 1) * rows), :],
        land.at[:, :, pl.ds(0, (count - 1) * rows), :],
        mixed_v.at[:, pl.ds(0, (count - 1) * rows), :],
        mixed_a.at[pl.ds(0, half - 1)],
    )
    landed = [land_aq, land_c, video_self, audio_out]
    landed += [land.at[:, h] for h in range(video_each)]

    def outgoing(k, peer):
        return pltpu.make_async_remote_copy(
            src_ref=ways[k][0](peer),
            dst_ref=ways[k][1](me),
            send_sem=send_sem.at[ways[k][2]],
            recv_sem=recv_sem.at[ways[k][3]],
            device_id=device(peer),
            device_id_type=pl.DeviceIdType.MESH,
        )

    def kept(k):
        return pltpu.make_async_copy(ways[k][0](me), ways[k][1](me), recv_sem.at[ways[k][3]])

    def await_landed(i):
        pltpu.make_async_copy(landed[i], landed[i], recv_sem.at[i]).wait()

    def await_sent(i):
        pltpu.make_async_copy(sent[i], sent[i], send_sem.at[i]).wait()

    def near_copy(array, near, slot, peer):
        return pltpu.make_async_remote_copy(
            src_ref=array,
            dst_ref=near.at[slot],
            send_sem=near_send.at[slot // 2],
            recv_sem=near_recv.at[slot // 2],
            device_id=device(peer),
            device_id_type=pl.DeviceIdType.MESH,
        )

    near_pairs = ((aud_k, near_k), (aud_v, near_v))

    def send_right():
        for array, near in near_pairs:
            near_copy(array, near, 0, me + 1).start()

    def send_left():
        for array, near in near_pairs:
            near_copy(array, near, 2, me - 1).start()

    def await_near(semaphore):
        both = near_k.at[pl.ds(0, 2)]
        pltpu.make_async_copy(both, both, semaphore).wait()

    def send(k, peer_of, steps):
        def one(t, carry):
            outgoing(k, peer_of(t)).start()
            return carry

        lax.fori_loop(0, steps, one, 0)

    pair = sub_count - 1
    audio_only = audio_ways[1:]

    def send_keep(ks):
        for k in ks:
            send(k, core_peer, pair)
            kept(k).start()

    @pl.when(inner)
    def _():
        pl.semaphore_wait(barrier, 2 * sub_count - 1)
        for t in range(sub_count):
            signal(barrier, near_outer(t))
        for k in early:
            send(k, far_inner, sub_count)

        @pl.when(side == 0)
        def _():
            send_right()

            @pl.when(core > 0)
            def _():
                send_left()

        @pl.when(side == 1)
        def _():
            send_left()

            @pl.when(core < sub_count - 1)
            def _():
                send_right()

        send_keep(early[:1] + audio_only)
        pl.semaphore_wait(ready_sem.at[side], sub_count)

        @pl.when((side == 0) & (core == 0))
        def _():
            send_left()

        @pl.when((side == 1) & (core == sub_count - 1))
        def _():
            send_right()

        for k in early[:1] + audio_only + early[1:] + late:
            send(k, near_outer, sub_count)
        pl.semaphore_wait(ready_sem.at[1 - side], sub_count)
        signal(all_sem, near_outer(0))
        for k in early:
            send(k, far_outer, sub_count)
        for k in late:
            send(k, far_inner, sub_count)
        for k in late:
            send(k, far_outer, sub_count)
        send_keep(early[1:] + late)

    @pl.when(outer)
    def _():
        pl.semaphore_wait(barrier, 2 * sub_count - 1)
        for t in range(sub_count):
            signal(ready_sem.at[side], near_inner(t))
            signal(ready_sem.at[side], far_inner(t))

        for k in early[:1]:
            send(k, far_inner, sub_count)

        @pl.when(me < count - 1)
        def _():
            send_right()

        @pl.when(me > 0)
        def _():
            send_left()

        for k in early[:1] + audio_only:
            send(k, near_inner, sub_count)
        send_keep(early[:1] + audio_only)
        pl.semaphore_wait(all_sem, 1)
        for k in early[:1]:
            send(k, far_outer, sub_count)
        for k in early[1:] + late:
            send(k, near_inner, sub_count)
        for ks in (early[1:], late):
            for k in ks:
                send(k, far_outer, sub_count)
            for k in ks:
                send(k, far_inner, sub_count)
        send_keep(early[1:] + late)

    @pl.when(me == 0)
    def _():
        for array, near in near_pairs:
            near[0] = jnp.zeros(near.shape[1:], near.dtype)

    @pl.when(me == count - 1)
    def _():
        for array, near in near_pairs:
            near[2] = jnp.zeros(near.shape[1:], near.dtype)

    for copy in own:
        copy.wait()

    @pl.when(me > 0)
    def _():
        await_near(near_recv.at[0])

    @pl.when(me < count - 1)
    def _():
        await_near(near_recv.at[1])

    spans = windows.shape[1]
    tile = (me * rows + lax.broadcasted_iota(jnp.int32, (rows, spans), 0)) // TILE_LEN
    bounds = local_windows[...]
    inside = (bounds[0:1, :] <= tile) & (tile < bounds[1:2, :])
    inside = jnp.where(inside, 1.0, 0.0).astype(jnp.bfloat16)
    seen = []
    for slot in range(3):
        stretch = lax.broadcasted_iota(jnp.int32, (spans, audio_rows), 1) // STRETCH_LEN
        stretch = stretch + (me + slot - 1) * (audio_rows // STRETCH_LEN)
        picks = stretch == lax.broadcasted_iota(jnp.int32, (spans, audio_rows), 0)
        picks = jnp.where(picks, 1.0, 0.0).astype(jnp.bfloat16)
        part = jnp.dot(inside, picks, preferred_element_type=jnp.float32)
        seen.append(jnp.concatenate([part] * (LANES // AUDIO_DIM), axis=0))

    for b in range(cross_q.shape[1] // LANES):
        lanes = slice(b * LANES, (b + 1) * LANES)
        stacked = lane_heads(local_cq[:, lanes])
        scores = []
        for slot in range(3):
            part = lax.dot_general(
                stacked,
                near_k[slot, :, lanes],
                (((1,), (1,)), ((), ())),
                preferred_element_type=jnp.float32,
            )
            scores.append(jnp.where(seen[slot] > 0.5, part, jnp.float32(-1e30)))
        peak = jnp.max(jnp.maximum(jnp.maximum(scores[0], scores[1]), scores[2]), axis=1, keepdims=True)
        factor = jnp.float32(audio_scaling * math.log2(math.e))
        weights = [jnp.exp2((part - peak) * factor) for part in scores]
        summed = jnp.sum(weights[0] + weights[1] + weights[2], axis=1, keepdims=True)
        mixed = sum(
            jnp.dot(
                weights[slot].astype(jnp.bfloat16),
                near_v[slot, :, lanes],
                preferred_element_type=jnp.float32,
            )
            for slot in range(3)
        )
        video_cross[:, lanes] = merge_lane_heads(mixed / summed, rows).astype(jnp.bfloat16)

    def part_copy(j, array, land):
        return pltpu.make_async_remote_copy(
            src_ref=array,
            dst_ref=land,
            send_sem=part_send.at[j],
            recv_sem=part_recv.at[j],
            device_id=device((me + half) % count),
            device_id_type=pl.DeviceIdType.MESH,
        )

    part_copies = [part_copy(0, far_part, got_part), part_copy(1, far_stat, got_stat)]
    each = LANES // AUDIO_DIM
    levels = half * blocks_each * each
    folds = level_folds(levels, audio_rows)
    span = LANES // folds
    stat_row = lax.broadcasted_iota(jnp.int32, (LANES, LANES), 0) // span
    stat_lane = lax.broadcasted_iota(jnp.int32, (LANES, LANES), 1)

    def audio_parts(first_source, part, stat):
        def one(j, stats):
            queries = land_aq[first_source + j]
            for b in range(blocks_each):
                lanes = slice(b * LANES, (b + 1) * LANES)
                mixed, peak, summed = softmax_mix(
                    lane_heads(queries[:, lanes]), land_c[0, :, lanes], land_c[1, :, lanes], audio_scaling
                )
                part[j, :, lanes] = merge_lane_heads(mixed, audio_rows).astype(part.dtype)
                level = peak * jnp.float32(audio_scaling * math.log2(math.e)) + jnp.log2(summed)
                rest = jnp.zeros((span - audio_rows, 1), jnp.float32)
                for i in range(each):
                    index = (j * blocks_each + b) * each + i
                    picked = stat_lane * folds + stat_row == index
                    held = level[i * audio_rows : (i + 1) * audio_rows]
                    stats = jnp.where(picked, jnp.concatenate([held, rest] * folds, axis=0), stats)
            return stats

        stats = lax.fori_loop(0, half, one, jnp.zeros((LANES, LANES), jnp.float32))
        stat[...] = stats.T[: stat.shape[0]]

    def merge_parts(peer):
        j = peer % half
        unpacked = []
        for stat in (own_stat, got_stat):
            rest = jnp.zeros((LANES - stat.shape[0], LANES), jnp.float32)
            unpacked.append(jnp.concatenate([stat[...], rest], axis=0).T)
        for b in range(blocks_each):
            lanes = slice(b * LANES, (b + 1) * LANES)
            shares = []
            for i in range(each):
                picked = stat_lane * folds + stat_row == (j * blocks_each + b) * each + i
                mine, other = (
                    sum(kept_rows[g * span : g * span + audio_rows] for g in range(folds))
                    for kept_rows in (
                        jnp.sum(jnp.where(picked, wide, 0.0), axis=1, keepdims=True)
                        for wide in unpacked
                    )
                )
                peak = jnp.maximum(mine, other)
                mine = jnp.exp2(mine - peak)
                other = jnp.exp2(other - peak)
                total = mine + other
                shares.append((mine / total, other / total))
            own_share, got_share = (
                merge_lane_heads(
                    jnp.concatenate(
                        [jnp.broadcast_to(s[w], (audio_rows, LANES)) for s in shares], axis=0
                    ),
                    audio_rows,
                )
                for w in range(2)
            )
            merged = own_part[j, :, lanes] * own_share
            merged = merged + got_part[j, :, lanes].astype(jnp.float32) * got_share
            mixed_a[j, :, lanes] = merged.astype(jnp.bfloat16)

    await_landed(0)
    await_landed(1)
    audio_parts((1 - side) * half, far_part, far_stat)
    audio_parts(side * half, own_part, own_stat)

    def mix_video(h, source):
        mixed, peak, summed = softmax_mix(
            land[2, h, row(source), :], land[0, h], land[1, h], video_scaling
        )
        mixed_v[h, row(source), :] = mixed.astype(jnp.bfloat16)

    for copy in part_copies:
        copy.start()

    def gated(turn):
        return inner & (turn == 0)

    def delayed(turn):
        return (inner | (side == 1)) & (turn == 1)

    def send_held(condition):
        for earlier in range(video_each - 1):
            for i in range(2 * sub_count):

                @pl.when(condition(i // sub_count))
                def _():
                    outgoing(first + earlier, out_peer(i)).start()

    def merge_all():
        for copy in part_copies:
            copy.wait()
        merged = len(ways) - 1

        def one_merge(t, carry):
            merge_parts(peer_near(t))

            @pl.when(t < half - 1)
            def _():
                outgoing(merged, peer_near(t)).start()

            return carry

        lax.fori_loop(0, half, one_merge, 0)
        kept(merged).start()

    for h in range(video_each):
        await_landed(4 + h)
        last = h == video_each - 1
        if last:
            send_held(gated)

        order = last_peer if last else out_peer

        def one(t, carry, h=h, last=last, order=order):
            mix_video(h, order(t))
            now = t > 0
            if not last:
                turn = (t - 1) // sub_count
                now = now & jnp.logical_not(gated(turn) | delayed(turn))

            @pl.when(now)
            def _():
                outgoing(first + h, order(t - 1)).start()

            if last:

                @pl.when(t == sub_count)
                def _():
                    send_held(delayed)

                @pl.when(t == 2 * sub_count)
                def _():
                    merge_all()

            return carry

        lax.fori_loop(0, count, one, 0)
        kept(first + h).start()
    for i in range(len(sent)):
        await_sent(i)
    await_landed(2)
    await_landed(3)

    @pl.when(me < count - 1)
    def _():
        await_near(near_send.at[0])

    @pl.when(me > 0)
    def _():
        await_near(near_send.at[1])


def level_folds(levels, audio_rows):
    folds = 1
    while levels % (2 * folds) == 0 and levels > 8 * folds and LANES >= 2 * folds * audio_rows:
        folds = 2 * folds
    return folds


def store_kernel(*refs):
    copies = [pltpu.make_async_copy(refs[i], refs[3 + i], refs[6].at[i]) for i in range(3)]
    for copy in copies:
        copy.start()
    for copy in copies:
        copy.wait()


def exchanged_body(count, sub_count, *arrays):
    vid_q, vid_k, vid_v, aud_q, cross_k, cross_v, cross_q, aud_k, aud_v, windows = arrays
    rows = vid_q.shape[0]
    audio_rows = aud_q.shape[0]
    video_each = vid_q.shape[1] // HEAD_DIM // count
    halves = count // 2
    width = aud_q.shape[1] // halves
    levels = aud_q.shape[1] // AUDIO_DIM
    levels = -(-levels // level_folds(levels, audio_rows) // 8) * 8
    half = jnp.bfloat16
    place = pl.BlockSpec(memory_space=pl.ANY)
    held = pl.pallas_call(
        partial(exchange_kernel, count, sub_count),
        out_shape=tuple(pltpu.VMEM(a.shape, half) for a in (vid_q, aud_q, cross_q)),
        in_specs=[place] * 10,
        out_specs=(pl.BlockSpec(memory_space=pltpu.VMEM),) * 3,
        scratch_shapes=[
            pltpu.VMEM((3, video_each, count * rows, HEAD_DIM), half),
            pltpu.VMEM((count, audio_rows, width), half),
            pltpu.VMEM((2, halves * rows, width), half),
            pltpu.VMEM((video_each, count * rows, HEAD_DIM), half),
            pltpu.VMEM((halves, audio_rows, width), half),
            pltpu.VMEM((halves, audio_rows, width), jnp.float32),
            pltpu.VMEM((levels, LANES), jnp.float32),
            pltpu.VMEM((halves, audio_rows, width), half),
            pltpu.VMEM((levels, LANES), jnp.float32),
            pltpu.VMEM((halves, audio_rows, width), half),
            pltpu.VMEM((levels, LANES), jnp.float32),
            pltpu.VMEM((3, audio_rows, aud_k.shape[1]), half),
            pltpu.VMEM((3, audio_rows, aud_k.shape[1]), half),
            pltpu.VMEM(cross_q.shape, half),
            pltpu.VMEM(windows.shape, windows.dtype),
            pltpu.SemaphoreType.DMA((5,)),
            pltpu.SemaphoreType.DMA((4 + video_each,)),
            pltpu.SemaphoreType.DMA((2,)),
            pltpu.SemaphoreType.DMA((2,)),
            pltpu.SemaphoreType.DMA((2,)),
            pltpu.SemaphoreType.DMA((2,)),
            pltpu.SemaphoreType.DMA((4,)),
            pltpu.SemaphoreType.REGULAR((2,)),
            pltpu.SemaphoreType.REGULAR,
        ],
        compiler_params=pltpu.CompilerParams(collective_id=0, has_side_effects=True),
        name="joint_attention",
    )(*arrays)
    return pl.pallas_call(
        store_kernel,
        out_shape=tuple(jax.ShapeDtypeStruct(a.shape, half) for a in (vid_q, aud_q, cross_q)),
        in_specs=[pl.BlockSpec(memory_space=pltpu.VMEM)] * 3,
        out_specs=(place, place, place),
        scratch_shapes=[pltpu.SemaphoreType.DMA((3,))],
        name="store_results",
    )(*[pltpu.with_memory_space_constraint(x, pltpu.VMEM) for x in held])


def body(*arrays):
    sub_count = lax.axis_size("sub")
    count = lax.axis_size("seq") * sub_count
    video_heads = arrays[0].shape[1] // HEAD_DIM
    audio_heads = arrays[3].shape[1] // AUDIO_DIM
    halved = count == 4 * sub_count and max(audio_heads, arrays[3].shape[0]) <= LANES
    if halved and video_heads % count == 0 and audio_heads % count == 0:
        return exchanged_body(count, sub_count, *arrays)
    return gathered_body(*arrays)


def solution(mesh):
    return jax.shard_map(
        body,
        mesh=mesh,
        in_specs=(
            P(("grp", "seq", "sub"), "head"),
            P(("grp", "seq", "sub"), "head"),
            P(("grp", "seq", "sub"), "head"),
            P(("grp", "seq", "sub"), "head"),
            P(("grp", "seq", "sub"), "head"),
            P(("grp", "seq", "sub"), "head"),
            P(("grp", "seq", "sub"), "head"),
            P(("grp", "seq", "sub"), "head"),
            P(("grp", "seq", "sub"), "head"),
            P(None, "grp"),
        ),
        out_specs=(
            P(("grp", "seq", "sub"), "head"),
            P(("grp", "seq", "sub"), "head"),
            P(("grp", "seq", "sub"), "head"),
        ),
        check_vma=False,
    )
```

```python
from functools import partial
import math

import jax
import jax.numpy as jnp
from jax import lax
from jax.experimental import pallas as pl
from jax.experimental.pallas import tpu as pltpu
from jax.sharding import PartitionSpec as P

HEAD_DIM = 128
AUDIO_DIM = 64
TILE_LEN = 32
STRETCH_LEN = 8


def extended(cells, sides, width):
    for axis, dim in sides:
        count = lax.axis_size(axis)
        ends = count - 1
        head = lax.slice_in_dim(cells, 0, width, axis=dim)
        tail = lax.slice_in_dim(cells, cells.shape[dim] - width, cells.shape[dim], axis=dim)
        cells = jnp.concatenate(
            [
                lax.ppermute(tail, axis, [(i, (i + 1) % count) for i in range(ends)]),
                cells,
                lax.ppermute(head, axis, [((i + 1) % count, i) for i in range(ends)]),
            ],
            axis=dim,
        )
    return cells


def start_state(query_count, head_count, head_size):
    running = jnp.full((head_count, query_count), -jnp.inf, jnp.float32)
    summed = jnp.zeros((head_count, query_count), jnp.float32)
    numerator = jnp.zeros((head_count, query_count, head_size), jnp.float32)
    return (running, summed, numerator)


def absorb(state_in, queries, key_rows, value_rows, head_count, scaling, visible):
    running, summed, numerator = state_in
    query_count = queries.shape[0]
    key_count = key_rows.shape[0]
    head_size = queries.shape[1] // head_count
    scores = (
        jnp.einsum(
            "qhe,khe->hqk",
            queries.reshape(query_count, head_count, head_size),
            key_rows.reshape(key_count, head_count, head_size),
            preferred_element_type=jnp.float32,
        )
        * scaling
    )
    if visible is not None:
        scores = jnp.where(visible[None], scores, jnp.float32(-1e30))
    newest = jnp.maximum(running, jnp.max(scores, axis=2))
    shrink = jnp.exp(running - newest)
    weights = jnp.exp(scores - newest[:, :, None])
    summed = summed * shrink + jnp.sum(weights, axis=2)
    numerator = numerator * shrink[:, :, None] + jnp.einsum(
        "hqk,khe->hqe",
        weights.astype(jnp.bfloat16),
        value_rows.reshape(key_count, head_count, head_size),
        preferred_element_type=jnp.float32,
    )
    return (newest, summed, numerator)


def block_split(total_rows):
    block_rows = total_rows
    while block_rows > 512 and block_rows % 2 == 0:
        block_rows = block_rows // 2
    return (block_rows, total_rows // block_rows)


def fold_keys(state_in, shards_in, offset, queries, head_count, scaling):
    key_rows, value_rows = shards_in
    block_rows, block_count = block_split(key_rows.shape[0])
    key_blocks = key_rows.reshape(block_count, block_rows, key_rows.shape[1])
    value_blocks = value_rows.reshape(block_count, block_rows, value_rows.shape[1])

    def one_block(state, paired):
        return (absorb(state, queries, paired[0], paired[1], head_count, scaling, None), None)

    result, unused = lax.scan(one_block, state_in, (key_blocks, value_blocks))
    return result


def normalize_heads(state_in):
    running, summed, numerator = state_in
    mixed = numerator / summed[:, :, None]
    return mixed.transpose(1, 0, 2).reshape(mixed.shape[1], -1).astype(jnp.bfloat16)


def gathered_body(vid_q, vid_k, vid_v, aud_q, cross_k, cross_v, cross_q, aud_k, aud_v, windows):
    video_heads = vid_q.shape[1] // HEAD_DIM
    video_scaling = 1.0 / math.sqrt(HEAD_DIM)
    audio_heads = aud_q.shape[1] // AUDIO_DIM
    audio_scaling = 1.0 / math.sqrt(AUDIO_DIM)
    moved_q, moved_k, moved_v = (
        lax.all_to_all(vid_q, "sub", split_axis=1, concat_axis=0, tiled=True),
        lax.all_to_all(vid_k, "sub", split_axis=1, concat_axis=0, tiled=True),
        lax.all_to_all(vid_v, "sub", split_axis=1, concat_axis=0, tiled=True),
    )
    pair_heads = video_heads // lax.axis_size("sub")
    folder = partial(fold_keys, queries=moved_q, head_count=pair_heads, scaling=video_scaling)
    state = folder(
        start_state(moved_q.shape[0], pair_heads, HEAD_DIM),
        (
            lax.all_gather(moved_k, "seq", axis=0, tiled=True),
            lax.all_gather(moved_v, "seq", axis=0, tiled=True),
        ),
        jnp.int32(0),
    )
    video_self = lax.all_to_all(
        normalize_heads(state), "sub", split_axis=0, concat_axis=1, tiled=True
    )
    folder = partial(fold_keys, queries=aud_q, head_count=audio_heads, scaling=audio_scaling)
    state = folder(
        start_state(aud_q.shape[0], audio_heads, AUDIO_DIM),
        (
            lax.all_gather(cross_k, ("seq", "sub"), axis=0, tiled=True),
            lax.all_gather(cross_v, ("seq", "sub"), axis=0, tiled=True),
        ),
        jnp.int32(0),
    )
    audio_out = normalize_heads(state)
    audio_rows = aud_k.shape[0]
    key_width = aud_k.shape[1]
    padded_rows = extended(
        jnp.concatenate((aud_k, aud_v), axis=1), ((("seq", "sub"), 0),), audio_rows
    )
    near_keys = padded_rows[:, :key_width]
    near_values = padded_rows[:, key_width:]
    position = lax.axis_index(("seq", "sub"))
    audio_index = (position - 1) * audio_rows + jnp.arange(padded_rows.shape[0], dtype=jnp.int32)
    stretch_index = audio_index // STRETCH_LEN
    stretch_ids = jnp.arange(windows.shape[1], dtype=jnp.int32)
    onehot = stretch_index[:, None] == stretch_ids[None, :]
    first_tile = jnp.sum(jnp.where(onehot, windows[0][None, :], 0), axis=1)
    after_tile = jnp.sum(jnp.where(onehot, windows[1][None, :], 0), axis=1)
    video_rows = cross_q.shape[0]
    video_tile = (position * video_rows + jnp.arange(video_rows, dtype=jnp.int32)) // TILE_LEN
    visible = (first_tile[None, :] <= video_tile[:, None]) & (
        video_tile[:, None] < after_tile[None, :]
    )
    state = absorb(
        start_state(video_rows, audio_heads, AUDIO_DIM),
        cross_q,
        near_keys,
        near_values,
        audio_heads,
        audio_scaling,
        visible,
    )
    video_cross = normalize_heads(state)
    return (video_self, audio_out, video_cross)


LANES = 128
AXES = ("seq", "sub")


def softmax_mix(queries, key_rows, value_rows, scaling):
    scores = lax.dot_general(
        queries, key_rows, (((1,), (1,)), ((), ())), preferred_element_type=jnp.float32
    )
    peak = jnp.max(scores, axis=1, keepdims=True)
    weights = jnp.exp2((scores - peak) * jnp.float32(scaling * math.log2(math.e)))
    summed = jnp.sum(weights, axis=1, keepdims=True)
    mixed = jnp.dot(
        weights.astype(jnp.bfloat16), value_rows, preferred_element_type=jnp.float32
    )
    return mixed / summed, peak, summed


def lane_heads(block):
    wide = block.astype(jnp.float32)
    lane = lax.broadcasted_iota(jnp.int32, wide.shape, 1) // AUDIO_DIM
    parts = [jnp.where(lane == i, wide, 0.0) for i in range(LANES // AUDIO_DIM)]
    return jnp.concatenate(parts, axis=0).astype(jnp.bfloat16)


def merge_lane_heads(stacked, rows):
    lane = lax.broadcasted_iota(jnp.int32, (rows, LANES), 1) // AUDIO_DIM
    merged = stacked[:rows]
    for i in range(1, LANES // AUDIO_DIM):
        merged = jnp.where(lane == i, stacked[i * rows : (i + 1) * rows], merged)
    return merged


def exchange_kernel(
    count,
    sub_count,
    vid_q,
    vid_k,
    vid_v,
    aud_q,
    cross_k,
    cross_v,
    cross_q,
    aud_k,
    aud_v,
    windows,
    video_self,
    audio_out,
    video_cross,
    land,
    land_aq,
    land_c,
    mixed_v,
    mixed_a,
    own_part,
    own_stat,
    far_part,
    far_stat,
    got_part,
    got_stat,
    near_k,
    near_v,
    local_cq,
    local_windows,
    send_sem,
    recv_sem,
    near_send,
    near_recv,
    part_send,
    part_recv,
    local_sem,
    ready_sem,
    all_sem,
    pair_sem,
):
    rows = vid_q.shape[0]
    audio_rows = aud_q.shape[0]
    video_each = vid_q.shape[1] // HEAD_DIM // count
    half = count // 2
    blocks_each = aud_q.shape[1] // LANES // half
    width = blocks_each * LANES
    video_scaling = 1.0 / math.sqrt(HEAD_DIM)
    audio_scaling = 1.0 / math.sqrt(AUDIO_DIM)
    me = lax.axis_index("seq") * sub_count + lax.axis_index("sub")

    side = me // half
    place = me % half

    def device(peer):
        return {"seq": peer // sub_count, "sub": peer % sub_count}

    def peer_near(t):
        return side * half + (place + 1 + t) % half

    chip = me // sub_count
    core = me % sub_count
    inner = (me >= half - sub_count) & (me < half + sub_count)
    outer = jnp.logical_not(inner)

    def inner_of(which, t):
        return half - (1 - which) * sub_count + (core + t) % sub_count

    def outer_of(which, t):
        return which * (half + sub_count) + (core + t) % sub_count

    def core_peer(t):
        return chip * sub_count + (core + 1 + t) % sub_count

    def near_inner(t):
        return inner_of(side, t)

    def near_outer(t):
        return outer_of(side, t)

    def far_inner(t):
        return inner_of(1 - side, t)

    def far_inner_rest(t):
        return inner_of(1 - side, t + 1)

    def far_outer(t):
        return outer_of(1 - side, t)

    def last_peer(t):
        turn = t // sub_count
        kind = turn
        for i, k in enumerate((0, 1, 2)):
            kind = jnp.where(outer & (turn == i), k, kind)
        return out_peer(kind * sub_count + t % sub_count)

    def out_peer(t):
        turn = t // sub_count
        chips = count // sub_count
        there = jnp.where(turn == side, chips // 2 - side, chip)
        there = jnp.where(turn == 1 - side, (1 - side) * (chips - 1), there)
        there = jnp.where(turn == 2, 2 * (chip // 2) + 1 - chip % 2, there)
        shift = t + turn // (chips - 1)
        return there * sub_count + (core + shift) % sub_count

    def signal(semaphore, peer):
        pl.semaphore_signal(
            semaphore, inc=1, device_id=device(peer), device_id_type=pl.DeviceIdType.MESH
        )

    barrier = pltpu.get_barrier_semaphore()

    @pl.when(inner)
    def _():
        signal(barrier, far_inner(0))

    @pl.when(outer)
    def _():
        for t in range(sub_count - 1):
            signal(barrier, core_peer(t))

    own = [
        pltpu.make_async_copy(cross_q, local_cq, local_sem.at[0]),
        pltpu.make_async_copy(aud_k, near_k.at[1], local_sem.at[1]),
        pltpu.make_async_copy(aud_v, near_v.at[1], local_sem.at[2]),
        pltpu.make_async_copy(windows, local_windows, local_sem.at[3]),
    ]
    for copy in own:
        copy.start()

    def column(index):
        return pl.ds(pl.multiple_of(index * LANES, LANES), LANES)

    def row(index):
        return pl.ds(pl.multiple_of(index * rows, rows), rows)

    def columns(index):
        return pl.ds(pl.multiple_of(index * width, LANES), width)

    def video_way(array, which, h):
        return (
            lambda peer: array.at[:, column(peer * video_each + h)],
            lambda source: land.at[which, h, row(source), :],
            2,
            4 + h,
        )

    def half_way(array, which):
        return (
            lambda peer: array.at[:, columns(peer % half)],
            lambda source: land_c.at[which, row(source % half), :],
            1,
            1,
        )

    ways = [
        (
            lambda peer: aud_q.at[:, columns(peer % half)],
            lambda source: land_aq.at[source],
            0,
            0,
        )
    ]
    audio_ways = [0]
    video_ways = []
    for h in range(video_each):
        video_ways.append(list(range(len(ways), len(ways) + 3)))
        for which, array in enumerate((vid_k, vid_v, vid_q)):
            ways.append(video_way(array, which, h))
        if h == 0:
            for which, array in enumerate((cross_k, cross_v)):
                audio_ways.append(len(ways))
                ways.append(half_way(array, which))
    first = len(ways)
    early = audio_ways[:1] + video_ways[0]
    late = [k for kinds in video_ways[1:] for k in kinds]
    for h in range(video_each):
        ways.append(
            (
                lambda peer, h=h: mixed_v.at[h, row(peer), :],
                lambda source, h=h: video_self.at[:, column(source * video_each + h)],
                3,
                2,
            )
        )
    ways.append(
        (
            lambda peer: mixed_a.at[peer % half],
            lambda source: audio_out.at[:, columns(source % half)],
            4,
            3,
        )
    )
    sent = (
        land_aq.at[pl.ds(0, count - 1)],
        land_c.at[:, pl.ds(0, (half - 1) * rows), :],
        land.at[:, :, pl.ds(0, (count - 1) * rows), :],
        mixed_v.at[:, pl.ds(0, (count - 1) * rows), :],
        mixed_a.at[pl.ds(0, half - 1)],
    )
    landed = [land_aq, land_c, video_self, audio_out]
    landed += [land.at[:, h] for h in range(video_each)]

    def outgoing(k, peer):
        return pltpu.make_async_remote_copy(
            src_ref=ways[k][0](peer),
            dst_ref=ways[k][1](me),
            send_sem=send_sem.at[ways[k][2]],
            recv_sem=recv_sem.at[ways[k][3]],
            device_id=device(peer),
            device_id_type=pl.DeviceIdType.MESH,
        )

    def kept(k):
        return pltpu.make_async_copy(ways[k][0](me), ways[k][1](me), recv_sem.at[ways[k][3]])

    def await_landed(i):
        pltpu.make_async_copy(landed[i], landed[i], recv_sem.at[i]).wait()

    def await_sent(i):
        pltpu.make_async_copy(sent[i], sent[i], send_sem.at[i]).wait()

    def near_copy(array, near, slot, peer):
        return pltpu.make_async_remote_copy(
            src_ref=array,
            dst_ref=near.at[slot],
            send_sem=near_send.at[slot // 2],
            recv_sem=near_recv.at[slot // 2],
            device_id=device(peer),
            device_id_type=pl.DeviceIdType.MESH,
        )

    near_pairs = ((aud_k, near_k), (aud_v, near_v))

    def send_right():
        for array, near in near_pairs:
            near_copy(array, near, 0, me + 1).start()

    def send_left():
        for array, near in near_pairs:
            near_copy(array, near, 2, me - 1).start()

    def await_near(semaphore):
        both = near_k.at[pl.ds(0, 2)]
        pltpu.make_async_copy(both, both, semaphore).wait()

    def send(k, peer_of, steps):
        def one(t, carry):
            outgoing(k, peer_of(t)).start()
            return carry

        lax.fori_loop(0, steps, one, 0)

    pair = sub_count - 1
    audio_only = audio_ways[1:]

    def send_keep(ks):
        for k in ks:
            send(k, core_peer, pair)
            kept(k).start()

    @pl.when(inner)
    def _():
        leads = core == sub_count - 1
        pl.semaphore_wait(barrier, jnp.where(leads, 1, 2))

        @pl.when(leads)
        def _():
            signal(barrier, core_peer(0))

        @pl.when(jnp.logical_not(leads))
        def _():
            signal(pair_sem, core_peer(0))

        for k in early:
            send(k, far_inner, 1)
        for t in range(sub_count):
            signal(barrier, near_outer(t))

        @pl.when(leads)
        def _():
            pl.semaphore_wait(pair_sem, 1)

        for k in early:
            send(k, far_inner_rest, sub_count - 1)

        @pl.when(side == 0)
        def _():
            send_right()

            @pl.when(core > 0)
            def _():
                send_left()

        @pl.when(side == 1)
        def _():
            send_left()

            @pl.when(core < sub_count - 1)
            def _():
                send_right()

        send_keep(early[:1] + audio_only)
        pl.semaphore_wait(ready_sem.at[side], sub_count)

        @pl.when((side == 0) & (core == 0))
        def _():
            send_left()

        @pl.when((side == 1) & (core == sub_count - 1))
        def _():
            send_right()

        for k in early[:1] + audio_only + early[1:] + late:
            send(k, near_outer, sub_count)
        pl.semaphore_wait(ready_sem.at[1 - side], sub_count)
        signal(all_sem, near_outer(0))
        for k in early:
            send(k, far_outer, sub_count)
        for k in late:
            send(k, far_inner, sub_count)
        for k in late:
            send(k, far_outer, sub_count)
        send_keep(early[1:] + late)

    @pl.when(outer)
    def _():
        pl.semaphore_wait(barrier, 2 * sub_count - 1)
        for t in range(sub_count):
            signal(ready_sem.at[side], near_inner(t))
            signal(ready_sem.at[side], far_inner(t))

        for k in early[:1]:
            send(k, far_inner, sub_count)

        @pl.when(me < count - 1)
        def _():
            send_right()

        @pl.when(me > 0)
        def _():
            send_left()

        for k in early[:1] + audio_only:
            send(k, near_inner, sub_count)
        send_keep(early[:1] + audio_only)
        pl.semaphore_wait(all_sem, 1)
        for k in early[:1]:
            send(k, far_outer, sub_count)
        for k in early[1:] + late:
            send(k, near_inner, sub_count)
        for ks in (early[1:], late):
            for k in ks:
                send(k, far_outer, sub_count)
            for k in ks:
                send(k, far_inner, sub_count)
        send_keep(early[1:] + late)

    @pl.when(me == 0)
    def _():
        for array, near in near_pairs:
            near[0] = jnp.zeros(near.shape[1:], near.dtype)

    @pl.when(me == count - 1)
    def _():
        for array, near in near_pairs:
            near[2] = jnp.zeros(near.shape[1:], near.dtype)

    for copy in own:
        copy.wait()

    @pl.when(me > 0)
    def _():
        await_near(near_recv.at[0])

    @pl.when(me < count - 1)
    def _():
        await_near(near_recv.at[1])

    spans = windows.shape[1]
    tile = (me * rows + lax.broadcasted_iota(jnp.int32, (rows, spans), 0)) // TILE_LEN
    bounds = local_windows[...]
    inside = (bounds[0:1, :] <= tile) & (tile < bounds[1:2, :])
    inside = jnp.where(inside, 1.0, 0.0).astype(jnp.bfloat16)
    seen = []
    for slot in range(3):
        stretch = lax.broadcasted_iota(jnp.int32, (spans, audio_rows), 1) // STRETCH_LEN
        stretch = stretch + (me + slot - 1) * (audio_rows // STRETCH_LEN)
        picks = stretch == lax.broadcasted_iota(jnp.int32, (spans, audio_rows), 0)
        picks = jnp.where(picks, 1.0, 0.0).astype(jnp.bfloat16)
        part = jnp.dot(inside, picks, preferred_element_type=jnp.float32)
        seen.append(jnp.concatenate([part] * (LANES // AUDIO_DIM), axis=0))

    for b in range(cross_q.shape[1] // LANES):
        lanes = slice(b * LANES, (b + 1) * LANES)
        stacked = lane_heads(local_cq[:, lanes])
        scores = []
        for slot in range(3):
            part = lax.dot_general(
                stacked,
                near_k[slot, :, lanes],
                (((1,), (1,)), ((), ())),
                preferred_element_type=jnp.float32,
            )
            scores.append(jnp.where(seen[slot] > 0.5, part, jnp.float32(-1e30)))
        peak = jnp.max(jnp.maximum(jnp.maximum(scores[0], scores[1]), scores[2]), axis=1, keepdims=True)
        factor = jnp.float32(audio_scaling * math.log2(math.e))
        weights = [jnp.exp2((part - peak) * factor) for part in scores]
        summed = jnp.sum(weights[0] + weights[1] + weights[2], axis=1, keepdims=True)
        mixed = sum(
            jnp.dot(
                weights[slot].astype(jnp.bfloat16),
                near_v[slot, :, lanes],
                preferred_element_type=jnp.float32,
            )
            for slot in range(3)
        )
        video_cross[:, lanes] = merge_lane_heads(mixed / summed, rows).astype(jnp.bfloat16)

    def part_copy(j, array, land):
        return pltpu.make_async_remote_copy(
            src_ref=array,
            dst_ref=land,
            send_sem=part_send.at[j],
            recv_sem=part_recv.at[j],
            device_id=device((me + half) % count),
            device_id_type=pl.DeviceIdType.MESH,
        )

    part_copies = [part_copy(0, far_part, got_part), part_copy(1, far_stat, got_stat)]
    each = LANES // AUDIO_DIM
    levels = half * blocks_each * each
    folds = level_folds(levels, audio_rows)
    span = LANES // folds
    stat_row = lax.broadcasted_iota(jnp.int32, (LANES, LANES), 0) // span
    stat_lane = lax.broadcasted_iota(jnp.int32, (LANES, LANES), 1)

    def audio_parts(first_source, part, stat):
        def one(j, stats):
            queries = land_aq[first_source + j]
            for b in range(blocks_each):
                lanes = slice(b * LANES, (b + 1) * LANES)
                mixed, peak, summed = softmax_mix(
                    lane_heads(queries[:, lanes]), land_c[0, :, lanes], land_c[1, :, lanes], audio_scaling
                )
                part[j, :, lanes] = merge_lane_heads(mixed, audio_rows).astype(part.dtype)
                level = peak * jnp.float32(audio_scaling * math.log2(math.e)) + jnp.log2(summed)
                rest = jnp.zeros((span - audio_rows, 1), jnp.float32)
                for i in range(each):
                    index = (j * blocks_each + b) * each + i
                    picked = stat_lane * folds + stat_row == index
                    held = level[i * audio_rows : (i + 1) * audio_rows]
                    stats = jnp.where(picked, jnp.concatenate([held, rest] * folds, axis=0), stats)
            return stats

        stats = lax.fori_loop(0, half, one, jnp.zeros((LANES, LANES), jnp.float32))
        stat[...] = stats.T[: stat.shape[0]]

    def merge_parts(peer):
        j = peer % half
        unpacked = []
        for stat in (own_stat, got_stat):
            rest = jnp.zeros((LANES - stat.shape[0], LANES), jnp.float32)
            unpacked.append(jnp.concatenate([stat[...], rest], axis=0).T)
        for b in range(blocks_each):
            lanes = slice(b * LANES, (b + 1) * LANES)
            shares = []
            for i in range(each):
                picked = stat_lane * folds + stat_row == (j * blocks_each + b) * each + i
                mine, other = (
                    sum(kept_rows[g * span : g * span + audio_rows] for g in range(folds))
                    for kept_rows in (
                        jnp.sum(jnp.where(picked, wide, 0.0), axis=1, keepdims=True)
                        for wide in unpacked
                    )
                )
                peak = jnp.maximum(mine, other)
                mine = jnp.exp2(mine - peak)
                other = jnp.exp2(other - peak)
                total = mine + other
                shares.append((mine / total, other / total))
            own_share, got_share = (
                merge_lane_heads(
                    jnp.concatenate(
                        [jnp.broadcast_to(s[w], (audio_rows, LANES)) for s in shares], axis=0
                    ),
                    audio_rows,
                )
                for w in range(2)
            )
            merged = own_part[j, :, lanes] * own_share
            merged = merged + got_part[j, :, lanes].astype(jnp.float32) * got_share
            mixed_a[j, :, lanes] = merged.astype(jnp.bfloat16)

    await_landed(0)
    await_landed(1)
    audio_parts((1 - side) * half, far_part, far_stat)
    audio_parts(side * half, own_part, own_stat)

    def mix_video(h, source):
        mixed, peak, summed = softmax_mix(
            land[2, h, row(source), :], land[0, h], land[1, h], video_scaling
        )
        mixed_v[h, row(source), :] = mixed.astype(jnp.bfloat16)

    for copy in part_copies:
        copy.start()

    def gated(turn):
        return inner & (turn == 0)

    def delayed(turn):
        return (inner | (side == 1)) & (turn == 1)

    def send_held(condition):
        for earlier in range(video_each - 1):
            for i in range(2 * sub_count):

                @pl.when(condition(i // sub_count))
                def _():
                    outgoing(first + earlier, out_peer(i)).start()

    def merge_all():
        for copy in part_copies:
            copy.wait()
        merged = len(ways) - 1

        def one_merge(t, carry):
            merge_parts(peer_near(t))

            @pl.when(t < half - 1)
            def _():
                outgoing(merged, peer_near(t)).start()

            return carry

        lax.fori_loop(0, half, one_merge, 0)
        kept(merged).start()

    for h in range(video_each):
        await_landed(4 + h)
        last = h == video_each - 1
        if last:
            send_held(gated)

        order = last_peer if last else out_peer

        def one(t, carry, h=h, last=last, order=order):
            mix_video(h, order(t))
            now = t > 0
            if not last:
                turn = (t - 1) // sub_count
                now = now & jnp.logical_not(gated(turn) | delayed(turn))

            @pl.when(now)
            def _():
                outgoing(first + h, order(t - 1)).start()

            if last:

                @pl.when(t == sub_count)
                def _():
                    send_held(delayed)

                @pl.when(t == 2 * sub_count)
                def _():
                    merge_all()

            return carry

        lax.fori_loop(0, count, one, 0)
        kept(first + h).start()
    for i in range(len(sent)):
        await_sent(i)
    await_landed(2)
    await_landed(3)

    @pl.when(me < count - 1)
    def _():
        await_near(near_send.at[0])

    @pl.when(me > 0)
    def _():
        await_near(near_send.at[1])


def level_folds(levels, audio_rows):
    folds = 1
    while levels % (2 * folds) == 0 and levels > 8 * folds and LANES >= 2 * folds * audio_rows:
        folds = 2 * folds
    return folds


def store_kernel(*refs):
    copies = [pltpu.make_async_copy(refs[i], refs[3 + i], refs[6].at[i]) for i in range(3)]
    for copy in copies:
        copy.start()
    for copy in copies:
        copy.wait()


def exchanged_body(count, sub_count, *arrays):
    vid_q, vid_k, vid_v, aud_q, cross_k, cross_v, cross_q, aud_k, aud_v, windows = arrays
    rows = vid_q.shape[0]
    audio_rows = aud_q.shape[0]
    video_each = vid_q.shape[1] // HEAD_DIM // count
    halves = count // 2
    width = aud_q.shape[1] // halves
    levels = aud_q.shape[1] // AUDIO_DIM
    levels = -(-levels // level_folds(levels, audio_rows) // 8) * 8
    half = jnp.bfloat16
    place = pl.BlockSpec(memory_space=pl.ANY)
    held = pl.pallas_call(
        partial(exchange_kernel, count, sub_count),
        out_shape=tuple(pltpu.VMEM(a.shape, half) for a in (vid_q, aud_q, cross_q)),
        in_specs=[place] * 10,
        out_specs=(pl.BlockSpec(memory_space=pltpu.VMEM),) * 3,
        scratch_shapes=[
            pltpu.VMEM((3, video_each, count * rows, HEAD_DIM), half),
            pltpu.VMEM((count, audio_rows, width), half),
            pltpu.VMEM((2, halves * rows, width), half),
            pltpu.VMEM((video_each, count * rows, HEAD_DIM), half),
            pltpu.VMEM((halves, audio_rows, width), half),
            pltpu.VMEM((halves, audio_rows, width), jnp.float32),
            pltpu.VMEM((levels, LANES), jnp.float32),
            pltpu.VMEM((halves, audio_rows, width), half),
            pltpu.VMEM((levels, LANES), jnp.float32),
            pltpu.VMEM((halves, audio_rows, width), half),
            pltpu.VMEM((levels, LANES), jnp.float32),
            pltpu.VMEM((3, audio_rows, aud_k.shape[1]), half),
            pltpu.VMEM((3, audio_rows, aud_k.shape[1]), half),
            pltpu.VMEM(cross_q.shape, half),
            pltpu.VMEM(windows.shape, windows.dtype),
            pltpu.SemaphoreType.DMA((5,)),
            pltpu.SemaphoreType.DMA((4 + video_each,)),
            pltpu.SemaphoreType.DMA((2,)),
            pltpu.SemaphoreType.DMA((2,)),
            pltpu.SemaphoreType.DMA((2,)),
            pltpu.SemaphoreType.DMA((2,)),
            pltpu.SemaphoreType.DMA((4,)),
            pltpu.SemaphoreType.REGULAR((2,)),
            pltpu.SemaphoreType.REGULAR,
            pltpu.SemaphoreType.REGULAR,
        ],
        compiler_params=pltpu.CompilerParams(collective_id=0, has_side_effects=True),
        name="joint_attention",
    )(*arrays)
    return pl.pallas_call(
        store_kernel,
        out_shape=tuple(jax.ShapeDtypeStruct(a.shape, half) for a in (vid_q, aud_q, cross_q)),
        in_specs=[pl.BlockSpec(memory_space=pltpu.VMEM)] * 3,
        out_specs=(place, place, place),
        scratch_shapes=[pltpu.SemaphoreType.DMA((3,))],
        name="store_results",
    )(*[pltpu.with_memory_space_constraint(x, pltpu.VMEM) for x in held])


def body(*arrays):
    sub_count = lax.axis_size("sub")
    count = lax.axis_size("seq") * sub_count
    video_heads = arrays[0].shape[1] // HEAD_DIM
    audio_heads = arrays[3].shape[1] // AUDIO_DIM
    halved = sub_count == 2 and count == 4 * sub_count and max(audio_heads, arrays[3].shape[0]) <= LANES
    if halved and video_heads % count == 0 and audio_heads % count == 0:
        return exchanged_body(count, sub_count, *arrays)
    return gathered_body(*arrays)


def solution(mesh):
    return jax.shard_map(
        body,
        mesh=mesh,
        in_specs=(
            P(("grp", "seq", "sub"), "head"),
            P(("grp", "seq", "sub"), "head"),
            P(("grp", "seq", "sub"), "head"),
            P(("grp", "seq", "sub"), "head"),
            P(("grp", "seq", "sub"), "head"),
            P(("grp", "seq", "sub"), "head"),
            P(("grp", "seq", "sub"), "head"),
            P(("grp", "seq", "sub"), "head"),
            P(("grp", "seq", "sub"), "head"),
            P(None, "grp"),
        ),
        out_specs=(
            P(("grp", "seq", "sub"), "head"),
            P(("grp", "seq", "sub"), "head"),
            P(("grp", "seq", "sub"), "head"),
        ),
        check_vma=False,
    )
```

```python
from functools import partial
import math

import jax
import jax.numpy as jnp
from jax import lax
from jax.experimental import pallas as pl
from jax.experimental.pallas import tpu as pltpu
from jax.sharding import PartitionSpec as P

HEAD_DIM = 128
AUDIO_DIM = 64
TILE_LEN = 32
STRETCH_LEN = 8


def extended(cells, sides, width):
    for axis, dim in sides:
        count = lax.axis_size(axis)
        ends = count - 1
        head = lax.slice_in_dim(cells, 0, width, axis=dim)
        tail = lax.slice_in_dim(cells, cells.shape[dim] - width, cells.shape[dim], axis=dim)
        cells = jnp.concatenate(
            [
                lax.ppermute(tail, axis, [(i, (i + 1) % count) for i in range(ends)]),
                cells,
                lax.ppermute(head, axis, [((i + 1) % count, i) for i in range(ends)]),
            ],
            axis=dim,
        )
    return cells


def start_state(query_count, head_count, head_size):
    running = jnp.full((head_count, query_count), -jnp.inf, jnp.float32)
    summed = jnp.zeros((head_count, query_count), jnp.float32)
    numerator = jnp.zeros((head_count, query_count, head_size), jnp.float32)
    return (running, summed, numerator)


def absorb(state_in, queries, key_rows, value_rows, head_count, scaling, visible):
    running, summed, numerator = state_in
    query_count = queries.shape[0]
    key_count = key_rows.shape[0]
    head_size = queries.shape[1] // head_count
    scores = (
        jnp.einsum(
            "qhe,khe->hqk",
            queries.reshape(query_count, head_count, head_size),
            key_rows.reshape(key_count, head_count, head_size),
            preferred_element_type=jnp.float32,
        )
        * scaling
    )
    if visible is not None:
        scores = jnp.where(visible[None], scores, jnp.float32(-1e30))
    newest = jnp.maximum(running, jnp.max(scores, axis=2))
    shrink = jnp.exp(running - newest)
    weights = jnp.exp(scores - newest[:, :, None])
    summed = summed * shrink + jnp.sum(weights, axis=2)
    numerator = numerator * shrink[:, :, None] + jnp.einsum(
        "hqk,khe->hqe",
        weights.astype(jnp.bfloat16),
        value_rows.reshape(key_count, head_count, head_size),
        preferred_element_type=jnp.float32,
    )
    return (newest, summed, numerator)


def block_split(total_rows):
    block_rows = total_rows
    while block_rows > 512 and block_rows % 2 == 0:
        block_rows = block_rows // 2
    return (block_rows, total_rows // block_rows)


def fold_keys(state_in, shards_in, offset, queries, head_count, scaling):
    key_rows, value_rows = shards_in
    block_rows, block_count = block_split(key_rows.shape[0])
    key_blocks = key_rows.reshape(block_count, block_rows, key_rows.shape[1])
    value_blocks = value_rows.reshape(block_count, block_rows, value_rows.shape[1])

    def one_block(state, paired):
        return (absorb(state, queries, paired[0], paired[1], head_count, scaling, None), None)

    result, unused = lax.scan(one_block, state_in, (key_blocks, value_blocks))
    return result


def normalize_heads(state_in):
    running, summed, numerator = state_in
    mixed = numerator / summed[:, :, None]
    return mixed.transpose(1, 0, 2).reshape(mixed.shape[1], -1).astype(jnp.bfloat16)


def gathered_body(vid_q, vid_k, vid_v, aud_q, cross_k, cross_v, cross_q, aud_k, aud_v, windows):
    video_heads = vid_q.shape[1] // HEAD_DIM
    video_scaling = 1.0 / math.sqrt(HEAD_DIM)
    audio_heads = aud_q.shape[1] // AUDIO_DIM
    audio_scaling = 1.0 / math.sqrt(AUDIO_DIM)
    moved_q, moved_k, moved_v = (
        lax.all_to_all(vid_q, "sub", split_axis=1, concat_axis=0, tiled=True),
        lax.all_to_all(vid_k, "sub", split_axis=1, concat_axis=0, tiled=True),
        lax.all_to_all(vid_v, "sub", split_axis=1, concat_axis=0, tiled=True),
    )
    pair_heads = video_heads // lax.axis_size("sub")
    folder = partial(fold_keys, queries=moved_q, head_count=pair_heads, scaling=video_scaling)
    state = folder(
        start_state(moved_q.shape[0], pair_heads, HEAD_DIM),
        (
            lax.all_gather(moved_k, "seq", axis=0, tiled=True),
            lax.all_gather(moved_v, "seq", axis=0, tiled=True),
        ),
        jnp.int32(0),
    )
    video_self = lax.all_to_all(
        normalize_heads(state), "sub", split_axis=0, concat_axis=1, tiled=True
    )
    folder = partial(fold_keys, queries=aud_q, head_count=audio_heads, scaling=audio_scaling)
    state = folder(
        start_state(aud_q.shape[0], audio_heads, AUDIO_DIM),
        (
            lax.all_gather(cross_k, ("seq", "sub"), axis=0, tiled=True),
            lax.all_gather(cross_v, ("seq", "sub"), axis=0, tiled=True),
        ),
        jnp.int32(0),
    )
    audio_out = normalize_heads(state)
    audio_rows = aud_k.shape[0]
    key_width = aud_k.shape[1]
    padded_rows = extended(
        jnp.concatenate((aud_k, aud_v), axis=1), ((("seq", "sub"), 0),), audio_rows
    )
    near_keys = padded_rows[:, :key_width]
    near_values = padded_rows[:, key_width:]
    position = lax.axis_index(("seq", "sub"))
    audio_index = (position - 1) * audio_rows + jnp.arange(padded_rows.shape[0], dtype=jnp.int32)
    stretch_index = audio_index // STRETCH_LEN
    stretch_ids = jnp.arange(windows.shape[1], dtype=jnp.int32)
    onehot = stretch_index[:, None] == stretch_ids[None, :]
    first_tile = jnp.sum(jnp.where(onehot, windows[0][None, :], 0), axis=1)
    after_tile = jnp.sum(jnp.where(onehot, windows[1][None, :], 0), axis=1)
    video_rows = cross_q.shape[0]
    video_tile = (position * video_rows + jnp.arange(video_rows, dtype=jnp.int32)) // TILE_LEN
    visible = (first_tile[None, :] <= video_tile[:, None]) & (
        video_tile[:, None] < after_tile[None, :]
    )
    state = absorb(
        start_state(video_rows, audio_heads, AUDIO_DIM),
        cross_q,
        near_keys,
        near_values,
        audio_heads,
        audio_scaling,
        visible,
    )
    video_cross = normalize_heads(state)
    return (video_self, audio_out, video_cross)


LANES = 128
AXES = ("seq", "sub")


def softmax_mix(queries, key_rows, value_rows, scaling):
    scores = lax.dot_general(
        queries, key_rows, (((1,), (1,)), ((), ())), preferred_element_type=jnp.float32
    )
    peak = jnp.max(scores, axis=1, keepdims=True)
    weights = jnp.exp2((scores - peak) * jnp.float32(scaling * math.log2(math.e)))
    summed = jnp.sum(weights, axis=1, keepdims=True)
    mixed = jnp.dot(
        weights.astype(jnp.bfloat16), value_rows, preferred_element_type=jnp.float32
    )
    return mixed / summed, peak, summed


def lane_heads(block):
    wide = block.astype(jnp.float32)
    lane = lax.broadcasted_iota(jnp.int32, wide.shape, 1) // AUDIO_DIM
    parts = [jnp.where(lane == i, wide, 0.0) for i in range(LANES // AUDIO_DIM)]
    return jnp.concatenate(parts, axis=0).astype(jnp.bfloat16)


def merge_lane_heads(stacked, rows):
    lane = lax.broadcasted_iota(jnp.int32, (rows, LANES), 1) // AUDIO_DIM
    merged = stacked[:rows]
    for i in range(1, LANES // AUDIO_DIM):
        merged = jnp.where(lane == i, stacked[i * rows : (i + 1) * rows], merged)
    return merged


def exchange_kernel(
    count,
    sub_count,
    vid_q,
    vid_k,
    vid_v,
    aud_q,
    cross_k,
    cross_v,
    cross_q,
    aud_k,
    aud_v,
    windows,
    video_self,
    audio_out,
    video_cross,
    land,
    land_aq,
    land_c,
    mixed_v,
    mixed_a,
    own_part,
    own_stat,
    far_part,
    far_stat,
    got_part,
    got_stat,
    near_k,
    near_v,
    local_cq,
    local_windows,
    send_sem,
    recv_sem,
    near_send,
    near_recv,
    part_send,
    part_recv,
    local_sem,
    ready_sem,
    all_sem,
    pair_sem,
):
    rows = vid_q.shape[0]
    audio_rows = aud_q.shape[0]
    video_each = vid_q.shape[1] // HEAD_DIM // count
    half = count // 2
    blocks_each = aud_q.shape[1] // LANES // half
    width = blocks_each * LANES
    video_scaling = 1.0 / math.sqrt(HEAD_DIM)
    audio_scaling = 1.0 / math.sqrt(AUDIO_DIM)
    me = lax.axis_index("seq") * sub_count + lax.axis_index("sub")

    side = me // half
    place = me % half

    def device(peer):
        return {"seq": peer // sub_count, "sub": peer % sub_count}

    def peer_near(t):
        return side * half + (place + 1 + t) % half

    chip = me // sub_count
    core = me % sub_count
    inner = (me >= half - sub_count) & (me < half + sub_count)
    outer = jnp.logical_not(inner)

    def inner_of(which, t):
        return half - (1 - which) * sub_count + (core + t) % sub_count

    def outer_of(which, t):
        return which * (half + sub_count) + (core + t) % sub_count

    def core_peer(t):
        return chip * sub_count + (core + 1 + t) % sub_count

    def near_inner(t):
        return inner_of(side, t)

    def near_outer(t):
        return outer_of(side, t)

    def far_inner(t):
        return inner_of(1 - side, t)

    def far_inner_rest(t):
        return inner_of(1 - side, t + 1)

    def far_outer(t):
        return outer_of(1 - side, t)

    def last_peer(t):
        turn = t // sub_count
        kind = turn
        for i, k in enumerate((0, 1, 2)):
            kind = jnp.where(outer & (turn == i), k, kind)
        return out_peer(kind * sub_count + t % sub_count)

    def out_peer(t):
        turn = t // sub_count
        chips = count // sub_count
        there = jnp.where(turn == side, chips // 2 - side, chip)
        there = jnp.where(turn == 1 - side, (1 - side) * (chips - 1), there)
        there = jnp.where(turn == 2, 2 * (chip // 2) + 1 - chip % 2, there)
        shift = t + turn // (chips - 1)
        return there * sub_count + (core + shift) % sub_count

    def signal(semaphore, peer):
        pl.semaphore_signal(
            semaphore, inc=1, device_id=device(peer), device_id_type=pl.DeviceIdType.MESH
        )

    barrier = pltpu.get_barrier_semaphore()

    @pl.when(inner)
    def _():
        signal(barrier, far_inner(0))

    @pl.when(outer)
    def _():
        for t in range(sub_count - 1):
            signal(barrier, core_peer(t))

    own = [
        pltpu.make_async_copy(cross_q, local_cq, local_sem.at[0]),
        pltpu.make_async_copy(aud_k, near_k.at[1], local_sem.at[1]),
        pltpu.make_async_copy(aud_v, near_v.at[1], local_sem.at[2]),
        pltpu.make_async_copy(windows, local_windows, local_sem.at[3]),
    ]
    for copy in own:
        copy.start()

    def column(index):
        return pl.ds(pl.multiple_of(index * LANES, LANES), LANES)

    def row(index):
        return pl.ds(pl.multiple_of(index * rows, rows), rows)

    def columns(index):
        return pl.ds(pl.multiple_of(index * width, LANES), width)

    def video_way(array, which, h):
        return (
            lambda peer: array.at[:, column(peer * video_each + h)],
            lambda source: land.at[which, h, row(source), :],
            2,
            4 + h,
        )

    def half_way(array, which):
        return (
            lambda peer: array.at[:, columns(peer % half)],
            lambda source: land_c.at[which, row(source % half), :],
            1,
            1,
        )

    ways = [
        (
            lambda peer: aud_q.at[:, columns(peer % half)],
            lambda source: land_aq.at[source],
            0,
            0,
        )
    ]
    audio_ways = [0]
    video_ways = []
    for h in range(video_each):
        video_ways.append(list(range(len(ways), len(ways) + 3)))
        for which, array in enumerate((vid_k, vid_v, vid_q)):
            ways.append(video_way(array, which, h))
        if h == 0:
            for which, array in enumerate((cross_k, cross_v)):
                audio_ways.append(len(ways))
                ways.append(half_way(array, which))
    first = len(ways)
    early = audio_ways[:1] + video_ways[0]
    late = [k for kinds in video_ways[1:] for k in kinds]
    for h in range(video_each):
        ways.append(
            (
                lambda peer, h=h: mixed_v.at[h, row(peer), :],
                lambda source, h=h: video_self.at[:, column(source * video_each + h)],
                3,
                2,
            )
        )
    ways.append(
        (
            lambda peer: mixed_a.at[peer % half],
            lambda source: audio_out.at[:, columns(source % half)],
            4,
            3,
        )
    )
    sent = (
        land_aq.at[pl.ds(0, count - 1)],
        land_c.at[:, pl.ds(0, (half - 1) * rows), :],
        land.at[:, :, pl.ds(0, (count - 1) * rows), :],
        mixed_v.at[:, pl.ds(0, (count - 1) * rows), :],
        mixed_a.at[pl.ds(0, half - 1)],
    )
    landed = [land_aq, land_c, video_self, audio_out]
    landed += [land.at[:, h] for h in range(video_each)]

    def outgoing(k, peer):
        return pltpu.make_async_remote_copy(
            src_ref=ways[k][0](peer),
            dst_ref=ways[k][1](me),
            send_sem=send_sem.at[ways[k][2]],
            recv_sem=recv_sem.at[ways[k][3]],
            device_id=device(peer),
            device_id_type=pl.DeviceIdType.MESH,
        )

    def kept(k):
        return pltpu.make_async_copy(ways[k][0](me), ways[k][1](me), recv_sem.at[ways[k][3]])

    def await_landed(i):
        pltpu.make_async_copy(landed[i], landed[i], recv_sem.at[i]).wait()

    def await_sent(i):
        pltpu.make_async_copy(sent[i], sent[i], send_sem.at[i]).wait()

    def near_copy(array, near, slot, peer):
        return pltpu.make_async_remote_copy(
            src_ref=array,
            dst_ref=near.at[slot],
            send_sem=near_send.at[slot // 2],
            recv_sem=near_recv.at[slot // 2],
            device_id=device(peer),
            device_id_type=pl.DeviceIdType.MESH,
        )

    near_pairs = ((aud_k, near_k), (aud_v, near_v))

    def send_right():
        for array, near in near_pairs:
            near_copy(array, near, 0, me + 1).start()

    def send_left():
        for array, near in near_pairs:
            near_copy(array, near, 2, me - 1).start()

    def await_near(semaphore):
        both = near_k.at[pl.ds(0, 2)]
        pltpu.make_async_copy(both, both, semaphore).wait()

    def send(k, peer_of, steps):
        def one(t, carry):
            outgoing(k, peer_of(t)).start()
            return carry

        lax.fori_loop(0, steps, one, 0)

    pair = sub_count - 1
    audio_only = audio_ways[1:]

    def send_keep(ks):
        for k in ks:
            send(k, core_peer, pair)
            kept(k).start()

    @pl.when(inner)
    def _():
        leads = core == sub_count - 1
        pl.semaphore_wait(barrier, jnp.where(leads, 1, 2))

        @pl.when(leads)
        def _():
            signal(barrier, core_peer(0))

        @pl.when(jnp.logical_not(leads))
        def _():
            signal(pair_sem, core_peer(0))

        for k in early:
            send(k, far_inner, 1)
        for t in range(sub_count):
            signal(barrier, near_outer(t))

        @pl.when(leads)
        def _():
            pl.semaphore_wait(pair_sem, 1)

        for k in early:
            send(k, far_inner_rest, sub_count - 1)

        @pl.when(side == 0)
        def _():
            send_right()

            @pl.when(core > 0)
            def _():
                send_left()

        @pl.when(side == 1)
        def _():
            send_left()

            @pl.when(core < sub_count - 1)
            def _():
                send_right()

        send_keep(early[:1] + audio_only)
        pl.semaphore_wait(ready_sem.at[side], sub_count)

        @pl.when((side == 0) & (core == 0))
        def _():
            send_left()

        @pl.when((side == 1) & (core == sub_count - 1))
        def _():
            send_right()

        for k in early[:1] + audio_only + early[1:] + late:
            send(k, near_outer, sub_count)
        pl.semaphore_wait(ready_sem.at[1 - side], sub_count)
        signal(all_sem, near_outer(0))
        for k in early:
            send(k, far_outer, sub_count)
        for k in late:
            send(k, far_inner, sub_count)
        for k in late:
            send(k, far_outer, sub_count)
        send_keep(early[1:] + late)

    @pl.when(outer)
    def _():
        pl.semaphore_wait(barrier, 2 * sub_count - 1)
        for t in range(sub_count):
            signal(ready_sem.at[side], near_inner(t))
            signal(ready_sem.at[side], far_inner(t))

        for k in early[:1]:
            send(k, far_inner, sub_count)

        @pl.when(me < count - 1)
        def _():
            send_right()

        @pl.when(me > 0)
        def _():
            send_left()

        for k in early[:1] + audio_only:
            send(k, near_inner, sub_count)
        send_keep(early[:1] + audio_only)
        pl.semaphore_wait(all_sem, 1)
        for k in early[:1]:
            send(k, far_outer, sub_count)
        for k in early[1:] + late:
            send(k, near_inner, sub_count)
        for ks in (early[1:], late):
            for k in ks:
                send(k, far_outer, sub_count)
            for k in ks:
                send(k, far_inner, sub_count)
        send_keep(early[1:] + late)

    @pl.when(me == 0)
    def _():
        for array, near in near_pairs:
            near[0] = jnp.zeros(near.shape[1:], near.dtype)

    @pl.when(me == count - 1)
    def _():
        for array, near in near_pairs:
            near[2] = jnp.zeros(near.shape[1:], near.dtype)

    for copy in own:
        copy.wait()

    @pl.when(me > 0)
    def _():
        await_near(near_recv.at[0])

    @pl.when(me < count - 1)
    def _():
        await_near(near_recv.at[1])

    spans = windows.shape[1]
    tile = (me * rows + lax.broadcasted_iota(jnp.int32, (rows, spans), 0)) // TILE_LEN
    bounds = local_windows[...]
    inside = (bounds[0:1, :] <= tile) & (tile < bounds[1:2, :])
    inside = jnp.where(inside, 1.0, 0.0).astype(jnp.bfloat16)
    seen = []
    for slot in range(3):
        stretch = lax.broadcasted_iota(jnp.int32, (spans, audio_rows), 1) // STRETCH_LEN
        stretch = stretch + (me + slot - 1) * (audio_rows // STRETCH_LEN)
        picks = stretch == lax.broadcasted_iota(jnp.int32, (spans, audio_rows), 0)
        picks = jnp.where(picks, 1.0, 0.0).astype(jnp.bfloat16)
        part = jnp.dot(inside, picks, preferred_element_type=jnp.float32)
        seen.append(jnp.concatenate([part] * (LANES // AUDIO_DIM), axis=0))

    for b in range(cross_q.shape[1] // LANES):
        lanes = slice(b * LANES, (b + 1) * LANES)
        stacked = lane_heads(local_cq[:, lanes])
        scores = []
        for slot in range(3):
            part = lax.dot_general(
                stacked,
                near_k[slot, :, lanes],
                (((1,), (1,)), ((), ())),
                preferred_element_type=jnp.float32,
            )
            scores.append(jnp.where(seen[slot] > 0.5, part, jnp.float32(-1e30)))
        peak = jnp.max(jnp.maximum(jnp.maximum(scores[0], scores[1]), scores[2]), axis=1, keepdims=True)
        factor = jnp.float32(audio_scaling * math.log2(math.e))
        weights = [jnp.exp2((part - peak) * factor) for part in scores]
        summed = jnp.sum(weights[0] + weights[1] + weights[2], axis=1, keepdims=True)
        mixed = sum(
            jnp.dot(
                weights[slot].astype(jnp.bfloat16),
                near_v[slot, :, lanes],
                preferred_element_type=jnp.float32,
            )
            for slot in range(3)
        )
        video_cross[:, lanes] = merge_lane_heads(mixed / summed, rows).astype(jnp.bfloat16)

    def part_copy(j, array, land):
        return pltpu.make_async_remote_copy(
            src_ref=array,
            dst_ref=land,
            send_sem=part_send.at[j],
            recv_sem=part_recv.at[j],
            device_id=device((me + half) % count),
            device_id_type=pl.DeviceIdType.MESH,
        )

    part_copies = [part_copy(0, far_part, got_part), part_copy(1, far_stat, got_stat)]
    each = LANES // AUDIO_DIM
    levels = half * blocks_each * each
    folds = level_folds(levels, audio_rows)
    span = LANES // folds
    stat_row = lax.broadcasted_iota(jnp.int32, (LANES, LANES), 0) // span
    stat_lane = lax.broadcasted_iota(jnp.int32, (LANES, LANES), 1)

    def audio_parts(first_source, part, stat):
        def one(j, stats):
            queries = land_aq[first_source + j]
            for b in range(blocks_each):
                lanes = slice(b * LANES, (b + 1) * LANES)
                mixed, peak, summed = softmax_mix(
                    lane_heads(queries[:, lanes]), land_c[0, :, lanes], land_c[1, :, lanes], audio_scaling
                )
                part[j, :, lanes] = merge_lane_heads(mixed, audio_rows).astype(part.dtype)
                level = peak * jnp.float32(audio_scaling * math.log2(math.e)) + jnp.log2(summed)
                rest = jnp.zeros((span - audio_rows, 1), jnp.float32)
                for i in range(each):
                    index = (j * blocks_each + b) * each + i
                    picked = stat_lane * folds + stat_row == index
                    held = level[i * audio_rows : (i + 1) * audio_rows]
                    stats = jnp.where(picked, jnp.concatenate([held, rest] * folds, axis=0), stats)
            return stats

        stats = lax.fori_loop(0, half, one, jnp.zeros((LANES, LANES), jnp.float32))
        stat[...] = stats.T[: stat.shape[0]]

    def merge_parts(peer):
        j = peer % half
        unpacked = []
        for stat in (own_stat, got_stat):
            rest = jnp.zeros((LANES - stat.shape[0], LANES), jnp.float32)
            unpacked.append(jnp.concatenate([stat[...], rest], axis=0).T)
        for b in range(blocks_each):
            lanes = slice(b * LANES, (b + 1) * LANES)
            shares = []
            for i in range(each):
                picked = stat_lane * folds + stat_row == (j * blocks_each + b) * each + i
                mine, other = (
                    sum(kept_rows[g * span : g * span + audio_rows] for g in range(folds))
                    for kept_rows in (
                        jnp.sum(jnp.where(picked, wide, 0.0), axis=1, keepdims=True)
                        for wide in unpacked
                    )
                )
                peak = jnp.maximum(mine, other)
                mine = jnp.exp2(mine - peak)
                other = jnp.exp2(other - peak)
                total = mine + other
                shares.append((mine / total, other / total))
            own_share, got_share = (
                merge_lane_heads(
                    jnp.concatenate(
                        [jnp.broadcast_to(s[w], (audio_rows, LANES)) for s in shares], axis=0
                    ),
                    audio_rows,
                )
                for w in range(2)
            )
            merged = own_part[j, :, lanes] * own_share
            merged = merged + got_part[j, :, lanes].astype(jnp.float32) * got_share
            mixed_a[j, :, lanes] = merged.astype(jnp.bfloat16)

    await_landed(0)
    await_landed(1)
    audio_parts((1 - side) * half, far_part, far_stat)
    audio_parts(side * half, own_part, own_stat)

    def mix_video(h, source):
        mixed, peak, summed = softmax_mix(
            land[2, h, row(source), :], land[0, h], land[1, h], video_scaling
        )
        mixed_v[h, row(source), :] = mixed.astype(jnp.bfloat16)

    for copy in part_copies:
        copy.start()

    def gated(turn):
        return inner & (turn == 0)

    def delayed(turn):
        return (side == 1) & (turn == 1)

    def send_held(condition):
        for earlier in range(video_each - 1):
            for i in range(2 * sub_count):

                @pl.when(condition(i // sub_count))
                def _():
                    outgoing(first + earlier, out_peer(i)).start()

    def merge_all():
        for copy in part_copies:
            copy.wait()
        merged = len(ways) - 1

        def one_merge(t, carry):
            merge_parts(peer_near(t))

            @pl.when(t < half - 1)
            def _():
                outgoing(merged, peer_near(t)).start()

            return carry

        lax.fori_loop(0, half, one_merge, 0)
        kept(merged).start()

    for h in range(video_each):
        await_landed(4 + h)
        last = h == video_each - 1
        if last:
            send_held(gated)

        order = last_peer if last else out_peer

        def one(t, carry, h=h, last=last, order=order):
            mix_video(h, order(t))
            now = t > 0
            if not last:
                turn = (t - 1) // sub_count
                now = now & jnp.logical_not(gated(turn) | delayed(turn))

            @pl.when(now)
            def _():
                outgoing(first + h, order(t - 1)).start()

            if last:

                @pl.when(t == sub_count)
                def _():
                    send_held(delayed)

                @pl.when(t == 2 * sub_count)
                def _():
                    merge_all()

            return carry

        lax.fori_loop(0, count, one, 0)
        kept(first + h).start()
    for i in range(len(sent)):
        await_sent(i)
    await_landed(2)
    await_landed(3)

    @pl.when(me < count - 1)
    def _():
        await_near(near_send.at[0])

    @pl.when(me > 0)
    def _():
        await_near(near_send.at[1])


def level_folds(levels, audio_rows):
    folds = 1
    while levels % (2 * folds) == 0 and levels > 8 * folds and LANES >= 2 * folds * audio_rows:
        folds = 2 * folds
    return folds


def store_kernel(*refs):
    copies = [pltpu.make_async_copy(refs[i], refs[3 + i], refs[6].at[i]) for i in range(3)]
    for copy in copies:
        copy.start()
    for copy in copies:
        copy.wait()


def exchanged_body(count, sub_count, *arrays):
    vid_q, vid_k, vid_v, aud_q, cross_k, cross_v, cross_q, aud_k, aud_v, windows = arrays
    rows = vid_q.shape[0]
    audio_rows = aud_q.shape[0]
    video_each = vid_q.shape[1] // HEAD_DIM // count
    halves = count // 2
    width = aud_q.shape[1] // halves
    levels = aud_q.shape[1] // AUDIO_DIM
    levels = -(-levels // level_folds(levels, audio_rows) // 8) * 8
    half = jnp.bfloat16
    place = pl.BlockSpec(memory_space=pl.ANY)
    held = pl.pallas_call(
        partial(exchange_kernel, count, sub_count),
        out_shape=tuple(pltpu.VMEM(a.shape, half) for a in (vid_q, aud_q, cross_q)),
        in_specs=[place] * 10,
        out_specs=(pl.BlockSpec(memory_space=pltpu.VMEM),) * 3,
        scratch_shapes=[
            pltpu.VMEM((3, video_each, count * rows, HEAD_DIM), half),
            pltpu.VMEM((count, audio_rows, width), half),
            pltpu.VMEM((2, halves * rows, width), half),
            pltpu.VMEM((video_each, count * rows, HEAD_DIM), half),
            pltpu.VMEM((halves, audio_rows, width), half),
            pltpu.VMEM((halves, audio_rows, width), jnp.float32),
            pltpu.VMEM((levels, LANES), jnp.float32),
            pltpu.VMEM((halves, audio_rows, width), half),
            pltpu.VMEM((levels, LANES), jnp.float32),
            pltpu.VMEM((halves, audio_rows, width), half),
            pltpu.VMEM((levels, LANES), jnp.float32),
            pltpu.VMEM((3, audio_rows, aud_k.shape[1]), half),
            pltpu.VMEM((3, audio_rows, aud_k.shape[1]), half),
            pltpu.VMEM(cross_q.shape, half),
            pltpu.VMEM(windows.shape, windows.dtype),
            pltpu.SemaphoreType.DMA((5,)),
            pltpu.SemaphoreType.DMA((4 + video_each,)),
            pltpu.SemaphoreType.DMA((2,)),
            pltpu.SemaphoreType.DMA((2,)),
            pltpu.SemaphoreType.DMA((2,)),
            pltpu.SemaphoreType.DMA((2,)),
            pltpu.SemaphoreType.DMA((4,)),
            pltpu.SemaphoreType.REGULAR((2,)),
            pltpu.SemaphoreType.REGULAR,
            pltpu.SemaphoreType.REGULAR,
        ],
        compiler_params=pltpu.CompilerParams(collective_id=0, has_side_effects=True),
        name="joint_attention",
    )(*arrays)
    return pl.pallas_call(
        store_kernel,
        out_shape=tuple(jax.ShapeDtypeStruct(a.shape, half) for a in (vid_q, aud_q, cross_q)),
        in_specs=[pl.BlockSpec(memory_space=pltpu.VMEM)] * 3,
        out_specs=(place, place, place),
        scratch_shapes=[pltpu.SemaphoreType.DMA((3,))],
        name="store_results",
    )(*[pltpu.with_memory_space_constraint(x, pltpu.VMEM) for x in held])


def body(*arrays):
    sub_count = lax.axis_size("sub")
    count = lax.axis_size("seq") * sub_count
    video_heads = arrays[0].shape[1] // HEAD_DIM
    audio_heads = arrays[3].shape[1] // AUDIO_DIM
    halved = sub_count == 2 and count == 4 * sub_count and max(audio_heads, arrays[3].shape[0]) <= LANES
    if halved and video_heads % count == 0 and audio_heads % count == 0:
        return exchanged_body(count, sub_count, *arrays)
    return gathered_body(*arrays)


def solution(mesh):
    return jax.shard_map(
        body,
        mesh=mesh,
        in_specs=(
            P(("grp", "seq", "sub"), "head"),
            P(("grp", "seq", "sub"), "head"),
            P(("grp", "seq", "sub"), "head"),
            P(("grp", "seq", "sub"), "head"),
            P(("grp", "seq", "sub"), "head"),
            P(("grp", "seq", "sub"), "head"),
            P(("grp", "seq", "sub"), "head"),
            P(("grp", "seq", "sub"), "head"),
            P(("grp", "seq", "sub"), "head"),
            P(None, "grp"),
        ),
        out_specs=(
            P(("grp", "seq", "sub"), "head"),
            P(("grp", "seq", "sub"), "head"),
            P(("grp", "seq", "sub"), "head"),
        ),
        check_vma=False,
    )
```

```python
from functools import partial
import math

import jax
import jax.numpy as jnp
from jax import lax
from jax.experimental import pallas as pl
from jax.experimental.pallas import tpu as pltpu
from jax.sharding import PartitionSpec as P

HEAD_DIM = 128
AUDIO_DIM = 64
TILE_LEN = 32
STRETCH_LEN = 8


def extended(cells, sides, width):
    for axis, dim in sides:
        count = lax.axis_size(axis)
        ends = count - 1
        head = lax.slice_in_dim(cells, 0, width, axis=dim)
        tail = lax.slice_in_dim(cells, cells.shape[dim] - width, cells.shape[dim], axis=dim)
        cells = jnp.concatenate(
            [
                lax.ppermute(tail, axis, [(i, (i + 1) % count) for i in range(ends)]),
                cells,
                lax.ppermute(head, axis, [((i + 1) % count, i) for i in range(ends)]),
            ],
            axis=dim,
        )
    return cells


def start_state(query_count, head_count, head_size):
    running = jnp.full((head_count, query_count), -jnp.inf, jnp.float32)
    summed = jnp.zeros((head_count, query_count), jnp.float32)
    numerator = jnp.zeros((head_count, query_count, head_size), jnp.float32)
    return (running, summed, numerator)


def absorb(state_in, queries, key_rows, value_rows, head_count, scaling, visible):
    running, summed, numerator = state_in
    query_count = queries.shape[0]
    key_count = key_rows.shape[0]
    head_size = queries.shape[1] // head_count
    scores = (
        jnp.einsum(
            "qhe,khe->hqk",
            queries.reshape(query_count, head_count, head_size),
            key_rows.reshape(key_count, head_count, head_size),
            preferred_element_type=jnp.float32,
        )
        * scaling
    )
    if visible is not None:
        scores = jnp.where(visible[None], scores, jnp.float32(-1e30))
    newest = jnp.maximum(running, jnp.max(scores, axis=2))
    shrink = jnp.exp(running - newest)
    weights = jnp.exp(scores - newest[:, :, None])
    summed = summed * shrink + jnp.sum(weights, axis=2)
    numerator = numerator * shrink[:, :, None] + jnp.einsum(
        "hqk,khe->hqe",
        weights.astype(jnp.bfloat16),
        value_rows.reshape(key_count, head_count, head_size),
        preferred_element_type=jnp.float32,
    )
    return (newest, summed, numerator)


def block_split(total_rows):
    block_rows = total_rows
    while block_rows > 512 and block_rows % 2 == 0:
        block_rows = block_rows // 2
    return (block_rows, total_rows // block_rows)


def fold_keys(state_in, shards_in, offset, queries, head_count, scaling):
    key_rows, value_rows = shards_in
    block_rows, block_count = block_split(key_rows.shape[0])
    key_blocks = key_rows.reshape(block_count, block_rows, key_rows.shape[1])
    value_blocks = value_rows.reshape(block_count, block_rows, value_rows.shape[1])

    def one_block(state, paired):
        return (absorb(state, queries, paired[0], paired[1], head_count, scaling, None), None)

    result, unused = lax.scan(one_block, state_in, (key_blocks, value_blocks))
    return result


def normalize_heads(state_in):
    running, summed, numerator = state_in
    mixed = numerator / summed[:, :, None]
    return mixed.transpose(1, 0, 2).reshape(mixed.shape[1], -1).astype(jnp.bfloat16)


def gathered_body(vid_q, vid_k, vid_v, aud_q, cross_k, cross_v, cross_q, aud_k, aud_v, windows):
    video_heads = vid_q.shape[1] // HEAD_DIM
    video_scaling = 1.0 / math.sqrt(HEAD_DIM)
    audio_heads = aud_q.shape[1] // AUDIO_DIM
    audio_scaling = 1.0 / math.sqrt(AUDIO_DIM)
    moved_q, moved_k, moved_v = (
        lax.all_to_all(vid_q, "sub", split_axis=1, concat_axis=0, tiled=True),
        lax.all_to_all(vid_k, "sub", split_axis=1, concat_axis=0, tiled=True),
        lax.all_to_all(vid_v, "sub", split_axis=1, concat_axis=0, tiled=True),
    )
    pair_heads = video_heads // lax.axis_size("sub")
    folder = partial(fold_keys, queries=moved_q, head_count=pair_heads, scaling=video_scaling)
    state = folder(
        start_state(moved_q.shape[0], pair_heads, HEAD_DIM),
        (
            lax.all_gather(moved_k, "seq", axis=0, tiled=True),
            lax.all_gather(moved_v, "seq", axis=0, tiled=True),
        ),
        jnp.int32(0),
    )
    video_self = lax.all_to_all(
        normalize_heads(state), "sub", split_axis=0, concat_axis=1, tiled=True
    )
    folder = partial(fold_keys, queries=aud_q, head_count=audio_heads, scaling=audio_scaling)
    state = folder(
        start_state(aud_q.shape[0], audio_heads, AUDIO_DIM),
        (
            lax.all_gather(cross_k, ("seq", "sub"), axis=0, tiled=True),
            lax.all_gather(cross_v, ("seq", "sub"), axis=0, tiled=True),
        ),
        jnp.int32(0),
    )
    audio_out = normalize_heads(state)
    audio_rows = aud_k.shape[0]
    key_width = aud_k.shape[1]
    padded_rows = extended(
        jnp.concatenate((aud_k, aud_v), axis=1), ((("seq", "sub"), 0),), audio_rows
    )
    near_keys = padded_rows[:, :key_width]
    near_values = padded_rows[:, key_width:]
    position = lax.axis_index(("seq", "sub"))
    audio_index = (position - 1) * audio_rows + jnp.arange(padded_rows.shape[0], dtype=jnp.int32)
    stretch_index = audio_index // STRETCH_LEN
    stretch_ids = jnp.arange(windows.shape[1], dtype=jnp.int32)
    onehot = stretch_index[:, None] == stretch_ids[None, :]
    first_tile = jnp.sum(jnp.where(onehot, windows[0][None, :], 0), axis=1)
    after_tile = jnp.sum(jnp.where(onehot, windows[1][None, :], 0), axis=1)
    video_rows = cross_q.shape[0]
    video_tile = (position * video_rows + jnp.arange(video_rows, dtype=jnp.int32)) // TILE_LEN
    visible = (first_tile[None, :] <= video_tile[:, None]) & (
        video_tile[:, None] < after_tile[None, :]
    )
    state = absorb(
        start_state(video_rows, audio_heads, AUDIO_DIM),
        cross_q,
        near_keys,
        near_values,
        audio_heads,
        audio_scaling,
        visible,
    )
    video_cross = normalize_heads(state)
    return (video_self, audio_out, video_cross)


LANES = 128
AXES = ("seq", "sub")


def softmax_mix(queries, key_rows, value_rows, scaling):
    scores = lax.dot_general(
        queries, key_rows, (((1,), (1,)), ((), ())), preferred_element_type=jnp.float32
    )
    peak = jnp.max(scores, axis=1, keepdims=True)
    weights = jnp.exp2((scores - peak) * jnp.float32(scaling * math.log2(math.e)))
    summed = jnp.sum(weights, axis=1, keepdims=True)
    mixed = jnp.dot(
        weights.astype(jnp.bfloat16), value_rows, preferred_element_type=jnp.float32
    )
    return mixed / summed, peak, summed


def lane_heads(block):
    wide = block.astype(jnp.float32)
    lane = lax.broadcasted_iota(jnp.int32, wide.shape, 1) // AUDIO_DIM
    parts = [jnp.where(lane == i, wide, 0.0) for i in range(LANES // AUDIO_DIM)]
    return jnp.concatenate(parts, axis=0).astype(jnp.bfloat16)


def merge_lane_heads(stacked, rows):
    lane = lax.broadcasted_iota(jnp.int32, (rows, LANES), 1) // AUDIO_DIM
    merged = stacked[:rows]
    for i in range(1, LANES // AUDIO_DIM):
        merged = jnp.where(lane == i, stacked[i * rows : (i + 1) * rows], merged)
    return merged


def exchange_kernel(
    count,
    sub_count,
    vid_q,
    vid_k,
    vid_v,
    aud_q,
    cross_k,
    cross_v,
    cross_q,
    aud_k,
    aud_v,
    windows,
    video_self,
    audio_out,
    video_cross,
    land,
    land_aq,
    land_c,
    mixed_v,
    mixed_a,
    own_part,
    own_stat,
    far_part,
    far_stat,
    got_part,
    got_stat,
    near_k,
    near_v,
    local_cq,
    local_windows,
    send_sem,
    recv_sem,
    near_send,
    near_recv,
    part_send,
    part_recv,
    local_sem,
    ready_sem,
    all_sem,
    pair_sem,
):
    rows = vid_q.shape[0]
    audio_rows = aud_q.shape[0]
    video_each = vid_q.shape[1] // HEAD_DIM // count
    half = count // 2
    blocks_each = aud_q.shape[1] // LANES // half
    width = blocks_each * LANES
    video_scaling = 1.0 / math.sqrt(HEAD_DIM)
    audio_scaling = 1.0 / math.sqrt(AUDIO_DIM)
    me = lax.axis_index("seq") * sub_count + lax.axis_index("sub")

    side = me // half
    place = me % half

    def device(peer):
        return {"seq": peer // sub_count, "sub": peer % sub_count}

    def peer_near(t):
        return side * half + (place + 1 + t) % half

    chip = me // sub_count
    core = me % sub_count
    inner = (me >= half - sub_count) & (me < half + sub_count)
    outer = jnp.logical_not(inner)

    def inner_of(which, t):
        return half - (1 - which) * sub_count + (core + t) % sub_count

    def outer_of(which, t):
        return which * (half + sub_count) + (core + t) % sub_count

    def core_peer(t):
        return chip * sub_count + (core + 1 + t) % sub_count

    def near_inner(t):
        return inner_of(side, t)

    def near_outer(t):
        return outer_of(side, t)

    def far_inner(t):
        return inner_of(1 - side, t)

    def far_inner_rest(t):
        return inner_of(1 - side, t + 1)

    def far_outer(t):
        return outer_of(1 - side, t)

    def last_peer(t):
        turn = t // sub_count
        kind = turn
        for i, k in enumerate((0, 1, 2)):
            kind = jnp.where(outer & (turn == i), k, kind)
        return out_peer(kind * sub_count + t % sub_count)

    def out_peer(t):
        turn = t // sub_count
        chips = count // sub_count
        there = jnp.where(turn == side, chips // 2 - side, chip)
        there = jnp.where(turn == 1 - side, (1 - side) * (chips - 1), there)
        there = jnp.where(turn == 2, 2 * (chip // 2) + 1 - chip % 2, there)
        shift = t + turn // (chips - 1)
        first_core = jnp.where((side == 0) & (turn == 1), 0, core)
        return there * sub_count + (first_core + shift) % sub_count

    def signal(semaphore, peer):
        pl.semaphore_signal(
            semaphore, inc=1, device_id=device(peer), device_id_type=pl.DeviceIdType.MESH
        )

    barrier = pltpu.get_barrier_semaphore()

    @pl.when(inner)
    def _():
        signal(barrier, far_inner(0))

    @pl.when(outer)
    def _():
        for t in range(sub_count - 1):
            signal(barrier, core_peer(t))

    own = [
        pltpu.make_async_copy(cross_q, local_cq, local_sem.at[0]),
        pltpu.make_async_copy(aud_k, near_k.at[1], local_sem.at[1]),
        pltpu.make_async_copy(aud_v, near_v.at[1], local_sem.at[2]),
        pltpu.make_async_copy(windows, local_windows, local_sem.at[3]),
    ]
    for copy in own:
        copy.start()

    def column(index):
        return pl.ds(pl.multiple_of(index * LANES, LANES), LANES)

    def row(index):
        return pl.ds(pl.multiple_of(index * rows, rows), rows)

    def columns(index):
        return pl.ds(pl.multiple_of(index * width, LANES), width)

    def video_way(array, which, h):
        return (
            lambda peer: array.at[:, column(peer * video_each + h)],
            lambda source: land.at[which, h, row(source), :],
            2,
            4 + h,
        )

    def half_way(array, which):
        return (
            lambda peer: array.at[:, columns(peer % half)],
            lambda source: land_c.at[which, row(source % half), :],
            1,
            1,
        )

    ways = [
        (
            lambda peer: aud_q.at[:, columns(peer % half)],
            lambda source: land_aq.at[source],
            0,
            0,
        )
    ]
    audio_ways = [0]
    video_ways = []
    for h in range(video_each):
        video_ways.append(list(range(len(ways), len(ways) + 3)))
        for which, array in enumerate((vid_k, vid_v, vid_q)):
            ways.append(video_way(array, which, h))
        if h == 0:
            for which, array in enumerate((cross_k, cross_v)):
                audio_ways.append(len(ways))
                ways.append(half_way(array, which))
    first = len(ways)
    early = audio_ways[:1] + video_ways[0]
    late = [k for kinds in video_ways[1:] for k in kinds]
    for h in range(video_each):
        ways.append(
            (
                lambda peer, h=h: mixed_v.at[h, row(peer), :],
                lambda source, h=h: video_self.at[:, column(source * video_each + h)],
                3,
                2,
            )
        )
    ways.append(
        (
            lambda peer: mixed_a.at[peer % half],
            lambda source: audio_out.at[:, columns(source % half)],
            4,
            3,
        )
    )
    sent = (
        land_aq.at[pl.ds(0, count - 1)],
        land_c.at[:, pl.ds(0, (half - 1) * rows), :],
        land.at[:, :, pl.ds(0, (count - 1) * rows), :],
        mixed_v.at[:, pl.ds(0, (count - 1) * rows), :],
        mixed_a.at[pl.ds(0, half - 1)],
    )
    landed = [land_aq, land_c, video_self, audio_out]
    landed += [land.at[:, h] for h in range(video_each)]

    def outgoing(k, peer):
        return pltpu.make_async_remote_copy(
            src_ref=ways[k][0](peer),
            dst_ref=ways[k][1](me),
            send_sem=send_sem.at[ways[k][2]],
            recv_sem=recv_sem.at[ways[k][3]],
            device_id=device(peer),
            device_id_type=pl.DeviceIdType.MESH,
        )

    def kept(k):
        return pltpu.make_async_copy(ways[k][0](me), ways[k][1](me), recv_sem.at[ways[k][3]])

    def await_landed(i):
        pltpu.make_async_copy(landed[i], landed[i], recv_sem.at[i]).wait()

    def await_sent(i):
        pltpu.make_async_copy(sent[i], sent[i], send_sem.at[i]).wait()

    def near_copy(array, near, slot, peer):
        return pltpu.make_async_remote_copy(
            src_ref=array,
            dst_ref=near.at[slot],
            send_sem=near_send.at[slot // 2],
            recv_sem=near_recv.at[slot // 2],
            device_id=device(peer),
            device_id_type=pl.DeviceIdType.MESH,
        )

    near_pairs = ((aud_k, near_k), (aud_v, near_v))

    def send_right():
        for array, near in near_pairs:
            near_copy(array, near, 0, me + 1).start()

    def send_left():
        for array, near in near_pairs:
            near_copy(array, near, 2, me - 1).start()

    def await_near(semaphore):
        both = near_k.at[pl.ds(0, 2)]
        pltpu.make_async_copy(both, both, semaphore).wait()

    def send(k, peer_of, steps):
        def one(t, carry):
            outgoing(k, peer_of(t)).start()
            return carry

        lax.fori_loop(0, steps, one, 0)

    pair = sub_count - 1
    audio_only = audio_ways[1:]

    def send_keep(ks):
        for k in ks:
            send(k, core_peer, pair)
            kept(k).start()

    @pl.when(inner)
    def _():
        leads = core == sub_count - 1
        pl.semaphore_wait(barrier, jnp.where(leads, 1, 2))

        @pl.when(leads)
        def _():
            signal(barrier, core_peer(0))

        @pl.when(jnp.logical_not(leads))
        def _():
            signal(pair_sem, core_peer(0))

        for k in early:
            send(k, far_inner, 1)
        for t in range(sub_count):
            signal(barrier, near_outer(t))

        @pl.when(leads)
        def _():
            pl.semaphore_wait(pair_sem, 1)

        for k in early:
            send(k, far_inner_rest, sub_count - 1)

        @pl.when(side == 0)
        def _():
            send_right()

            @pl.when(core > 0)
            def _():
                send_left()

        @pl.when(side == 1)
        def _():
            send_left()

            @pl.when(core < sub_count - 1)
            def _():
                send_right()

        send_keep(early[:1] + audio_only)
        pl.semaphore_wait(ready_sem.at[side], sub_count)

        @pl.when((side == 0) & (core == 0))
        def _():
            send_left()

        @pl.when((side == 1) & (core == sub_count - 1))
        def _():
            send_right()

        for k in early[:1] + audio_only + early[1:] + late:
            send(k, near_outer, sub_count)
        pl.semaphore_wait(ready_sem.at[1 - side], sub_count)
        signal(all_sem, near_outer(0))
        for k in early:
            send(k, far_outer, sub_count)
        for k in late:
            send(k, far_inner, sub_count)
        for k in late:
            send(k, far_outer, sub_count)
        send_keep(early[1:] + late)

    @pl.when(outer)
    def _():
        pl.semaphore_wait(barrier, 2 * sub_count - 1)
        for t in range(sub_count):
            signal(ready_sem.at[side], near_inner(t))
            signal(ready_sem.at[side], far_inner(t))

        for k in early[:1]:
            send(k, far_inner, sub_count)

        @pl.when(me < count - 1)
        def _():
            send_right()

        @pl.when(me > 0)
        def _():
            send_left()

        for k in early[:1] + audio_only:
            send(k, near_inner, sub_count)
        send_keep(early[:1] + audio_only)
        pl.semaphore_wait(all_sem, 1)
        for k in early[:1]:
            send(k, far_outer, sub_count)
        for k in early[1:] + late:
            send(k, near_inner, sub_count)
        for ks in (early[1:], late):
            for k in ks:
                send(k, far_outer, sub_count)
            for k in ks:
                send(k, far_inner, sub_count)
        send_keep(early[1:] + late)

    @pl.when(me == 0)
    def _():
        for array, near in near_pairs:
            near[0] = jnp.zeros(near.shape[1:], near.dtype)

    @pl.when(me == count - 1)
    def _():
        for array, near in near_pairs:
            near[2] = jnp.zeros(near.shape[1:], near.dtype)

    for copy in own:
        copy.wait()

    @pl.when(me > 0)
    def _():
        await_near(near_recv.at[0])

    @pl.when(me < count - 1)
    def _():
        await_near(near_recv.at[1])

    spans = windows.shape[1]
    tile = (me * rows + lax.broadcasted_iota(jnp.int32, (rows, spans), 0)) // TILE_LEN
    bounds = local_windows[...]
    inside = (bounds[0:1, :] <= tile) & (tile < bounds[1:2, :])
    inside = jnp.where(inside, 1.0, 0.0).astype(jnp.bfloat16)
    seen = []
    for slot in range(3):
        stretch = lax.broadcasted_iota(jnp.int32, (spans, audio_rows), 1) // STRETCH_LEN
        stretch = stretch + (me + slot - 1) * (audio_rows // STRETCH_LEN)
        picks = stretch == lax.broadcasted_iota(jnp.int32, (spans, audio_rows), 0)
        picks = jnp.where(picks, 1.0, 0.0).astype(jnp.bfloat16)
        part = jnp.dot(inside, picks, preferred_element_type=jnp.float32)
        seen.append(jnp.concatenate([part] * (LANES // AUDIO_DIM), axis=0))

    for b in range(cross_q.shape[1] // LANES):
        lanes = slice(b * LANES, (b + 1) * LANES)
        stacked = lane_heads(local_cq[:, lanes])
        scores = []
        for slot in range(3):
            part = lax.dot_general(
                stacked,
                near_k[slot, :, lanes],
                (((1,), (1,)), ((), ())),
                preferred_element_type=jnp.float32,
            )
            scores.append(jnp.where(seen[slot] > 0.5, part, jnp.float32(-1e30)))
        peak = jnp.max(jnp.maximum(jnp.maximum(scores[0], scores[1]), scores[2]), axis=1, keepdims=True)
        factor = jnp.float32(audio_scaling * math.log2(math.e))
        weights = [jnp.exp2((part - peak) * factor) for part in scores]
        summed = jnp.sum(weights[0] + weights[1] + weights[2], axis=1, keepdims=True)
        mixed = sum(
            jnp.dot(
                weights[slot].astype(jnp.bfloat16),
                near_v[slot, :, lanes],
                preferred_element_type=jnp.float32,
            )
            for slot in range(3)
        )
        video_cross[:, lanes] = merge_lane_heads(mixed / summed, rows).astype(jnp.bfloat16)

    def part_copy(j, array, land):
        return pltpu.make_async_remote_copy(
            src_ref=array,
            dst_ref=land,
            send_sem=part_send.at[j],
            recv_sem=part_recv.at[j],
            device_id=device((me + half) % count),
            device_id_type=pl.DeviceIdType.MESH,
        )

    part_copies = [part_copy(0, far_part, got_part), part_copy(1, far_stat, got_stat)]
    each = LANES // AUDIO_DIM
    levels = half * blocks_each * each
    folds = level_folds(levels, audio_rows)
    span = LANES // folds
    stat_row = lax.broadcasted_iota(jnp.int32, (LANES, LANES), 0) // span
    stat_lane = lax.broadcasted_iota(jnp.int32, (LANES, LANES), 1)

    def audio_parts(first_source, part, stat):
        def one(j, stats):
            queries = land_aq[first_source + j]
            for b in range(blocks_each):
                lanes = slice(b * LANES, (b + 1) * LANES)
                mixed, peak, summed = softmax_mix(
                    lane_heads(queries[:, lanes]), land_c[0, :, lanes], land_c[1, :, lanes], audio_scaling
                )
                part[j, :, lanes] = merge_lane_heads(mixed, audio_rows).astype(part.dtype)
                level = peak * jnp.float32(audio_scaling * math.log2(math.e)) + jnp.log2(summed)
                rest = jnp.zeros((span - audio_rows, 1), jnp.float32)
                for i in range(each):
                    index = (j * blocks_each + b) * each + i
                    picked = stat_lane * folds + stat_row == index
                    held = level[i * audio_rows : (i + 1) * audio_rows]
                    stats = jnp.where(picked, jnp.concatenate([held, rest] * folds, axis=0), stats)
            return stats

        stats = lax.fori_loop(0, half, one, jnp.zeros((LANES, LANES), jnp.float32))
        stat[...] = stats.T[: stat.shape[0]]

    def merge_parts(peer):
        j = peer % half
        unpacked = []
        for stat in (own_stat, got_stat):
            rest = jnp.zeros((LANES - stat.shape[0], LANES), jnp.float32)
            unpacked.append(jnp.concatenate([stat[...], rest], axis=0).T)
        for b in range(blocks_each):
            lanes = slice(b * LANES, (b + 1) * LANES)
            shares = []
            for i in range(each):
                picked = stat_lane * folds + stat_row == (j * blocks_each + b) * each + i
                mine, other = (
                    sum(kept_rows[g * span : g * span + audio_rows] for g in range(folds))
                    for kept_rows in (
                        jnp.sum(jnp.where(picked, wide, 0.0), axis=1, keepdims=True)
                        for wide in unpacked
                    )
                )
                peak = jnp.maximum(mine, other)
                mine = jnp.exp2(mine - peak)
                other = jnp.exp2(other - peak)
                total = mine + other
                shares.append((mine / total, other / total))
            own_share, got_share = (
                merge_lane_heads(
                    jnp.concatenate(
                        [jnp.broadcast_to(s[w], (audio_rows, LANES)) for s in shares], axis=0
                    ),
                    audio_rows,
                )
                for w in range(2)
            )
            merged = own_part[j, :, lanes] * own_share
            merged = merged + got_part[j, :, lanes].astype(jnp.float32) * got_share
            mixed_a[j, :, lanes] = merged.astype(jnp.bfloat16)

    await_landed(0)
    await_landed(1)
    audio_parts((1 - side) * half, far_part, far_stat)
    audio_parts(side * half, own_part, own_stat)

    def mix_video(h, source):
        mixed, peak, summed = softmax_mix(
            land[2, h, row(source), :], land[0, h], land[1, h], video_scaling
        )
        mixed_v[h, row(source), :] = mixed.astype(jnp.bfloat16)

    for copy in part_copies:
        copy.start()

    def gated(turn):
        return inner & (turn == 0)

    def delayed(turn):
        return (inner | (side == 1)) & (turn == 1)

    def send_held(condition):
        for earlier in range(video_each - 1):
            for i in range(2 * sub_count):

                @pl.when(condition(i // sub_count))
                def _():
                    outgoing(first + earlier, out_peer(i)).start()

    def merge_all():
        for copy in part_copies:
            copy.wait()
        merged = len(ways) - 1

        def one_merge(t, carry):
            merge_parts(peer_near(t))

            @pl.when(t < half - 1)
            def _():
                outgoing(merged, peer_near(t)).start()

            return carry

        lax.fori_loop(0, half, one_merge, 0)
        kept(merged).start()

    for h in range(video_each):
        await_landed(4 + h)
        last = h == video_each - 1
        if last:
            send_held(gated)

        order = last_peer if last else out_peer

        def one(t, carry, h=h, last=last, order=order):
            mix_video(h, order(t))
            now = t > 0
            if not last:
                turn = (t - 1) // sub_count
                now = now & jnp.logical_not(gated(turn) | delayed(turn))

            @pl.when(now)
            def _():
                outgoing(first + h, order(t - 1)).start()

            if last:

                @pl.when(t == sub_count)
                def _():
                    send_held(delayed)

                @pl.when(t == 2 * sub_count)
                def _():
                    merge_all()

            return carry

        lax.fori_loop(0, count, one, 0)
        kept(first + h).start()
    for i in range(len(sent)):
        await_sent(i)
    await_landed(2)
    await_landed(3)

    @pl.when(me < count - 1)
    def _():
        await_near(near_send.at[0])

    @pl.when(me > 0)
    def _():
        await_near(near_send.at[1])


def level_folds(levels, audio_rows):
    folds = 1
    while levels % (2 * folds) == 0 and levels > 8 * folds and LANES >= 2 * folds * audio_rows:
        folds = 2 * folds
    return folds


def store_kernel(*refs):
    copies = [pltpu.make_async_copy(refs[i], refs[3 + i], refs[6].at[i]) for i in range(3)]
    for copy in copies:
        copy.start()
    for copy in copies:
        copy.wait()


def exchanged_body(count, sub_count, *arrays):
    vid_q, vid_k, vid_v, aud_q, cross_k, cross_v, cross_q, aud_k, aud_v, windows = arrays
    rows = vid_q.shape[0]
    audio_rows = aud_q.shape[0]
    video_each = vid_q.shape[1] // HEAD_DIM // count
    halves = count // 2
    width = aud_q.shape[1] // halves
    levels = aud_q.shape[1] // AUDIO_DIM
    levels = -(-levels // level_folds(levels, audio_rows) // 8) * 8
    half = jnp.bfloat16
    place = pl.BlockSpec(memory_space=pl.ANY)
    held = pl.pallas_call(
        partial(exchange_kernel, count, sub_count),
        out_shape=tuple(pltpu.VMEM(a.shape, half) for a in (vid_q, aud_q, cross_q)),
        in_specs=[place] * 10,
        out_specs=(pl.BlockSpec(memory_space=pltpu.VMEM),) * 3,
        scratch_shapes=[
            pltpu.VMEM((3, video_each, count * rows, HEAD_DIM), half),
            pltpu.VMEM((count, audio_rows, width), half),
            pltpu.VMEM((2, halves * rows, width), half),
            pltpu.VMEM((video_each, count * rows, HEAD_DIM), half),
            pltpu.VMEM((halves, audio_rows, width), half),
            pltpu.VMEM((halves, audio_rows, width), jnp.float32),
            pltpu.VMEM((levels, LANES), jnp.float32),
            pltpu.VMEM((halves, audio_rows, width), half),
            pltpu.VMEM((levels, LANES), jnp.float32),
            pltpu.VMEM((halves, audio_rows, width), half),
            pltpu.VMEM((levels, LANES), jnp.float32),
            pltpu.VMEM((3, audio_rows, aud_k.shape[1]), half),
            pltpu.VMEM((3, audio_rows, aud_k.shape[1]), half),
            pltpu.VMEM(cross_q.shape, half),
            pltpu.VMEM(windows.shape, windows.dtype),
            pltpu.SemaphoreType.DMA((5,)),
            pltpu.SemaphoreType.DMA((4 + video_each,)),
            pltpu.SemaphoreType.DMA((2,)),
            pltpu.SemaphoreType.DMA((2,)),
            pltpu.SemaphoreType.DMA((2,)),
            pltpu.SemaphoreType.DMA((2,)),
            pltpu.SemaphoreType.DMA((4,)),
            pltpu.SemaphoreType.REGULAR((2,)),
            pltpu.SemaphoreType.REGULAR,
            pltpu.SemaphoreType.REGULAR,
        ],
        compiler_params=pltpu.CompilerParams(collective_id=0, has_side_effects=True),
        name="joint_attention",
    )(*arrays)
    return pl.pallas_call(
        store_kernel,
        out_shape=tuple(jax.ShapeDtypeStruct(a.shape, half) for a in (vid_q, aud_q, cross_q)),
        in_specs=[pl.BlockSpec(memory_space=pltpu.VMEM)] * 3,
        out_specs=(place, place, place),
        scratch_shapes=[pltpu.SemaphoreType.DMA((3,))],
        name="store_results",
    )(*[pltpu.with_memory_space_constraint(x, pltpu.VMEM) for x in held])


def body(*arrays):
    sub_count = lax.axis_size("sub")
    count = lax.axis_size("seq") * sub_count
    video_heads = arrays[0].shape[1] // HEAD_DIM
    audio_heads = arrays[3].shape[1] // AUDIO_DIM
    halved = sub_count == 2 and count == 4 * sub_count and max(audio_heads, arrays[3].shape[0]) <= LANES
    if halved and video_heads % count == 0 and audio_heads % count == 0:
        return exchanged_body(count, sub_count, *arrays)
    return gathered_body(*arrays)


def solution(mesh):
    return jax.shard_map(
        body,
        mesh=mesh,
        in_specs=(
            P(("grp", "seq", "sub"), "head"),
            P(("grp", "seq", "sub"), "head"),
            P(("grp", "seq", "sub"), "head"),
            P(("grp", "seq", "sub"), "head"),
            P(("grp", "seq", "sub"), "head"),
            P(("grp", "seq", "sub"), "head"),
            P(("grp", "seq", "sub"), "head"),
            P(("grp", "seq", "sub"), "head"),
            P(("grp", "seq", "sub"), "head"),
            P(None, "grp"),
        ),
        out_specs=(
            P(("grp", "seq", "sub"), "head"),
            P(("grp", "seq", "sub"), "head"),
            P(("grp", "seq", "sub"), "head"),
        ),
        check_vma=False,
    )
```
